32 devices in a mesh: dp: 8 (over y, x, core), tensor: 4 (over z).
Axes of the slice: x: 2, y: 2, z: 4, core: 2. Of those that a mesh axis runs over, the one named last changes fastest.
Arguments:
- tokens: bfloat16 [12608, 512], P(('dp', 'tensor')), may hold values from -11 to 11
- cotangent: bfloat16 [12608, 512], P(('dp', 'tensor')), may hold values from -11 to 11
- routes: int32 [12608, 2], P('dp'), may hold values from 0 to 3, as said below
- slots: int32 [12608, 2], P('dp'), may hold values from -1 to 787, as said below
- norm_gains: bfloat16 [2, 512], P(None, 'dp'), may hold values from 0.5 to 1.5
- norm_biases: bfloat16 [2, 512], P(None, 'dp'), may hold values from -1 to 1
- w_qkv: bfloat16 [3, 512, 512], P(None, 'dp', 'tensor'), may hold values from -0.25 to 0.25
- qv_bias: bfloat16 [2, 512], P(None, ('tensor', 'dp')), may hold values from -1 to 1
- w_out: bfloat16 [512, 512], P('tensor', 'dp'), may hold values from -2 to 2
- out_bias: bfloat16 [512], P('dp'), may hold values from -1 to 1
- w_router: bfloat16 [512, 4], P('dp'), may hold values from -0.25 to 0.25
- w_up: bfloat16 [4, 512, 2048], P(None, 'dp', 'tensor'), may hold values from -0.25 to 0.25
- up_bias: bfloat16 [4, 2048], P(None, ('tensor', 'dp')), may hold values from -1 to 1
- w_down: bfloat16 [4, 2048, 512], P(None, 'tensor', 'dp'), may hold values from -0.5 to 0.5
- down_bias: bfloat16 [4, 512], P(None, 'dp'), may hold values from -1 to 1
Outputs:
- layer_out: float32 [12608, 512], P(('dp', 'tensor'))
- grad_tokens: float32 [12608, 512], P(('dp', 'tensor'))
- grad_norm_gains: float32 [2, 512], P(None, 'dp')
- grad_norm_biases: float32 [2, 512], P(None, 'dp')
- grad_qkv: float32 [3, 512, 512], P(None, 'dp', 'tensor')
- grad_qv_bias: float32 [2, 512], P(None, ('tensor', 'dp'))
- grad_out: float32 [512, 512], P('tensor', 'dp')
- grad_out_bias: float32 [512], P('dp')
- grad_router: float32 [512, 4], P('dp')
- grad_up: float32 [4, 512, 2048], P(None, 'dp', 'tensor')
- grad_up_bias: float32 [4, 2048], P(None, ('tensor', 'dp'))
- grad_down: float32 [4, 2048, 512], P(None, 'tensor', 'dp')
- grad_down_bias: float32 [4, 512], P(None, 'dp')
The draws below stay inside these ranges and needn't reach their ends.
Inputs may be any that keep to these rules, and one draw needn't show every extreme that they name: `routes`: the two entries of a row name different experts. Within the 1576 rows of one index of dp, the pairs that name an expert take its slots 0, 1, 2, ... in the order of rows and, within a row, of entries; a pair past the first 788 of its expert has -1.
All inputs are finite; a program needn't handle non-finite values.
Results may differ from the reference program's by a relative error of at most 0.025.
Values may be sent and summed in bfloat16 or wider, within the bound.
No kernel may reach another device: no remote copies, remote signals or barrier semaphores. Data moves between devices by JAX's collectives and lax.ppermute only.
A program may use at most 128 MiB of HBM per device.

```python
import jax
import jax.numpy as jnp
from jax import lax

D = 512
HEADS = 8
HD = 64
FF = 2048
EXPERTS = 4
TOP = 2
SEQ = 197
IMG_DEV = 8
TOKG = 1576
TOKENS = 12608
CAP = 788


def rising_scale():
    image_index = jnp.arange(TOKENS, dtype=jnp.int32) // SEQ
    image_count = TOKENS // SEQ
    return 1.0 + 0.732 * image_index.astype(jnp.float32) / max(image_count - 1, 1)


def draw_tokens(key, part):
    scale_col = rising_scale()[:, None]
    return (jnp.clip(jax.random.normal(key, (TOKENS, D), jnp.float32), -6.0, 6.0) * scale_col).astype(jnp.bfloat16)


def draw_cotangent(key, part):
    own_key = jax.random.fold_in(key, 11)
    scale_col = rising_scale()[:, None]
    return (jnp.clip(jax.random.normal(own_key, (TOKENS, D), jnp.float32), -6.0, 6.0) * scale_col).astype(jnp.bfloat16)


def route_table(key):
    route_key = jax.random.fold_in(key, 5)
    first_key, second_key = jax.random.split(route_key)
    first_pick = jax.random.randint(first_key, (TOKENS,), 0, EXPERTS, dtype=jnp.int32)
    offset_draw = jax.random.randint(second_key, (TOKENS,), 1, EXPERTS, dtype=jnp.int32)
    second = (first_pick + offset_draw) % EXPERTS
    route_pairs = jnp.stack([first_pick, second], axis=1)
    flat_routes = route_pairs.reshape(TOKENS // TOKG, TOKG * TOP)
    member = (flat_routes[:, :, None] == jnp.arange(EXPERTS, dtype=jnp.int32)).astype(jnp.int32)
    before = jnp.cumsum(member, axis=1) - member
    rank_own = jnp.sum(before * member, axis=2)
    slot_table = jnp.where(rank_own < CAP, rank_own, -1).reshape(TOKENS, TOP)
    return (route_pairs, slot_table.astype(jnp.int32))


def draw_routes(key, part):
    return route_table(key)[0]


def draw_slots(key, part):
    return route_table(key)[1]


def block_levels(key, extent, pieces, smallest, high):
    gain = 1.0
    for dim, parts in pieces:
        draws = jax.random.uniform(jax.random.fold_in(jax.random.fold_in(key, 6), dim), (parts,), jnp.float32, smallest / len(pieces), high / len(pieces))
        gain = gain * jnp.repeat(jnp.exp(draws), extent[dim] // parts).reshape((-1,) + (1,) * (len(extent) - 1 - dim))
    return gain


def bell_draw(key, dims, deviation, bound, pieces=(), kind=jnp.bfloat16):
    array = deviation * jax.random.normal(key, dims, jnp.float32)
    if pieces:
        array = array * block_levels(key, dims, pieces, -0.22, 0.18)
    return jnp.clip(array, -bound, bound).astype(kind)


def setup_inputs(seed: int = 0) -> dict:
    splits = jax.random.split(jax.random.key(seed), 16)
    return {
        "tokens": draw_tokens(jax.random.fold_in(splits[15], 71), 0),
        "cotangent": draw_cotangent(jax.random.fold_in(splits[15], 71), 0),
        "routes": draw_routes(jax.random.fold_in(splits[15], 71), 0),
        "slots": draw_slots(jax.random.fold_in(splits[15], 71), 0),
        "norm_gains": jnp.clip(1.0 + 0.1 * jax.random.normal(splits[4], (2, D), jnp.float32), 0.5, 1.5).astype(jnp.bfloat16),
        "norm_biases": bell_draw(splits[5], (2, D), 0.2, 1.0, ((1, 8),)),
        "w_qkv": bell_draw(splits[6], (3, D, D), D ** -0.5, 0.25, ((1, 8), (2, 4))),
        "qv_bias": bell_draw(splits[7], (2, D), 0.2, 1.0, ((1, 32),)),
        "w_out": bell_draw(splits[8], (D, D), (D // 64) ** -0.5, 2.0, ((0, 4), (1, 8))),
        "out_bias": bell_draw(splits[9], (D,), 0.2, 1.0, ((0, 8),)),
        "w_router": bell_draw(splits[10], (D, EXPERTS), D ** -0.5, 0.25, ((0, 8),)),
        "w_up": bell_draw(splits[11], (EXPERTS, D, FF), D ** -0.5, 0.25, ((1, 8), (2, 4))),
        "up_bias": bell_draw(splits[12], (EXPERTS, FF), 0.2, 1.0, ((1, 32),)),
        "w_down": bell_draw(splits[13], (EXPERTS, FF, D), (FF // 16) ** -0.5, 0.5, ((1, 4), (2, 8))),
        "down_bias": bell_draw(splits[14], (EXPERTS, D), 0.2, 1.0, ((1, 8),)),
    }


epsilon = 1e-06
precise = lax.Precision.HIGHEST

@jax.custom_vjp
def low(v):
    return lax.optimization_barrier(v.astype(jnp.bfloat16)).astype(jnp.float32)

@jax.custom_vjp
def low_back(v):
    return v

def low_keep(v):
    return (low(v), None)

def low_pass(kept, grad):
    return (grad,)

def back_keep(v):
    return (v, None)

def back_low(kept, grad):
    return (low(grad),)
low.defvjp(low_keep, low_pass)
low_back.defvjp(back_keep, back_low)

def both_ways(value):
    return low(low_back(value))

def layer_norm(values_in, gain_row, bias_row):
    center = values_in - lax.optimization_barrier(jnp.mean(values_in, axis=-1, keepdims=True))
    inverse = lax.rsqrt(lax.optimization_barrier(jnp.mean(center * center, axis=-1, keepdims=True)) + epsilon)
    return center * inverse * gain_row + bias_row

def forward(tokens_f, gains_f, biases_f, qkv_f, qv_bias_f, out_f, out_bias_f, router_f, up_f, up_bias_f, down_f, down_bias_f, routes, slots):
    groups = TOKENS // TOKG
    hn_first = low(layer_norm(tokens_f, gains_f[0], biases_f[0]))
    shape_four = (IMG_DEV, SEQ, HEADS, HD)

    def attend(group_rows):
        projected = jnp.einsum('td,sdc->stc', group_rows, qkv_f, precision=precise)
        queries = both_ways(projected[0] + qv_bias_f[0])
        key_rows = both_ways(projected[1])
        values = both_ways(projected[2] + qv_bias_f[1])
        scores = low_back(jnp.einsum('ishd,ijhd->ihsj', queries.reshape(shape_four), key_rows.reshape(shape_four), precision=precise) * HD ** (-0.5))
        attn_probs = low(jax.nn.softmax(scores, axis=-1))
        mixed = jnp.einsum('ihsj,ijhd->ishd', attn_probs, values.reshape(shape_four), precision=precise)
        return both_ways(mixed.reshape(TOKG, D))
    heads_out = lax.map(jax.checkpoint(attend), hn_first.reshape(groups, TOKG, D)).reshape(TOKENS, D)
    branch_attn = low_back(jnp.dot(heads_out, out_f, precision=precise) + out_bias_f)
    resid_mid = tokens_f + branch_attn
    hn_second = low(layer_norm(resid_mid, gains_f[1], biases_f[1]))
    logits = jnp.dot(hn_second, router_f, precision=precise)
    probs_all = jax.nn.softmax(logits, axis=-1)
    choose = (routes[:, :, None] == jnp.arange(EXPERTS, dtype=jnp.int32)).astype(probs_all.dtype)
    gates = low(lax.optimization_barrier(jnp.sum(choose * probs_all[:, None, :], axis=-1)))

    def experts_of(group_in):
        rows_in, route_rows, slot_rows, gate_rows = group_in
        target = jnp.where(slot_rows >= 0, route_rows * CAP + slot_rows, EXPERTS * CAP).reshape(-1).astype(jnp.int32)
        spread_rows = jnp.broadcast_to(rows_in[:, None, :], (TOKG, TOP, D)).reshape(TOKG * TOP, D)
        buffer = jnp.zeros((EXPERTS * CAP, D), rows_in.dtype).at[target].set(spread_rows, mode='drop').reshape(EXPERTS, CAP, D)
        pre_act = low_back(jnp.einsum('ecd,edf->ecf', buffer, up_f, precision=precise) + up_bias_f[:, None, :])
        hidden = low(jax.nn.gelu(pre_act, approximate=False))
        expert_rows = low_back(jnp.einsum('ecf,efd->ecd', hidden, down_f, precision=precise) + down_bias_f[:, None, :])
        picked = jnp.take(expert_rows.reshape(EXPERTS * CAP, D), target, axis=0, mode='fill', fill_value=0.0).reshape(TOKG, TOP, D)
        return lax.optimization_barrier(jnp.sum(gate_rows[:, :, None] * picked, axis=1))
    moe_rows = lax.map(jax.checkpoint(experts_of), (hn_second.reshape(groups, TOKG, D), routes.reshape(groups, TOKG, TOP), slots.reshape(groups, TOKG, TOP), gates.reshape(groups, TOKG, TOP))).reshape(TOKENS, D)
    branch_moe = low_back(moe_rows)
    return resid_mid + branch_moe

def reference(tokens, cotangent, routes, slots, norm_gains, norm_biases, w_qkv, qv_bias, w_out, out_bias, w_router, w_up, up_bias, w_down, down_bias):
    floats = [array_in.astype(jnp.float32) for array_in in (tokens, norm_gains, norm_biases, w_qkv, qv_bias, w_out, out_bias, w_router, w_up, up_bias, w_down, down_bias)]

    def run_layer(*params):
        return forward(*params, routes, slots)
    layer_out, pullback = jax.vjp(run_layer, *floats)
    gradients = pullback(cotangent.astype(jnp.float32))
    return (layer_out, gradients[0], gradients[1], gradients[2], gradients[3], gradients[4], gradients[5], gradients[6], gradients[7], gradients[8], gradients[9], gradients[10], gradients[11])
```

```python
from functools import partial

import jax
import jax.numpy as jnp
from jax import lax
from jax.experimental import pallas as pl
from jax.experimental.pallas import tpu as pltpu
from jax.sharding import PartitionSpec as P

HD = 64
EXPERTS = 4
SEQ = 197
IMG_DEV = 8
CAP = 788
PAD = 200
GROWS = 8
WIN = 224
SLOTROWS = 800
SLOTBUF = (CAP // 16) * 16 + WIN
EPS = 1e-06
BF = jnp.bfloat16
F4 = jnp.float32
NEG = -1e30
LANES = 128

NN = (((1,), (0,)), ((), ()))
NT = (((1,), (1,)), ((), ()))
TN = (((0,), (0,)), ((), ()))

VM = pl.BlockSpec(memory_space=pltpu.VMEM)
SM = pl.BlockSpec(memory_space=pltpu.SMEM)


def mm(a, b, dims=NN):
    return lax.dot_general(a, b, dims, preferred_element_type=F4)


def params():
    return pltpu.CompilerParams(vmem_limit_bytes=60 * 1024 * 1024)


def cost(us):
    return pl.CostEstimate(flops=0, transcendentals=0, bytes_accessed=int(us * 3.3e6))


def xor_send(x, axis, n, mask):
    return lax.ppermute(x, axis, [(i, i ^ mask) for i in range(n)])


def ring_order(n):
    return [0] + list(range(1, n, 2)) + list(range(2, n, 2))[::-1]


def ring_step(x, n, back):
    ring = ring_order(n)
    pairs = [(ring[p], ring[(p + (-1 if back else 1)) % n]) for p in range(n)]
    return lax.ppermute(x, "tensor", pairs)


def ring_sources(n):
    ring = ring_order(n)
    pos = {r: p for p, r in enumerate(ring)}
    return [[ring[(pos[r] - s) % n] for s in range(n)] for r in range(n)]


def stages_of(n):
    if n <= 8:
        inter = list(range(2, n, 2))
        return ([[1]] if n > 1 else []) + ([inter] if inter else [])
    out, bit = [], 1
    while bit < n:
        out.append([bit])
        bit *= 2
    return out


def gather_dp(x, n):
    parts = [((0,), x[None])]
    for stage in reversed(stages_of(n)):
        new = []
        for mask in stage:
            for masks, arr in parts:
                new.append((tuple(k ^ mask for k in masks), xor_send(arr, "dp", n, mask)))
        parts = parts + new
        if n > 8 and stage != [1]:
            parts = [
                (sum((m for m, _ in parts), ()), jnp.concatenate([a for _, a in parts], axis=0))
            ]
    return parts


def scatter_dp(even, odd, n, later):
    got = xor_send(odd, "dp", n, 1)
    masks = list(range(0, n, 2))
    own = {k: even[i] for i, k in enumerate(masks)}
    new = {k: got[i] for i, k in enumerate(masks)}
    own = {k: (own[k].astype(F4) + new[k].astype(F4)).astype(BF) for k in masks}
    stages = stages_of(n)[1:]
    for at, stage in enumerate(stages):
        span = 0
        for m in stage:
            span |= m
        rest = [k for k in masks if not k & span]
        recv = []
        for m in stage:
            pack = [own[k ^ m] for k in rest]
            send = pack[0] if len(pack) == 1 else jnp.stack(pack)
            back = xor_send(send, "dp", n, m)
            recv.append([back] if len(pack) == 1 else [back[i] for i in range(len(pack))])
        masks = rest
        if at == len(stages) - 1:
            return [own[0]] + [r[0] for r in recv]
        own = {
            k: sum((r[i].astype(F4) for r in recv), own[k].astype(F4)).astype(BF)
            for i, k in enumerate(rest)
        }
    return [own[0]]


def add_all(parts):
    return sum((p.astype(F4) for p in parts[1:]), parts[0].astype(F4))


def moments(v, eps_rows):
    center = v - jnp.mean(v, axis=-1, keepdims=True)
    inv = lax.rsqrt(jnp.mean(center * center, axis=-1, keepdims=True) + eps_rows)
    return center * inv, inv


def norm_back(z, normed, inv):
    return inv * (
        z
        - jnp.mean(z, axis=-1, keepdims=True)
        - normed * jnp.mean(z * normed, axis=-1, keepdims=True)
    )


def attn_forward_kernel(masks, width, *refs):
    npieces = len(masks)
    ids = refs[0]
    pieces = refs[1 : 1 + npieces]
    x_ref, rows_ref, router_ref, dbias_ref, slot_ref = refs[1 + npieces : 6 + npieces]
    outs = refs[6 + npieces :]
    if npieces > 0 and masks[0] is not None:
        pay_ref, x1_ref, x1b_ref, q_ref, k_ref, v_ref, o_ref, pb_ref, pr_ref, w_ref = outs
        me, met = ids[0], ids[1]
        for group, ref in zip(masks, pieces):
            dr = ref.shape[3]
            for idx, mask in enumerate(group):
                i = jnp.bitwise_xor(me, mask)
                for jm in range(ref.shape[1]):
                    j = jnp.bitwise_xor(met, jm)
                    for s in range(4):
                        w_ref[
                            s,
                            pl.ds(pl.multiple_of(i * dr, dr), dr),
                            pl.ds(pl.multiple_of(j * LANES, LANES), LANES),
                        ] = ref[idx, jm, s]
    else:
        pay_ref, x1_ref, x1b_ref, q_ref, k_ref, v_ref, o_ref, pb_ref, pr_ref = outs
        w_ref = pieces[0]
    x = x_ref[...].astype(F4)
    n1, _ = moments(x, EPS)
    hn1 = (n1 * rows_ref[0:1, :] + rows_ref[2:3, :]).astype(BF)
    q_ref[...] = (mm(hn1, w_ref[0]) + rows_ref[5:6, :]).astype(BF)
    k_ref[...] = mm(hn1, w_ref[1]).astype(BF)
    v_ref[...] = (mm(hn1, w_ref[2]) + rows_ref[6:7, :]).astype(BF)
    lane = lax.broadcasted_iota(jnp.int32, (PAD, LANES), 1)
    col = lax.broadcasted_iota(jnp.int32, (PAD, PAD), 1)
    for pair in range(width // LANES):
        cols = slice(pair * LANES, (pair + 1) * LANES)
        qp, kp, vp = q_ref[:, cols], k_ref[:, cols], v_ref[:, cols]
        acc = jnp.zeros((PAD, LANES), F4)
        for half in range(2):
            mine = (lane < HD) if half == 0 else (lane >= HD)
            qm = jnp.where(mine, qp * jnp.asarray(HD ** (-0.5), BF), jnp.zeros_like(qp))
            s = mm(qm, kp, NT)
            s = jnp.where(col < SEQ, s, NEG)
            e = jnp.exp(s - jnp.max(s, axis=-1, keepdims=True))
            p = (e * (1.0 / jnp.sum(e, axis=-1, keepdims=True))).astype(BF)
            pb_ref[2 * pair + half] = p
            acc = acc + mm(p, jnp.where(mine, vp, jnp.zeros_like(vp)))
        o_ref[:, cols] = acc.astype(BF)
    x1 = x + (mm(o_ref[...], w_ref[3], NT) + rows_ref[4:5, :])
    x1_ref[...] = x1
    n2, _ = moments(x1, EPS)
    hn2 = (n2 * rows_ref[1:2, :] + rows_ref[3:4, :]).astype(BF)
    logits = mm(router_ref[...], hn2, NT)
    row = lax.broadcasted_iota(jnp.int32, logits.shape, 0)
    logits = jnp.where(row < EXPERTS, logits, NEG)
    e = jnp.exp(logits - jnp.max(logits, axis=0, keepdims=True))
    probs = e / jnp.sum(e, axis=0, keepdims=True)
    pr_ref[...] = probs
    gates = jnp.where(slot_ref[...] >= 0, probs, 0.0).astype(BF)
    pay_ref[0:PAD, :] = hn2
    pay_ref[PAD:, :] = jnp.zeros((GROWS, width), BF)
    pay_ref[PAD:, 0:PAD] = gates
    x1b_ref[...] = x1 + mm(gates, dbias_ref[...], TN)


def attn_forward(ids, weights, x, rows, router, dbias, slot, first):
    width = x.shape[1]
    heads = width // HD
    if first:
        masks = [m for m, _ in weights]
        arrays = [a for _, a in weights]
    else:
        masks, arrays = [None], [weights]
    shapes = [
        jax.ShapeDtypeStruct((PAD + GROWS, width), BF),
        jax.ShapeDtypeStruct((PAD, width), F4),
        jax.ShapeDtypeStruct((PAD, width), F4),
        jax.ShapeDtypeStruct((PAD, width), BF),
        jax.ShapeDtypeStruct((PAD, width), BF),
        jax.ShapeDtypeStruct((PAD, width), BF),
        jax.ShapeDtypeStruct((PAD, width), BF),
        jax.ShapeDtypeStruct((heads, PAD, PAD), BF),
        jax.ShapeDtypeStruct((8, PAD), F4),
    ]
    if first:
        shapes.append(jax.ShapeDtypeStruct((4, width, width), BF))
    return pl.pallas_call(
        partial(attn_forward_kernel, masks, width),
        out_shape=shapes,
        in_specs=[SM] + [VM] * (len(arrays) + 5),
        out_specs=[VM] * len(shapes),
        compiler_params=params(),
        cost_estimate=cost(8),
        name="attn_forward",
    )(ids, *arrays, x, rows, router, dbias, slot)


def one_hot(slot_row, base, rows):
    want = lax.broadcasted_iota(jnp.int32, (rows, slot_row.shape[1]), 0)
    return want == jnp.broadcast_to(slot_row - base, (rows, slot_row.shape[1]))


def dispatch_kernel(nshard, nimg, starts_ref, src_ref, slots_ref, *refs):
    count = nshard * nimg
    pays, cots = refs[:count], refs[count : 2 * count]
    buf_ref, dout_ref = refs[2 * count :]
    buf_ref[...] = jnp.zeros(buf_ref.shape, BF)
    dout_ref[...] = jnp.zeros(dout_ref.shape, BF)
    for s in range(nshard):
        for img in range(nimg):
            pay, cot = pays[s * nimg + img], cots[s * nimg + img]
            tile = src_ref[s] * nimg + img

            def body(e, carry, pay=pay, cot=cot, tile=tile):
                base = pl.multiple_of((starts_ref[tile * EXPERTS + e] // 16) * 16, 16)
                hit = one_hot(slots_ref[tile * EXPERTS + e], base, WIN)
                gate = pay[PAD:, 0:PAD].astype(F4)
                pick = lax.broadcasted_iota(jnp.int32, gate.shape, 0) == e
                gate = jnp.sum(jnp.where(pick, gate, 0.0), axis=0, keepdims=True)
                plain = jnp.where(hit, 1.0, 0.0).astype(BF)
                gated = jnp.where(hit, jnp.broadcast_to(gate, hit.shape), 0.0).astype(BF)
                at = pl.ds(base, WIN)
                buf_ref[e, at, :] = buf_ref[e, at, :] + mm(plain, pay[0:PAD, :]).astype(BF)
                dout_ref[e, at, :] = dout_ref[e, at, :] + mm(gated, cot[...]).astype(BF)
                return carry

            lax.fori_loop(0, EXPERTS, body, 0)


def dispatch(starts, src, slots, pays, cots, nshard, nimg):
    width = pays[0].shape[1]
    shape = jax.ShapeDtypeStruct((EXPERTS, SLOTBUF, width), BF)
    return pl.pallas_call(
        partial(dispatch_kernel, nshard, nimg),
        out_shape=[shape, shape],
        in_specs=[SM, SM] + [VM] * (1 + 2 * len(pays)),
        out_specs=[VM, VM],
        compiler_params=params(),
        cost_estimate=cost(8),
        name="dispatch",
    )(starts, src, slots, *pays, *cots)


def expert_kernel(masks, gmasks, *refs):
    npieces = len(masks)
    ids = refs[0]
    pieces = refs[1 : 1 + npieces]
    ub_ref, buf_ref, dout_ref = refs[1 + npieces : 4 + npieces]
    ngrads = len(gmasks)
    eo_ref, db_ref, gub_ref = refs[4 + npieces : 7 + npieces]
    grads = refs[7 + npieces : 7 + npieces + ngrads]
    up_ref, dn_ref, h_ref, dhp_ref, res_ref = refs[7 + npieces + ngrads :]
    me = ids[0]
    for group, ref in zip(masks, pieces):
        dr = ref.shape[3]
        for idx, mask in enumerate(group):
            at = pl.ds(pl.multiple_of(jnp.bitwise_xor(me, mask) * dr, dr), dr)
            up_ref[at, :] = ref[idx, 0, 0]
            dn_ref[at, :] = ref[idx, 1, 0]
    chunk = SLOTROWS // 2
    gub = jnp.zeros(gub_ref.shape, F4)
    for c in range(2):
        at = slice(c * chunk, (c + 1) * chunk)
        u = mm(buf_ref[at, :], up_ref[...]) + ub_ref[...]
        phi = 0.5 + 0.5 * lax.erf(u * (2.0 ** (-0.5)))
        slope = phi + u * (jnp.exp(-0.5 * u * u) * 0.3989422804014327)
        h_ref[at, :] = (u * phi).astype(BF)
        eo_ref[at, :] = mm(h_ref[at, :], dn_ref[...], NT).astype(BF)
        dh = mm(dout_ref[at, :], dn_ref[...])
        dhp = (dh * slope).astype(BF)
        dhp_ref[at, :] = dhp
        gub = gub + jnp.sum(dhp.astype(F4), axis=0, keepdims=True)
        db_ref[at, :] = mm(dhp, up_ref[...], NT).astype(BF)
    gub_ref[...] = gub
    tail = eo_ref.shape[0] - SLOTROWS
    eo_ref[SLOTROWS:, :] = jnp.zeros((tail, eo_ref.shape[1]), BF)
    db_ref[SLOTROWS:, :] = jnp.zeros((tail, eo_ref.shape[1]), BF)
    for which in range(2):
        if which == 0:
            res_ref[...] = mm(buf_ref[0:SLOTROWS, :], dhp_ref[...], TN)
        else:
            res_ref[...] = mm(dout_ref[0:SLOTROWS, :], h_ref[...], TN)
        for group, ref in zip(gmasks, grads):
            dr = ref.shape[3]
            for idx, mask in enumerate(group):
                at = pl.ds(pl.multiple_of(jnp.bitwise_xor(me, mask) * dr, dr), dr)
                ref[idx, which, 0] = res_ref[at, :].astype(BF)


def experts(ids, weights, ubias, buf, dout, gmasks):
    width = buf.shape[2]
    ff = ubias.shape[2]
    masks = [m for m, _ in weights]
    arrays = [a for _, a in weights]
    dr = arrays[0].shape[3]
    specs = [
        pl.BlockSpec((len(m), 2, 1, dr, ff), lambda e: (0, 0, e, 0, 0)) for m in masks
    ]
    slot_spec = pl.BlockSpec((None, SLOTBUF, width), lambda e: (e, 0, 0))
    row_spec = pl.BlockSpec((None, 1, ff), lambda e: (e, 0, 0))
    gspecs = [
        pl.BlockSpec((len(m), 2, 1, dr, ff), lambda e: (0, 0, e, 0, 0)) for m in gmasks
    ]
    return pl.pallas_call(
        partial(expert_kernel, masks, gmasks),
        grid=(EXPERTS,),
        out_shape=[
            jax.ShapeDtypeStruct((EXPERTS, SLOTBUF, width), BF),
            jax.ShapeDtypeStruct((EXPERTS, SLOTBUF, width), BF),
            jax.ShapeDtypeStruct((EXPERTS, 1, ff), F4),
        ]
        + [jax.ShapeDtypeStruct((len(m), 2, EXPERTS, dr, ff), BF) for m in gmasks],
        in_specs=[SM] + specs + [row_spec, slot_spec, slot_spec],
        out_specs=[slot_spec, slot_spec, row_spec] + gspecs,
        scratch_shapes=[
            pltpu.VMEM((width, ff), BF),
            pltpu.VMEM((width, ff), BF),
            pltpu.VMEM((SLOTROWS, ff), BF),
            pltpu.VMEM((SLOTROWS, ff), BF),
            pltpu.VMEM((width, ff), F4),
        ],
        compiler_params=params(),
        cost_estimate=cost(25),
        name="experts",
    )(ids, *arrays, ubias, buf, dout)


def combine_kernel(nshard, nimg, starts_ref, src_ref, slots_ref, eo_ref, db_ref, *refs):
    count = nshard * nimg
    pays, cots = refs[:count], refs[count : 2 * count]
    m_refs = refs[2 * count : 2 * count + nshard]
    d_refs = refs[2 * count + nshard : 3 * count + nshard]
    s_ref, g_ref, ecat_ref, dcat_ref = refs[3 * count + nshard :]
    width = eo_ref.shape[2]
    for s in range(nshard):
        for img in range(nimg):
            n = s * nimg + img
            pay, cot = pays[n], cots[n]
            tile = src_ref[s] * nimg + img

            def body(e, carry, pay=pay, tile=tile):
                base = pl.multiple_of((starts_ref[tile * EXPERTS + e] // 16) * 16, 16)
                hit = one_hot(slots_ref[tile * EXPERTS + e], base, WIN)
                gate = pay[PAD:, 0:PAD].astype(F4)
                pick = lax.broadcasted_iota(jnp.int32, gate.shape, 0) == e
                gate = jnp.sum(jnp.where(pick, gate, 0.0), axis=0, keepdims=True)
                to = pl.ds(pl.multiple_of(e * WIN, WIN), WIN)
                s_ref[to, :] = jnp.where(hit, 1.0, 0.0).astype(BF)
                g_ref[to, :] = jnp.where(hit, jnp.broadcast_to(gate, hit.shape), 0.0).astype(BF)
                ecat_ref[to, :] = eo_ref[e, pl.ds(base, WIN), :]
                dcat_ref[to, :] = db_ref[e, pl.ds(base, WIN), :]
                return carry

            lax.fori_loop(0, EXPERTS, body, 0)
            m_refs[s][img * PAD : (img + 1) * PAD, :] = mm(
                g_ref[...], ecat_ref[...], TN
            ).astype(BF)
            d_refs[n][0:PAD, :] = mm(s_ref[...], dcat_ref[...], TN).astype(BF)
            cross = mm(ecat_ref[...], cot[...], NT)
            rows = []
            for e in range(EXPERTS):
                at = slice(e * WIN, (e + 1) * WIN)
                rows.append(
                    jnp.sum(cross[at, :] * s_ref[at, :].astype(F4), axis=0, keepdims=True)
                )
            d_refs[n][PAD:, :] = jnp.zeros((GROWS, width), BF)
            d_refs[n][PAD:, 0:PAD] = jnp.concatenate(
                rows + [jnp.zeros((GROWS - EXPERTS, PAD), F4)], axis=0
            ).astype(BF)


def combine(starts, src, slots, eo, db, pays, cots, nshard, nimg):
    width = eo.shape[2]
    count = nshard * nimg
    shapes = [jax.ShapeDtypeStruct((nimg * PAD, width), BF)] * nshard + [
        jax.ShapeDtypeStruct((PAD + GROWS, width), BF)
    ] * count
    return pl.pallas_call(
        partial(combine_kernel, nshard, nimg),
        out_shape=shapes,
        in_specs=[SM, SM] + [VM] * (3 + 2 * count),
        out_specs=[VM] * len(shapes),
        scratch_shapes=[
            pltpu.VMEM((EXPERTS * WIN, PAD), BF),
            pltpu.VMEM((EXPERTS * WIN, PAD), BF),
            pltpu.VMEM((EXPERTS * WIN, width), BF),
            pltpu.VMEM((EXPERTS * WIN, width), BF),
        ],
        compiler_params=params(),
        cost_estimate=cost(10),
        name="combine",
    )(starts, src, slots, eo, db, *pays, *cots)


def attn_backward_kernel(
    recv_ref,
    own_ref,
    x_ref,
    cot_ref,
    x1_ref,
    q_ref,
    k_ref,
    v_ref,
    pb_ref,
    pr_ref,
    slot_ref,
    rows_ref,
    router_ref,
    dbias_ref,
    w_ref,
    gtok_ref,
    da_ref,
    dq_ref,
    dk_ref,
    dv_ref,
    hn1_ref,
    small_ref,
    do_ref,
):
    width = x_ref.shape[1]
    got = recv_ref[...].astype(F4) + own_ref[...].astype(F4)
    cot = cot_ref[...]
    cot_f = cot.astype(F4)
    keep = slot_ref[...] >= 0
    inner = mm(dbias_ref[...], cot, NT)
    dp = jnp.where(keep, got[PAD:, 0:PAD] + inner, 0.0)
    probs = pr_ref[...]
    dl = probs * (dp - jnp.sum(probs * dp, axis=0, keepdims=True))
    dl_low = dl.astype(BF)
    n2, inv2 = moments(x1_ref[...], EPS)
    hn2 = (n2 * rows_ref[1:2, :] + rows_ref[3:4, :]).astype(BF)
    gates = jnp.where(keep, probs, 0.0).astype(BF)
    small_ref[8:16, :] = mm(dl_low, hn2)
    small_ref[16:24, :] = mm(gates, cot)
    dh = got[0:PAD, :] + mm(dl_low, router_ref[...], TN)
    small_ref[1:2, :] = jnp.sum(dh * n2, axis=0, keepdims=True)
    small_ref[3:4, :] = jnp.sum(dh, axis=0, keepdims=True)
    dx1 = cot_f + norm_back(dh * rows_ref[1:2, :], n2, inv2)
    da = dx1.astype(BF)
    da_ref[...] = da
    small_ref[6:7, :] = jnp.sum(da.astype(F4), axis=0, keepdims=True)
    small_ref[7:8, :] = jnp.zeros((1, width), F4)
    do_ref[...] = mm(da, w_ref[3]).astype(BF)
    lane = lax.broadcasted_iota(jnp.int32, (PAD, LANES), 1)
    scale = HD ** (-0.5)
    for pair in range(width // LANES):
        cols = slice(pair * LANES, (pair + 1) * LANES)
        qp, kp, vp, dop = q_ref[:, cols], k_ref[:, cols], v_ref[:, cols], do_ref[:, cols]
        zero = jnp.zeros_like(qp)
        dq = jnp.zeros((PAD, LANES), F4)
        dk = jnp.zeros((PAD, LANES), F4)
        dv = jnp.zeros((PAD, LANES), F4)
        for half in range(2):
            mine = (lane < HD) if half == 0 else (lane >= HD)
            pb = pb_ref[2 * pair + half]
            dom = jnp.where(mine, dop, zero)
            dpb = mm(dom, vp, NT)
            p = pb.astype(F4)
            ds = (p * (dpb - jnp.sum(p * dpb, axis=-1, keepdims=True))).astype(BF)
            dv = dv + mm(pb, dom, TN)
            dq = dq + mm(ds, jnp.where(mine, kp, zero))
            dk = dk + mm(ds, jnp.where(mine, qp, zero), TN)
        dq_ref[:, cols] = (dq * scale).astype(BF)
        dk_ref[:, cols] = (dk * scale).astype(BF)
        dv_ref[:, cols] = dv.astype(BF)
    small_ref[4:5, :] = jnp.sum(dq_ref[...].astype(F4), axis=0, keepdims=True)
    small_ref[5:6, :] = jnp.sum(dv_ref[...].astype(F4), axis=0, keepdims=True)
    dh1 = (
        mm(dq_ref[...], w_ref[0], NT)
        + mm(dk_ref[...], w_ref[1], NT)
        + mm(dv_ref[...], w_ref[2], NT)
    )
    n1, inv1 = moments(x_ref[...].astype(F4), EPS)
    hn1_ref[...] = (n1 * rows_ref[0:1, :] + rows_ref[2:3, :]).astype(BF)
    small_ref[0:1, :] = jnp.sum(dh1 * n1, axis=0, keepdims=True)
    small_ref[2:3, :] = jnp.sum(dh1, axis=0, keepdims=True)
    gtok_ref[...] = dx1 + norm_back(dh1 * rows_ref[0:1, :], n1, inv1)


def attn_backward(recv, own, x, cot, x1, q, k, v, pb, pr, slot, rows, router, dbias, full):
    width = x.shape[1]
    shapes = [
        jax.ShapeDtypeStruct((PAD, width), F4),
        jax.ShapeDtypeStruct((PAD, width), BF),
        jax.ShapeDtypeStruct((PAD, width), BF),
        jax.ShapeDtypeStruct((PAD, width), BF),
        jax.ShapeDtypeStruct((PAD, width), BF),
        jax.ShapeDtypeStruct((PAD, width), BF),
        jax.ShapeDtypeStruct((24, width), F4),
    ]
    return pl.pallas_call(
        attn_backward_kernel,
        out_shape=shapes,
        in_specs=[VM] * 15,
        out_specs=[VM] * len(shapes),
        scratch_shapes=[pltpu.VMEM((PAD, width), BF)],
        compiler_params=params(),
        cost_estimate=cost(10),
        name="attn_backward",
    )(recv, own, x, cot, x1, q, k, v, pb, pr, slot, rows, router, dbias, full)


def weight_grad_kernel(nimg, gmasks, ids, *refs):
    ngrads = len(gmasks)
    groups = [refs[6 * i : 6 * i + 6] for i in range(nimg)]
    grads = refs[6 * nimg : 6 * nimg + ngrads]
    res_ref = refs[6 * nimg + ngrads]
    me, met = ids[0], ids[1]
    for s in range(4):
        total = None
        for hn1, dq, dk, dv, da, o in groups:
            left, right = [(hn1, dq), (hn1, dk), (hn1, dv), (da, o)][s]
            term = mm(left[...], right[...], TN)
            total = term if total is None else total + term
        res_ref[...] = total
        for group, ref in zip(gmasks, grads):
            dr = ref.shape[2] // 4
            for idx, mask in enumerate(group):
                i = jnp.bitwise_xor(me, mask)
                for jm in range(ref.shape[1]):
                    j = jnp.bitwise_xor(met, jm)
                    ref[idx, jm, s * dr : (s + 1) * dr, :] = res_ref[
                        pl.ds(pl.multiple_of(i * dr, dr), dr),
                        pl.ds(pl.multiple_of(j * LANES, LANES), LANES),
                    ].astype(BF)


def weight_grads(ids, operands, gmasks, nt, dr):
    nimg = len(operands)
    width = operands[0][0].shape[1]
    shapes = [jax.ShapeDtypeStruct((len(m), nt, 4 * dr, LANES), BF) for m in gmasks]
    return pl.pallas_call(
        partial(weight_grad_kernel, nimg, gmasks),
        out_shape=shapes,
        in_specs=[SM] + [VM] * (6 * nimg),
        out_specs=[VM] * len(shapes),
        scratch_shapes=[pltpu.VMEM((width, width), F4)],
        compiler_params=params(),
        cost_estimate=cost(5),
        name="weight_grads",
    )(ids, *[a for group in operands for a in group])


def per_device(
    nd,
    nt,
    tokens,
    cotangent,
    routes,
    slots,
    norm_gains,
    norm_biases,
    w_qkv,
    qv_bias,
    w_out,
    out_bias,
    w_router,
    w_up,
    up_bias,
    w_down,
    down_bias,
):
    me = lax.axis_index("dp").astype(jnp.int32)
    met = lax.axis_index("tensor").astype(jnp.int32)
    width = tokens.shape[1]
    dr = w_qkv.shape[1]
    nimg = IMG_DEV // nt
    direct = dr % 16 == 0
    ids = jnp.stack([me if direct else jnp.zeros_like(me), met])
    even, odd = list(range(0, nd, 2)), list(range(1, nd, 2))

    def canonical(parts):
        if direct:
            return parts
        masks = sum((m for m, _ in parts), ())
        arr = jnp.concatenate([a for _, a in parts], axis=0)
        place = [masks.index(k) for k in range(nd)]
        order = jnp.asarray(place, jnp.int32)[jnp.bitwise_xor(jnp.arange(nd), me)]
        arr = jnp.take(arr, order, axis=0)
        lead = arr.ndim - 2
        arr = jnp.moveaxis(arr, 0, lead - 1)
        arr = arr.reshape(arr.shape[: lead - 1] + (nd * dr,) + arr.shape[-1:])
        return [((0,), arr[None])]

    gmasks = [even, odd] if direct else [[0]]

    def halves(grads, lead, rows):
        if direct:
            return grads
        whole = grads[0][0]
        shape = whole.shape[:lead] + (rows, nd, dr) + whole.shape[-1:]
        whole = jnp.moveaxis(whole.reshape(shape), lead + 1, 0)
        whole = whole.reshape((nd,) + grads[0].shape[1 : lead + 1] + (rows * dr, whole.shape[-1]))
        return [
            jnp.take(whole, jnp.bitwise_xor(jnp.asarray(m, jnp.int32), me), axis=0)
            for m in (even, odd)
        ]

    chunk = jnp.concatenate([w_qkv, w_out.T[None]], axis=0)
    chunk_z = jnp.stack([chunk] + [xor_send(chunk, "tensor", nt, m) for m in range(1, nt)])
    small = jnp.concatenate(
        [
            norm_gains.reshape(-1),
            norm_biases.reshape(-1),
            out_bias,
            w_router.T.reshape(-1),
            down_bias.reshape(-1),
            up_bias.reshape(-1),
            qv_bias.reshape(-1),
        ]
    )
    small = lax.all_gather(small, "dp", axis=0)
    rows13 = small[:, : 13 * dr].reshape(nd, 13, dr).transpose(1, 0, 2).reshape(13, nd * dr)
    at = 13 * dr
    fr = up_bias.shape[1]
    ubias = small[:, at : at + EXPERTS * fr].reshape(nd, EXPERTS, fr).transpose(1, 0, 2)
    ubias = ubias.reshape(EXPERTS, 1, nd * fr).astype(F4)
    at += EXPERTS * fr
    qr = qv_bias.shape[1]
    qvb = small[:, at:].reshape(nd, 2, qr).transpose(1, 0, 2).reshape(2, nd * qr)
    qvb = lax.all_gather(qvb, "tensor", axis=1, tiled=True)
    rows = jnp.concatenate(
        [rows13[:5].astype(F4), qvb.astype(F4), jnp.zeros((1, width), F4)], axis=0
    )
    blank = jnp.zeros((EXPERTS, width), BF)
    router = jnp.concatenate([rows13[5:9], blank], axis=0)
    dbias = jnp.concatenate([rows13[9:13], blank], axis=0)
    weights = gather_dp(chunk_z, nd)

    pair_routes = routes.reshape(nt * nimg, 1, SEQ, 2)
    pair_slots = slots.reshape(nt * nimg, 1, SEQ, 2)
    ids4 = jnp.arange(8, dtype=jnp.int32)[None, :, None, None]
    table = jnp.max(jnp.where(pair_routes == ids4, pair_slots, -1), axis=-1)
    counts = jnp.sum((table >= 0).astype(jnp.int32), axis=-1)[:, :EXPERTS]
    tiles = nt * nimg
    before = (jnp.arange(tiles)[:, None] > jnp.arange(tiles)[None, :]).astype(jnp.int32)
    starts = jnp.sum(before[:, :, None] * counts[None], axis=1).reshape(-1)
    table = jnp.pad(table, ((0, 0), (0, 0), (0, PAD - SEQ)), constant_values=-1)
    my_slots = lax.dynamic_slice_in_dim(table, met * nimg, nimg, 0)
    table = table[:, :EXPERTS].reshape(tiles * EXPERTS, 1, PAD)
    src = jnp.asarray(ring_sources(nt), jnp.int32)[met]

    x_img = [
        jnp.pad(tokens[i * SEQ : (i + 1) * SEQ], ((0, PAD - SEQ), (0, 0))) for i in range(nimg)
    ]
    c_img = [
        jnp.pad(cotangent[i * SEQ : (i + 1) * SEQ], ((0, PAD - SEQ), (0, 0))) for i in range(nimg)
    ]
    cots = [list(c_img)]
    for s in range(1, nt):
        cots.append([ring_step(c, nt, False) for c in cots[-1]])
    cots = [c for group in cots for c in group]

    both = jnp.stack([w_up, w_down.transpose(0, 2, 1)])
    expert_weights = canonical(gather_dp(both, nd))

    saved = []
    full = canonical(weights)
    for i in range(nimg):
        res = attn_forward(ids, full, x_img[i], rows, router, dbias, my_slots[i], i == 0)
        if i == 0:
            full = res[-1]
        saved.append(res[:9])
    pays = [[r[0] for r in saved]]
    for s in range(1, nt):
        pays.append([ring_step(p, nt, False) for p in pays[-1]])
    pays = [p for group in pays for p in group]

    buf, dout = dispatch(starts, src, table, pays, cots, nt, nimg)
    res = experts(ids, expert_weights, ubias, buf, dout, gmasks)
    eo, db, gub = res[:3]
    egrads = halves(res[3:], 2, 1)
    res = combine(starts, src, table, eo, db, pays, cots, nt, nimg)
    m_parts, d_parts = res[:nt], res[nt:]

    recv = [d_parts[(nt - 1) * nimg + i] for i in range(nimg)]
    for s in range(nt - 2, -1, -1):
        recv = [ring_step(r, nt, True) for r in recv]
        if s > 0:
            recv = [
                (r.astype(F4) + d_parts[s * nimg + i].astype(F4)).astype(BF)
                for i, r in enumerate(recv)
            ]

    expert_sum = add_all(scatter_dp(egrads[0], egrads[1], nd, None))

    operands, smalls, gtoks = [], None, []
    for i in range(nimg):
        pay, x1, x1b, q, k, v, o, pb, pr = saved[i]
        gtok, da, dq, dk, dv, hn1, sm = attn_backward(
            recv[i],
            d_parts[i],
            x_img[i],
            c_img[i],
            x1,
            q,
            k,
            v,
            pb,
            pr,
            my_slots[i],
            rows,
            router,
            dbias,
            full,
        )
        gtoks.append(gtok[:SEQ])
        operands.append((hn1, dq, dk, dv, da, o))
        smalls = sm if smalls is None else smalls + sm
    grads = weight_grads(ids, operands, gmasks, nt, dr if direct else nd * dr)
    grads = halves(grads, 1, 4)

    gub_rows = jnp.zeros((nt, EXPERTS, gub.shape[2]), F4)
    gub_rows = lax.dynamic_update_slice(gub_rows, gub.reshape(1, EXPERTS, -1), (met, 0, 0))
    flat = jnp.concatenate([smalls, gub_rows.reshape(nt * EXPERTS, -1)], axis=0).astype(BF)

    parts = scatter_dp(grads[0], grads[1], nd, None)
    held = add_all(parts).astype(BF)
    for stage in stages_of(nd):
        flat = add_all([flat] + [xor_send(flat, "dp", nd, m) for m in stage]).astype(BF)
    mine = [held[0]] + [xor_send(held[m], "tensor", nt, m) for m in range(1, nt)]
    mine = add_all(mine)
    flat = add_all([flat] + [xor_send(flat, "tensor", nt, m) for m in range(1, nt)])

    m_got = m_parts[nt - 1]
    m_got, _ = lax.optimization_barrier((m_got, recv[-1]))
    for s in range(nt - 2, -1, -1):
        m_got = ring_step(m_got, nt, True)
        if s > 0:
            m_got = (m_got.astype(F4) + m_parts[s].astype(F4)).astype(BF)
    layer_out = jnp.concatenate(
        [
            saved[i][2][:SEQ]
            + (
                m_got[i * PAD : i * PAD + SEQ].astype(F4)
                + m_parts[0][i * PAD : i * PAD + SEQ].astype(F4)
            )
            for i in range(nimg)
        ],
        axis=0,
    )
    grad_tokens = jnp.concatenate(gtoks, axis=0)

    def dp_cut(lo, hi):
        return lax.dynamic_slice(flat, (lo, me * dr), (hi - lo, dr))

    zero = jnp.zeros_like(me)
    g_qvb = lax.dynamic_slice(flat, (zero + 4, (met * nd + me) * qr), (2, qr))
    g_ub = lax.dynamic_slice(flat, (24 + met * EXPERTS, me * fr), (EXPERTS, fr))
    g_qkv = mine[: 3 * dr].reshape(3, dr, LANES)
    g_out = mine[3 * dr :].T
    g_up = expert_sum[0]
    g_down = expert_sum[1].transpose(0, 2, 1)
    return (
        layer_out,
        grad_tokens,
        dp_cut(0, 2),
        dp_cut(2, 4),
        g_qkv,
        g_qvb,
        g_out,
        dp_cut(6, 7)[0],
        dp_cut(8, 12).T,
        g_up,
        g_ub,
        g_down,
        dp_cut(16, 20),
    )


def solution(mesh):
    nd, nt = mesh.shape["dp"], mesh.shape["tensor"]
    placed = (
        P(("dp", "tensor"), None),
        P(("dp", "tensor"), None),
        P("dp", None),
        P("dp", None),
        P(None, "dp"),
        P(None, "dp"),
        P(None, "dp", "tensor"),
        P(None, ("tensor", "dp")),
        P("tensor", "dp"),
        P("dp"),
        P("dp", None),
        P(None, "dp", "tensor"),
        P(None, ("tensor", "dp")),
        P(None, "tensor", "dp"),
        P(None, "dp"),
    )
    return jax.shard_map(
        partial(per_device, nd, nt),
        mesh=mesh,
        in_specs=placed,
        out_specs=(
            P(("dp", "tensor"), None),
            P(("dp", "tensor"), None),
            P(None, "dp"),
            P(None, "dp"),
            P(None, "dp", "tensor"),
            P(None, ("tensor", "dp")),
            P("tensor", "dp"),
            P("dp"),
            P("dp", None),
            P(None, "dp", "tensor"),
            P(None, ("tensor", "dp")),
            P(None, "tensor", "dp"),
            P(None, "dp"),
        ),
        check_vma=False,
    )
```

```python
from functools import partial

import jax
import jax.numpy as jnp
from jax import lax
from jax.experimental import pallas as pl
from jax.experimental.pallas import tpu as pltpu
from jax.sharding import PartitionSpec as P

HD = 64
EXPERTS = 4
SEQ = 197
IMG_DEV = 8
PAD = 200
SMALL = 16
EPS = 1e-06
BF = jnp.bfloat16
F4 = jnp.float32
NEG = -1e30
LANES = 128
HALF = 64

NN = (((1,), (0,)), ((), ()))
NT = (((1,), (1,)), ((), ()))
TN = (((0,), (0,)), ((), ()))

VM = pl.BlockSpec(memory_space=pltpu.VMEM)
SM = pl.BlockSpec(memory_space=pltpu.SMEM)


def mm(a, b, dims=NN):
    return lax.dot_general(a, b, dims, preferred_element_type=F4)


def params(mib=30):
    return pltpu.CompilerParams(vmem_limit_bytes=mib * 1024 * 1024)


def cost(us):
    return pl.CostEstimate(flops=0, transcendentals=0, bytes_accessed=int(us * 3.3e6))


def xor_send(x, axis, n, mask):
    return lax.ppermute(x, axis, [(i, i ^ mask) for i in range(n)])


def ring_order(n):
    return [0] + list(range(1, n, 2)) + list(range(2, n, 2))[::-1]


def ring_step(x, n, back):
    ring = ring_order(n)
    pairs = [(ring[p], ring[(p + (-1 if back else 1)) % n]) for p in range(n)]
    return lax.ppermute(x, "tensor", pairs)


def ring_sources(n):
    ring = ring_order(n)
    pos = {r: p for p, r in enumerate(ring)}
    return [[ring[(pos[r] - s) % n] for s in range(n)] for r in range(n)]


def stages_of(n):
    if n <= 8:
        inter = list(range(2, n, 2))
        return ([[1]] if n > 1 else []) + ([inter] if inter else [])
    out, bit = [], 1
    while bit < n:
        out.append([bit])
        bit *= 2
    return out


def gather_dp(x, n):
    parts = [((0,), x[None])]
    for stage in reversed(stages_of(n)):
        new = []
        for mask in stage:
            for masks, arr in parts:
                new.append((tuple(k ^ mask for k in masks), xor_send(arr, "dp", n, mask)))
        parts = parts + new
        if n > 8 and stage != [1]:
            parts = [
                (sum((m for m, _ in parts), ()), jnp.concatenate([a for _, a in parts], axis=0))
            ]
    return parts


def scatter_dp(even, odd, n, later):
    got = xor_send(odd, "dp", n, 1)
    masks = list(range(0, n, 2))
    own = {k: even[i] for i, k in enumerate(masks)}
    new = {k: got[i] for i, k in enumerate(masks)}
    own = {k: (own[k].astype(F4) + new[k].astype(F4)).astype(BF) for k in masks}
    stages = stages_of(n)[1:]
    for at, stage in enumerate(stages):
        span = 0
        for m in stage:
            span |= m
        rest = [k for k in masks if not k & span]
        recv = []
        for m in stage:
            pack = [own[k ^ m] for k in rest]
            send = pack[0] if len(pack) == 1 else jnp.stack(pack)
            back = xor_send(send, "dp", n, m)
            recv.append([back] if len(pack) == 1 else [back[i] for i in range(len(pack))])
        masks = rest
        if at == len(stages) - 1:
            return [own[0]] + [r[0] for r in recv]
        own = {
            k: sum((r[i].astype(F4) for r in recv), own[k].astype(F4)).astype(BF)
            for i, k in enumerate(rest)
        }
    return [own[0]]


def add_all(parts):
    return sum((p.astype(F4) for p in parts[1:]), parts[0].astype(F4))


def moments(v, eps_rows):
    center = v - jnp.mean(v, axis=-1, keepdims=True)
    inv = lax.rsqrt(jnp.mean(center * center, axis=-1, keepdims=True) + eps_rows)
    return center * inv, inv


def norm_back(z, normed, inv):
    return inv * (
        z
        - jnp.mean(z, axis=-1, keepdims=True)
        - normed * jnp.mean(z * normed, axis=-1, keepdims=True)
    )


def exact(ref, lo, hi):
    return ref[lo:hi, :].astype(BF)


GAIN, BIAS, OUTB, QVB, ROUTER, DBIAS, UBIAS, NROWS = 0, 2, 4, 5, 8, 16, 24, 32


def assemble_kernel(masks, ids, *refs):
    pieces, (w_ref, rows_ref) = refs[:-2], refs[-2:]
    me, met = ids[0], ids[1]
    rows_ref[...] = jnp.zeros(rows_ref.shape, F4)
    lane = lax.broadcasted_iota(jnp.int32, (SMALL, LANES), 1)
    low = lane < HALF
    where_of = {}
    for group, ref in zip(masks, pieces):
        dr = (ref.shape[2] - SMALL) // 4
        for idx, mask in enumerate(group):
            i = jnp.bitwise_xor(me, mask)
            where_of[mask] = (ref, idx)
            for jm in range(ref.shape[1]):
                j = jnp.bitwise_xor(met, jm)
                for s in range(4):
                    w_ref[
                        s,
                        pl.ds(pl.multiple_of(i * dr, dr), dr),
                        pl.ds(pl.multiple_of(j * LANES, LANES), LANES),
                    ] = ref[idx, jm, s * dr : (s + 1) * dr, :]
    odd = jnp.bitwise_and(me, 1) == 1
    nt = pieces[0].shape[1]

    def small(mask, jm):
        ref, idx = where_of[mask]
        return ref[idx, jm, 4 * dr :, :].astype(F4)

    for mask in range(0, len(where_of), 2):
        a, b = small(mask, 0), small(mask + 1, 0)
        first, second = jnp.where(odd, b, a), jnp.where(odd, a, b)
        lo = jnp.where(low, first, pltpu.roll(second, HALF, 1))
        hi = jnp.where(low, pltpu.roll(first, HALF, 1), second)
        tile = jnp.right_shift(jnp.bitwise_xor(me, mask), 1)
        at = pl.ds(pl.multiple_of(tile * LANES, LANES), LANES)
        rows_ref[0:5, at] = lo[0:5]
        rows_ref[ROUTER : ROUTER + EXPERTS, at] = lo[5:9]
        rows_ref[DBIAS : DBIAS + EXPERTS, at] = lo[9:13]
        rows_ref[UBIAS : UBIAS + EXPERTS, at] = hi[0:4]
    qr = LANES // len(where_of)
    mine = jnp.logical_and(lane >= HALF, lane < HALF + qr)
    for jm in range(nt):
        j = jnp.bitwise_xor(met, jm)
        total = jnp.zeros((SMALL, LANES), F4)
        for mask in range(len(where_of)):
            i = jnp.bitwise_xor(me, mask)
            part = jnp.where(mine, small(mask, jm), 0.0)
            total = total + pltpu.roll(part, jnp.bitwise_and(HALF + i * qr, LANES - 1), 1)
        rows_ref[QVB : QVB + 2, pl.ds(pl.multiple_of(j * LANES, LANES), LANES)] = total[4:6]


def assemble(ids, weights, width):
    masks = [m for m, _ in weights]
    arrays = [a for _, a in weights]
    return pl.pallas_call(
        partial(assemble_kernel, masks),
        out_shape=[
            jax.ShapeDtypeStruct((4, width, width), BF),
            jax.ShapeDtypeStruct((NROWS, width), F4),
        ],
        in_specs=[SM] + [VM] * len(arrays),
        out_specs=[VM, VM],
        compiler_params=params(),
        cost_estimate=cost(2),
        name="assemble",
    )(ids, *arrays)


def attn_forward_kernel(
    nimg, x_ref, rows_ref, w_ref, hn2_ref, x1_ref, q_ref, k_ref, v_ref, o_ref, pb_ref
):
    width = x_ref.shape[1]
    x = x_ref[...].astype(F4)
    n1, _ = moments(x, EPS)
    hn1 = (n1 * rows_ref[0:1, :] + rows_ref[2:3, :]).astype(BF)
    q_ref[...] = (mm(hn1, w_ref[0]) + rows_ref[5:6, :]).astype(BF)
    k_ref[...] = mm(hn1, w_ref[1]).astype(BF)
    v_ref[...] = (mm(hn1, w_ref[2]) + rows_ref[6:7, :]).astype(BF)
    lane = lax.broadcasted_iota(jnp.int32, (PAD, LANES), 1)
    col = lax.broadcasted_iota(jnp.int32, (PAD, PAD), 1)
    for img in range(nimg):
        at = slice(img * PAD, (img + 1) * PAD)
        for pair in range(width // LANES):
            cols = slice(pair * LANES, (pair + 1) * LANES)
            qp, kp, vp = q_ref[at, cols], k_ref[at, cols], v_ref[at, cols]
            acc = jnp.zeros((PAD, LANES), F4)
            for half in range(2):
                mine = (lane < HD) if half == 0 else (lane >= HD)
                qm = jnp.where(mine, qp * jnp.asarray(HD ** (-0.5), BF), jnp.zeros_like(qp))
                s = mm(qm, kp, NT)
                s = jnp.where(col < SEQ, s, NEG)
                e = jnp.exp(s - jnp.max(s, axis=-1, keepdims=True))
                p = (e * (1.0 / jnp.sum(e, axis=-1, keepdims=True))).astype(BF)
                pb_ref[img * (width // HD) + 2 * pair + half] = p
                acc = acc + mm(p, jnp.where(mine, vp, jnp.zeros_like(vp)))
            o_ref[at, cols] = acc.astype(BF)
    x1 = x + (mm(o_ref[...], w_ref[3], NT) + rows_ref[4:5, :])
    x1_ref[...] = x1
    n2, _ = moments(x1, EPS)
    hn2_ref[...] = (n2 * rows_ref[1:2, :] + rows_ref[3:4, :]).astype(BF)


def attn_forward(x, rows, full, nimg):
    count, width = x.shape
    heads = width // HD
    low = jax.ShapeDtypeStruct((count, width), BF)
    shapes = [
        low,
        jax.ShapeDtypeStruct((count, width), F4),
        low,
        low,
        low,
        low,
        jax.ShapeDtypeStruct((nimg * heads, PAD, PAD), BF),
    ]
    return pl.pallas_call(
        partial(attn_forward_kernel, nimg),
        out_shape=shapes,
        in_specs=[VM] * 3,
        out_specs=[VM] * len(shapes),
        compiler_params=params(),
        cost_estimate=cost(9),
        name="attn_forward",
    )(x, rows, full)


def gather_experts_kernel(masks, ids, *refs):
    pieces, (up_ref, dn_ref) = refs[:-2], refs[-2:]
    me = ids[0]
    for group, ref in zip(masks, pieces):
        dr, ff = ref.shape[3], ref.shape[4]
        for idx, mask in enumerate(group):
            at = pl.ds(pl.multiple_of(jnp.bitwise_xor(me, mask) * dr, dr), dr)
            for e in range(EXPERTS):
                up_ref[at, e * ff : (e + 1) * ff] = ref[idx, 0, e]
                dn_ref[at, e * ff : (e + 1) * ff] = ref[idx, 1, e]


def gather_experts(ids, weights, width):
    masks = [m for m, _ in weights]
    arrays = [a for _, a in weights]
    whole = jax.ShapeDtypeStruct((width, EXPERTS * arrays[0].shape[4]), BF)
    return pl.pallas_call(
        partial(gather_experts_kernel, masks),
        out_shape=[whole, whole],
        in_specs=[SM] + [VM] * len(arrays),
        out_specs=[VM, VM],
        compiler_params=params(),
        cost_estimate=cost(3),
        name="gather_experts",
    )(ids, *arrays)


def normal_parts(u):
    bell = jnp.exp(-0.5 * (u * u))
    t = 1.0 / (1.0 + (0.3275911 * 2.0 ** (-0.5)) * jnp.abs(u))
    poly = 0.5 * 1.061405429 * t + 0.5 * (-1.453152027)
    poly = poly * t + 0.5 * 1.421413741
    poly = poly * t + 0.5 * (-0.284496736)
    poly = poly * t + 0.5 * 0.254829592
    tail = poly * t * bell
    return jnp.where(u > 0.0, 1.0 - tail, tail), bell


def expert_kernel(
    nimg, shard, ids, keep_ref, hn2_ref, cot_ref, rows_ref, up_ref, dn_ref, m_ref, d_ref, hg_ref, dhp_ref, sm_ref
):
    own = shard == 0
    count = hn2_ref.shape[0]
    ff = hg_ref.shape[1] // EXPERTS
    hn2, cot = hn2_ref[...], cot_ref[...]
    router = exact(rows_ref, ROUTER, ROUTER + 8)
    lane = lax.broadcasted_iota(jnp.int32, (count, 8), 1)
    logits = jnp.where(lane < EXPERTS, mm(hn2, router, NT), NEG)
    e = jnp.exp(logits - jnp.max(logits, axis=-1, keepdims=True))
    probs = e / jnp.sum(e, axis=-1, keepdims=True)
    tile = ids[2 + shard] * nimg
    keep = jnp.concatenate([keep_ref[tile + i] for i in range(nimg)], axis=0)
    on = jnp.logical_or(lane == keep[:, 0:1], lane == keep[:, 1:2])
    gates = jnp.where(on, probs, 0.0).astype(BF)
    gates_f = gates.astype(F4)
    dp = jnp.zeros((count, 8), F4)
    if own:
        dbias = exact(rows_ref, DBIAS, DBIAS + 8)
        dp = mm(cot, dbias, NT)
    for e in range(EXPERTS):
        cols = slice(e * ff, (e + 1) * ff)
        gate = gates_f[:, e : e + 1]
        u = mm(hn2, up_ref[:, cols]) + rows_ref[UBIAS + e : UBIAS + e + 1, 0:ff]
        phi, bell = normal_parts(u)
        h = u * phi
        slope = phi + u * (bell * 0.3989422804014327)
        r = mm(cot, dn_ref[:, cols])
        dp = dp + jnp.where(lane == e, jnp.sum(h * r, axis=-1, keepdims=True), 0.0)
        hg_ref[:, cols] = (h * gate).astype(BF)
        dhp_ref[:, cols] = (r * slope * gate).astype(BF)
    dp = jnp.where(on, dp, 0.0)
    dl = (probs * (dp - jnp.sum(probs * dp, axis=-1, keepdims=True))).astype(BF)
    d_ref[...] = (mm(dhp_ref[...], up_ref[...], NT) + mm(dl, router)).astype(BF)
    m = mm(hg_ref[...], dn_ref[...], NT)
    sm_ref[0:8, :] = mm(dl, hn2, TN)
    if own:
        m = m + mm(gates, dbias)
        sm_ref[8:16, :] = mm(gates, cot, TN)
    else:
        sm_ref[8:16, :] = jnp.zeros((8, sm_ref.shape[1]), F4)
    m_ref[...] = m.astype(BF)


def expert_shard(ids, keep, hn2, cot, rows, up, dn, nimg, shard):
    count, width = hn2.shape
    wide = jax.ShapeDtypeStruct((count, up.shape[1]), BF)
    low = jax.ShapeDtypeStruct((count, width), BF)
    return pl.pallas_call(
        partial(expert_kernel, nimg, shard),
        out_shape=[low, low, wide, wide, jax.ShapeDtypeStruct((16, width), F4)],
        in_specs=[SM] + [VM] * 6,
        out_specs=[VM] * 5,
        compiler_params=params(),
        cost_estimate=cost(7),
        name="expert_shard",
    )(ids, keep, hn2, cot, rows, up, dn)


def expert_grad_kernel(nt, gmasks, ids, *refs):
    hn2s, cots, hgs, dhps = (refs[i * nt : (i + 1) * nt] for i in range(4))
    gub_ref = refs[4 * nt]
    grads = refs[4 * nt + 1 : 4 * nt + 1 + len(gmasks)]
    res_ref = refs[4 * nt + 1 + len(gmasks)]
    me = ids[0]
    ones = jnp.ones((8, hn2s[0].shape[0]), BF)
    sums = None
    for which in range(2):
        total = None
        for s in range(nt):
            if which == 0:
                term = mm(hn2s[s][...], dhps[s][...], TN)
                part = mm(ones, dhps[s][...])
                sums = part if sums is None else sums + part
            else:
                term = mm(cots[s][...], hgs[s][...], TN)
            total = term if total is None else total + term
        res_ref[...] = total
        for group, ref in zip(gmasks, grads):
            dr = ref.shape[3]
            for idx, mask in enumerate(group):
                at = pl.ds(pl.multiple_of(jnp.bitwise_xor(me, mask) * dr, dr), dr)
                ref[idx, which, 0] = res_ref[at, :].astype(BF)
    gub_ref[...] = sums[0:1, :]


def expert_grads(ids, hn2s, cots, hgs, dhps, gmasks, dr):
    nt = len(hn2s)
    count, width = hn2s[0].shape
    ff = hgs[0].shape[1] // EXPERTS
    fixed = pl.BlockSpec((count, width), lambda e: (0, 0))
    moving = pl.BlockSpec((count, ff), lambda e: (0, e))
    return pl.pallas_call(
        partial(expert_grad_kernel, nt, gmasks),
        grid=(EXPERTS,),
        out_shape=[jax.ShapeDtypeStruct((EXPERTS, 1, ff), F4)]
        + [jax.ShapeDtypeStruct((len(m), 2, EXPERTS, dr, ff), BF) for m in gmasks],
        in_specs=[SM] + [fixed] * (2 * nt) + [moving] * (2 * nt),
        out_specs=[pl.BlockSpec((None, 1, ff), lambda e: (e, 0, 0))]
        + [pl.BlockSpec((len(m), 2, 1, dr, ff), lambda e: (0, 0, e, 0, 0)) for m in gmasks],
        scratch_shapes=[pltpu.VMEM((width, ff), F4)],
        compiler_params=params(),
        cost_estimate=cost(9),
        name="expert_grads",
    )(ids, *hn2s, *cots, *hgs, *dhps)


def attn_backward_kernel(nimg, nsm, gmasks, direct, ids, *refs):
    ins = 13 + nsm
    (recv_ref, own_ref, x_ref, cot_ref, x1_ref, q_ref, k_ref, v_ref, o_ref, pb_ref) = refs[:10]
    rows_ref, w_ref, gub_ref = refs[10:13]
    sms = refs[13:ins]
    gtok_ref = refs[ins]
    ngrads = len(gmasks)
    grads = refs[ins + 1 : ins + 1 + ngrads]
    small_ref, do_ref, dq_ref, dk_ref, dv_ref, da_ref, hn1_ref, res_ref = refs[ins + 1 + ngrads :]
    width = x_ref.shape[1]
    dh = recv_ref[...].astype(F4) + own_ref[...].astype(F4)
    cot_f = cot_ref[...].astype(F4)
    n2, inv2 = moments(x1_ref[...], EPS)
    small_ref[...] = jnp.zeros(small_ref.shape, F4)
    small_ref[1:2, :] = jnp.sum(dh * n2, axis=0, keepdims=True)
    small_ref[3:4, :] = jnp.sum(dh, axis=0, keepdims=True)
    dx1 = cot_f + norm_back(dh * rows_ref[1:2, :], n2, inv2)
    da = dx1.astype(BF)
    da_ref[...] = da
    gtok_ref[...] = dx1
    small_ref[4:5, :] = jnp.sum(da.astype(F4), axis=0, keepdims=True)
    do_ref[...] = mm(da, w_ref[3]).astype(BF)
    lane = lax.broadcasted_iota(jnp.int32, (PAD, LANES), 1)
    scale = HD ** (-0.5)
    for img in range(nimg):
        at = slice(img * PAD, (img + 1) * PAD)
        for pair in range(width // LANES):
            cols = slice(pair * LANES, (pair + 1) * LANES)
            qp, kp, vp, dop = q_ref[at, cols], k_ref[at, cols], v_ref[at, cols], do_ref[at, cols]
            zero = jnp.zeros_like(qp)
            dq = jnp.zeros((PAD, LANES), F4)
            dk = jnp.zeros((PAD, LANES), F4)
            dv = jnp.zeros((PAD, LANES), F4)
            for half in range(2):
                mine = (lane < HD) if half == 0 else (lane >= HD)
                pb = pb_ref[img * (width // HD) + 2 * pair + half]
                dom = jnp.where(mine, dop, zero)
                dpb = mm(dom, vp, NT)
                p = pb.astype(F4)
                ds = (p * (dpb - jnp.sum(p * dpb, axis=-1, keepdims=True))).astype(BF)
                dv = dv + mm(pb, dom, TN)
                dq = dq + mm(ds, jnp.where(mine, kp, zero))
                dk = dk + mm(ds, jnp.where(mine, qp, zero), TN)
            dq_ref[at, cols] = (dq * scale).astype(BF)
            dk_ref[at, cols] = (dk * scale).astype(BF)
            dv_ref[at, cols] = dv.astype(BF)
    small_ref[QVB : QVB + 1, :] = jnp.sum(dq_ref[...].astype(F4), axis=0, keepdims=True)
    small_ref[QVB + 1 : QVB + 2, :] = jnp.sum(dv_ref[...].astype(F4), axis=0, keepdims=True)
    dh1 = (
        mm(dq_ref[...], w_ref[0], NT)
        + mm(dk_ref[...], w_ref[1], NT)
        + mm(dv_ref[...], w_ref[2], NT)
    )
    n1, inv1 = moments(x_ref[...].astype(F4), EPS)
    hn1_ref[...] = (n1 * rows_ref[0:1, :] + rows_ref[2:3, :]).astype(BF)
    small_ref[0:1, :] = jnp.sum(dh1 * n1, axis=0, keepdims=True)
    small_ref[2:3, :] = jnp.sum(dh1, axis=0, keepdims=True)
    gtok_ref[...] = gtok_ref[...] + norm_back(dh1 * rows_ref[0:1, :], n1, inv1)
    total = sms[0][...]
    for ref in sms[1:]:
        total = total + ref[...]
    small_ref[ROUTER : ROUTER + 16, :] = total
    for e in range(EXPERTS):
        small_ref[UBIAS + e : UBIAS + e + 1, 0 : gub_ref.shape[2]] = gub_ref[e]
    me, met = ids[0], ids[1]
    for s in range(4):
        left, right = [(hn1_ref, dq_ref), (hn1_ref, dk_ref), (hn1_ref, dv_ref), (da_ref, o_ref)][s]
        res_ref[...] = mm(left[...], right[...], TN)
        for group, ref in zip(gmasks, grads):
            dr = (ref.shape[2] - (SMALL if direct else 0)) // 4
            for idx, mask in enumerate(group):
                i = jnp.bitwise_xor(me, mask)
                for jm in range(ref.shape[1]):
                    j = jnp.bitwise_xor(met, jm)
                    ref[idx, jm, s * dr : (s + 1) * dr, :] = res_ref[
                        pl.ds(pl.multiple_of(i * dr, dr), dr),
                        pl.ds(pl.multiple_of(j * LANES, LANES), LANES),
                    ].astype(BF)
    if not direct:
        return
    lane = lax.broadcasted_iota(jnp.int32, (SMALL, LANES), 1)
    row = lax.broadcasted_iota(jnp.int32, (SMALL, LANES), 0)
    nd = sum(len(g) for g in gmasks)
    qr = LANES // nd
    blank = jnp.zeros((3, LANES), F4)
    for group, ref in zip(gmasks, grads):
        for idx, mask in enumerate(group):
            i = jnp.bitwise_xor(me, mask)
            odd = jnp.bitwise_and(i, 1) == 1
            tile = pl.ds(pl.multiple_of(jnp.right_shift(i, 1) * LANES, LANES), LANES)
            t = jnp.concatenate(
                [small_ref[0:5, tile], small_ref[ROUTER : ROUTER + 4, tile], small_ref[DBIAS : DBIAS + 4, tile], blank],
                axis=0,
            )
            lo = jnp.where(odd, pltpu.roll(t, HALF, 1), t)
            lo = jnp.where(lane < HALF, lo, 0.0)
            b = jnp.concatenate([small_ref[UBIAS : UBIAS + 8, tile], jnp.zeros((8, LANES), F4)], axis=0)
            hi = jnp.where(odd, b, pltpu.roll(b, HALF, 1))
            hi = jnp.where(jnp.logical_and(lane >= HALF, row < EXPERTS), hi, 0.0)
            for jm in range(ref.shape[1]):
                j = jnp.bitwise_xor(met, jm)
                g = small_ref[0:8, pl.ds(pl.multiple_of(j * LANES, LANES), LANES)]
                g = pltpu.roll(g, 7, 0)
                g = pltpu.roll(g, jnp.bitwise_and(HALF - i * qr + LANES, LANES - 1), 1)
                g = jnp.concatenate([g, jnp.zeros((8, LANES), F4)], axis=0)
                mine = jnp.logical_and(lane >= HALF, lane < HALF + qr)
                mine = jnp.logical_and(mine, jnp.logical_and(row >= 4, row < 6))
                block = lo + jnp.where(mine, g, 0.0)
                if jm == 0:
                    block = block + hi
                ref[idx, jm, 4 * dr :, :] = block.astype(BF)


def attn_backward(ids, recv, own, x, cot, saved, rows, full, gub, sms, gmasks, direct, nt, dr):
    x1, q, k, v, o, pb = saved
    count, width = x.shape
    nimg = count // PAD
    extra = SMALL if direct else 0
    shapes = [jax.ShapeDtypeStruct((count, width), F4)]
    shapes += [jax.ShapeDtypeStruct((len(m), nt, 4 * dr + extra, LANES), BF) for m in gmasks]
    shapes += [jax.ShapeDtypeStruct((NROWS, width), F4)]
    low = pltpu.VMEM((count, width), BF)
    return pl.pallas_call(
        partial(attn_backward_kernel, nimg, len(sms), gmasks, direct),
        out_shape=shapes,
        in_specs=[SM] + [VM] * (13 + len(sms)),
        out_specs=[VM] * len(shapes),
        scratch_shapes=[low] * 6 + [pltpu.VMEM((width, width), F4)],
        compiler_params=params(),
        cost_estimate=cost(16),
        name="attn_backward",
    )(ids, recv, own, x, cot, x1, q, k, v, o, pb, rows, full, gub, *sms)


def per_device(
    nd,
    nt,
    tokens,
    cotangent,
    routes,
    slots,
    norm_gains,
    norm_biases,
    w_qkv,
    qv_bias,
    w_out,
    out_bias,
    w_router,
    w_up,
    up_bias,
    w_down,
    down_bias,
):
    me = lax.axis_index("dp").astype(jnp.int32)
    met = lax.axis_index("tensor").astype(jnp.int32)
    width = tokens.shape[1]
    dr = w_qkv.shape[1]
    fr, qr = up_bias.shape[1], qv_bias.shape[1]
    ff = w_up.shape[2]
    nimg = IMG_DEV // nt
    direct = dr == HALF and fr == HALF and nd * qr == LANES and nd % 2 == 0
    src = jnp.asarray(ring_sources(nt), jnp.int32)[met]
    ids = jnp.concatenate([jnp.stack([me if direct else jnp.zeros_like(me), met]), src])
    even, odd = list(range(0, nd, 2)), list(range(1, nd, 2))

    def canonical(parts):
        if direct:
            return parts
        masks = sum((m for m, _ in parts), ())
        arr = jnp.concatenate([a for _, a in parts], axis=0)
        place = [masks.index(k) for k in range(nd)]
        order = jnp.asarray(place, jnp.int32)[jnp.bitwise_xor(jnp.arange(nd), me)]
        arr = jnp.take(arr, order, axis=0)
        lead = arr.ndim - 2
        arr = jnp.moveaxis(arr, 0, lead - 1)
        arr = arr.reshape(arr.shape[: lead - 1] + (nd * dr,) + arr.shape[-1:])
        return [((0,), arr[None])]

    gmasks = [even, odd] if direct else [[0]]

    def halves(grads, lead, rows):
        if direct:
            return grads
        whole = grads[0][0]
        shape = whole.shape[:lead] + (rows, nd, dr) + whole.shape[-1:]
        whole = jnp.moveaxis(whole.reshape(shape), lead + 1, 0)
        whole = whole.reshape((nd,) + grads[0].shape[1 : lead + 1] + (rows * dr, whole.shape[-1]))
        return [
            jnp.take(whole, jnp.bitwise_xor(jnp.asarray(m, jnp.int32), me), axis=0)
            for m in (even, odd)
        ]

    chunk = jnp.concatenate([w_qkv, w_out.T[None]], axis=0)
    if direct:
        wide = [
            jnp.concatenate(
                [norm_gains, norm_biases, out_bias[None], w_router.T, down_bias, jnp.zeros((3, dr), BF)],
                axis=0,
            ),
            jnp.concatenate(
                [up_bias, jnp.pad(qv_bias, ((0, 0), (0, dr - qr))), jnp.zeros((10, dr), BF)], axis=0
            ),
        ]
        chunk = jnp.concatenate([chunk.reshape(4 * dr, LANES), jnp.concatenate(wide, axis=1)], axis=0)
    chunk_z = jnp.stack([chunk] + [xor_send(chunk, "tensor", nt, m) for m in range(1, nt)])
    weights = gather_dp(chunk_z, nd)
    if direct:
        full, rows = assemble(ids, weights, width)
    else:
        full = canonical(weights)[0][1][0]
        at = jnp.bitwise_xor(jnp.arange(nt), met)
        full = jnp.take(full, at, axis=0).transpose(1, 2, 0, 3).reshape(4, width, width)

        def whole(v):
            return lax.all_gather(v, "dp", axis=v.ndim - 1, tiled=True).astype(F4)

        qvb = lax.all_gather(whole(qv_bias), "tensor", axis=1, tiled=True)
        four = jnp.zeros((4, width), F4)
        rows = [whole(norm_gains), whole(norm_biases), whole(out_bias[None]), qvb]
        rows += [jnp.zeros((1, width), F4), whole(w_router.T), four, whole(down_bias), four]
        rows += [jnp.pad(whole(up_bias), ((0, 0), (0, width - nd * fr))), four]
        rows = jnp.concatenate(rows, axis=0)

    def images(v):
        return jnp.concatenate(
            [jnp.pad(v[i * SEQ : (i + 1) * SEQ], ((0, PAD - SEQ), (0, 0))) for i in range(nimg)]
        )

    x, cot = images(tokens), images(cotangent)
    cots = [cot]
    for s in range(1, nt):
        cots.append(ring_step(cots[-1], nt, False))

    keep = jnp.where(slots >= 0, routes, -1).reshape(nt * nimg, SEQ, 2)
    keep = jnp.pad(keep, ((0, 0), (0, PAD - SEQ), (0, 0)), constant_values=-1)

    both = jnp.stack([w_up, w_down.transpose(0, 2, 1)])
    expert_weights = gather_dp(both, nd)
    if direct:
        up, dn = gather_experts(ids, expert_weights, width)
    else:
        flat = canonical(expert_weights)[0][1][0]
        up, dn = flat.transpose(0, 2, 1, 3).reshape(2, width, EXPERTS * ff)

    saved = attn_forward(x, rows, full, nimg)
    hn2s = [saved[0]]
    for s in range(1, nt):
        hn2s.append(ring_step(hn2s[-1], nt, False))
    shards = [
        expert_shard(ids, keep, hn2s[s], cots[s], rows, up, dn, nimg, s) for s in range(nt)
    ]

    def ring_sum(parts):
        total = parts[1]
        for s in range(2, nt):
            total = add_all([ring_step(total, nt, False), parts[s]]).astype(BF)
        return ring_step(total, nt, False)

    recv = ring_sum([r[1] for r in shards])
    res = expert_grads(
        ids,
        hn2s,
        cots,
        [r[2] for r in shards],
        [r[3] for r in shards],
        gmasks,
        dr if direct else width,
    )
    gub = res[0]
    egrads = halves(res[1:], 2, 1)
    expert_sum = add_all(scatter_dp(egrads[0], egrads[1], nd, None))

    res = attn_backward(
        ids,
        recv,
        shards[0][1],
        x,
        cot,
        saved[1:],
        rows,
        full,
        gub,
        [r[4] for r in shards],
        gmasks,
        direct,
        nt,
        dr if direct else width,
    )
    gtok, flat = res[0], res[-1]
    grads = halves(res[1:-1], 1, 4)
    held = add_all(scatter_dp(grads[0], grads[1], nd, None)).astype(BF)
    mine = [held[0]] + [xor_send(held[m], "tensor", nt, m) for m in range(1, nt)]
    mine = add_all(mine)

    m_got = ring_sum([r[0] for r in shards])

    def rows_of(v):
        return jnp.concatenate([v[i * PAD : i * PAD + SEQ] for i in range(nimg)])

    layer_out = rows_of(saved[1] + (m_got.astype(F4) + shards[0][0].astype(F4)))
    grad_tokens = rows_of(gtok)

    if direct:
        small = mine[4 * dr :]
        g_gain, g_bias, g_outb = small[0:2, :dr], small[2:4, :dr], small[4, :dr]
        g_router, g_dbias = small[5:9, :dr].T, small[9:13, :dr]
        g_ub, g_qvb = small[0:4, HALF:], small[4:6, HALF : HALF + qr]
    else:
        flat = lax.psum(flat, ("dp", "tensor"))
        g_ub = lax.psum(res[-1], "dp")
        g_ub = lax.dynamic_slice(g_ub, (UBIAS, me * fr), (EXPERTS, fr))
        cut = lax.dynamic_slice(flat, (0, me * dr), (NROWS, dr))
        g_gain, g_bias, g_outb = cut[0:2], cut[2:4], cut[4]
        g_router, g_dbias = cut[ROUTER : ROUTER + 4].T, cut[DBIAS : DBIAS + 4]
        g_qvb = lax.dynamic_slice(flat, (QVB, (met * nd + me) * qr), (2, qr))
    return (
        layer_out,
        grad_tokens,
        g_gain,
        g_bias,
        mine[: 3 * dr].reshape(3, dr, LANES),
        g_qvb,
        mine[3 * dr : 4 * dr].T,
        g_outb,
        g_router,
        expert_sum[0],
        g_ub,
        expert_sum[1].transpose(0, 2, 1),
        g_dbias,
    )


def solution(mesh):
    nd, nt = mesh.shape["dp"], mesh.shape["tensor"]
    placed = (
        P(("dp", "tensor"), None),
        P(("dp", "tensor"), None),
        P("dp", None),
        P("dp", None),
        P(None, "dp"),
        P(None, "dp"),
        P(None, "dp", "tensor"),
        P(None, ("tensor", "dp")),
        P("tensor", "dp"),
        P("dp"),
        P("dp", None),
        P(None, "dp", "tensor"),
        P(None, ("tensor", "dp")),
        P(None, "tensor", "dp"),
        P(None, "dp"),
    )
    return jax.shard_map(
        partial(per_device, nd, nt),
        mesh=mesh,
        in_specs=placed,
        out_specs=(
            P(("dp", "tensor"), None),
            P(("dp", "tensor"), None),
            P(None, "dp"),
            P(None, "dp"),
            P(None, "dp", "tensor"),
            P(None, ("tensor", "dp")),
            P("tensor", "dp"),
            P("dp"),
            P("dp", None),
            P(None, "dp", "tensor"),
            P(None, ("tensor", "dp")),
            P(None, "tensor", "dp"),
            P(None, "dp"),
        ),
        check_vma=False,
    )
```

```python
from functools import partial

import jax
import jax.numpy as jnp
import numpy as np
from jax import lax
from jax.experimental import pallas as pl
from jax.experimental.pallas import tpu as pltpu
from jax.sharding import PartitionSpec as P

HD = 64
EXPERTS = 4
SEQ = 197
IMG_DEV = 8
PAD = 200
SMALL = 16
EPS = 1e-06
BF = jnp.bfloat16
F4 = jnp.float32
NEG = -1e30
LANES = 128
HALF = 64

NN = (((1,), (0,)), ((), ()))
NT = (((1,), (1,)), ((), ()))
TN = (((0,), (0,)), ((), ()))

VM = pl.BlockSpec()
SM = pl.BlockSpec(memory_space=pltpu.SMEM)
ANY = pl.BlockSpec(memory_space=pltpu.HBM)


def mm(a, b, dims=NN):
    return lax.dot_general(a, b, dims, preferred_element_type=F4)


def params(mib=12):
    return pltpu.CompilerParams(vmem_limit_bytes=mib * 1024 * 1024)


def cost(us):
    return pl.CostEstimate(flops=0, transcendentals=0, bytes_accessed=int(us * 3.3e4))


def xor_send(x, axis, n, mask):
    return lax.ppermute(x, axis, [(i, i ^ mask) for i in range(n)])


def ring_order(n):
    return [0] + list(range(1, n, 2)) + list(range(2, n, 2))[::-1]


def ring_step(x, n, back):
    ring = ring_order(n)
    pairs = [(ring[p], ring[(p + (-1 if back else 1)) % n]) for p in range(n)]
    return lax.ppermute(x, "tensor", pairs)


def ring_sources(n):
    ring = ring_order(n)
    pos = {r: p for p, r in enumerate(ring)}
    return [[ring[(pos[r] - s) % n] for s in range(n)] for r in range(n)]


def stages_of(n):
    if n <= 8:
        inter = list(range(2, n, 2))
        return ([[1]] if n > 1 else []) + ([inter] if inter else [])
    out, bit = [], 1
    while bit < n:
        out.append([bit])
        bit *= 2
    return out


def gather_dp(x, n):
    parts = [((0,), x[None])]
    for stage in reversed(stages_of(n)):
        new = []
        for mask in stage:
            for masks, arr in parts:
                new.append((tuple(k ^ mask for k in masks), xor_send(arr, "dp", n, mask)))
        parts = parts + new
        if n > 8 and stage != [1]:
            parts = [
                (sum((m for m, _ in parts), ()), jnp.concatenate([a for _, a in parts], axis=0))
            ]
    return parts


def scatter_dp(even, odd, n):
    got = xor_send(odd, "dp", n, 1)
    masks = list(range(0, n, 2))
    own = {k: even[i] for i, k in enumerate(masks)}
    new = {k: got[i] for i, k in enumerate(masks)}
    own = {k: (own[k].astype(F4) + new[k].astype(F4)).astype(BF) for k in masks}
    stages = stages_of(n)[1:]
    for at, stage in enumerate(stages):
        span = 0
        for m in stage:
            span |= m
        rest = [k for k in masks if not k & span]
        recv = []
        for m in stage:
            pack = [own[k ^ m] for k in rest]
            send = pack[0] if len(pack) == 1 else jnp.stack(pack)
            back = xor_send(send, "dp", n, m)
            recv.append([back] if len(pack) == 1 else [back[i] for i in range(len(pack))])
        masks = rest
        if at == len(stages) - 1:
            return [own[0]] + [r[0] for r in recv]
        own = {
            k: sum((r[i].astype(F4) for r in recv), own[k].astype(F4)).astype(BF)
            for i, k in enumerate(rest)
        }
    return [own[0]]


def to(x, mask):
    return xor_send(x, "dp", 8, mask)


def plane_first(x):
    return x, to(x, 2), to(x, 4)


def plane_second(x, from_x, from_y):
    half = x.shape[0] // 2
    far = [to(from_x[:half], 4), to(from_y[half:], 2)]
    return jnp.stack([x, from_x, from_y, jnp.concatenate(far, axis=0)])


def gather_cores(quad):
    return [((0, 2, 4, 6), quad), ((1, 3, 5, 7), to(quad, 1))]


def scatter_first(even, got):
    half = even.shape[1] // 2
    low, high = slice(0, half), slice(half, 2 * half)

    def both(mask, part):
        return [(even, (mask // 2, part)), (got, (mask // 2, part))]

    return sums(
        [
            [both(0, low), both(4, low)],
            [both(0, high), both(2, high)],
            [both(2, low), both(6, low)],
            [both(4, high), both(6, high)],
        ]
    )


def scatter_second(keep_x, keep_y, got_x, got_y):
    pairs = [(keep_x, got_x), (keep_y, got_y)]
    return sums([[[(k, at), (g, at)]] for at in (1, 0) for k, g in pairs])


def after(x, *first):
    return lax.optimization_barrier((x, *first))[0]


def arrays(parts):
    return [a for _, a in parts]


def sums_kernel(outs, count, *refs):
    for groups, out in zip(outs, refs[count:]):
        for j, group in enumerate(groups):
            total = None
            for n, at in group:
                term = (refs[n][...] if at is None else refs[n][at]).astype(F4)
                total = term if total is None else total + term
            if len(groups) == 1:
                out[...] = total.astype(out.dtype)
            else:
                out[j] = total.astype(out.dtype)


def sums(outs):
    known, flat, index, shapes = {}, [], [], []
    for groups in outs:
        index.append([])
        for group in groups:
            index[-1].append([])
            for v, at in group:
                if id(v) not in known:
                    known[id(v)] = len(flat)
                    flat.append(v)
                index[-1][-1].append((known[id(v)], at))
        v, at = groups[0][0]
        shape = v.shape if at is None else np.broadcast_to(0, v.shape)[at].shape
        shapes.append(shape if len(groups) == 1 else (len(groups),) + shape)
    return pl.pallas_call(
        partial(sums_kernel, index, len(flat)),
        out_shape=[jax.ShapeDtypeStruct(v, BF) for v in shapes],
        in_specs=[VM] * len(flat),
        out_specs=[VM] * len(shapes),
        compiler_params=params(16),
        cost_estimate=cost(1),
        name="sums",
    )(*flat)


def finish_kernel(dr, qr, *refs):
    parts, outs = refs[:4], refs[4:]
    g_qkv, g_out, g_gain, g_bias, g_outb, g_router, g_dbias, g_ub, g_qvb = outs
    total = parts[0][...].astype(F4)
    for ref in parts[1:]:
        total = total + ref[...].astype(F4)
    for s in range(3):
        g_qkv[s] = total[s * dr : (s + 1) * dr]
    g_out[...] = total[3 * dr : 4 * dr]
    low = total[4 * dr :]
    high = pltpu.roll(low, HALF, 1)
    g_gain[...] = low[0:2, :HALF]
    g_bias[...] = low[2:4, :HALF]
    g_outb[...] = low[4:5, :HALF]
    g_router[...] = low[5:9, :HALF]
    g_dbias[...] = low[9:13, :HALF]
    g_ub[...] = high[0:4, :HALF]
    g_qvb[...] = high[4:6, :qr]


def finish(parts, dr, qr):
    rows = [(2, HALF), (2, HALF), (1, HALF), (EXPERTS, HALF), (EXPERTS, HALF), (EXPERTS, HALF), (2, qr)]
    shapes = [(3, dr, LANES), (dr, LANES)] + rows
    return pl.pallas_call(
        partial(finish_kernel, dr, qr),
        out_shape=[jax.ShapeDtypeStruct(v, F4) for v in shapes],
        in_specs=[VM] * 4,
        out_specs=[VM] * len(shapes),
        compiler_params=params(),
        cost_estimate=cost(1),
        name="finish",
    )(*parts)


def add_all(parts):
    return sum((p.astype(F4) for p in parts[1:]), parts[0].astype(F4))


def moments(v, eps_rows):
    center = v - jnp.mean(v, axis=-1, keepdims=True)
    inv = lax.rsqrt(jnp.mean(center * center, axis=-1, keepdims=True) + eps_rows)
    return center * inv, inv


def norm_back(z, normed, inv):
    return inv * (
        z
        - jnp.mean(z, axis=-1, keepdims=True)
        - normed * jnp.mean(z * normed, axis=-1, keepdims=True)
    )


def exact(ref, lo, hi):
    return ref[lo:hi, :].astype(BF)


GAIN, BIAS, OUTB, QVB, ROUTER, DBIAS, UBIAS, NROWS = 0, 2, 4, 5, 8, 16, 24, 32


def in_hbm(values):
    return [pltpu.with_memory_space_constraint(v, pltpu.HBM) for v in values]


def run_copies(pairs, sems):
    copies = [pltpu.make_async_copy(a, b, sems.at[n]) for n, (a, b) in enumerate(pairs)]
    for c in copies:
        c.start()
    for c in copies:
        c.wait()


def assemble_kernel(masks, ids, *refs):
    pieces, (w_ref, rows_ref, small_ref, sems) = refs[:-4], refs[-4:]
    me, met = ids[0], ids[1]
    pairs = []
    for group, ref in zip(masks, pieces):
        dr = (ref.shape[2] - SMALL) // 4
        for idx, mask in enumerate(group):
            i = jnp.bitwise_xor(me, mask)
            for jm in range(ref.shape[1]):
                j = jnp.bitwise_xor(met, jm)
                rows_at = pl.ds(pl.multiple_of(i * dr, dr), dr)
                lanes_at = pl.ds(pl.multiple_of(j * LANES, LANES), LANES)
                for s in range(4):
                    pairs.append(
                        (ref.at[idx, jm, s * dr : (s + 1) * dr], w_ref.at[s, rows_at, lanes_at])
                    )
                pairs.append((ref.at[idx, jm, 4 * dr : 4 * dr + SMALL], small_ref.at[mask, jm]))
    run_copies(pairs, sems)
    rows_ref[...] = jnp.zeros(rows_ref.shape, F4)
    lane = lax.broadcasted_iota(jnp.int32, (SMALL, LANES), 1)
    low = lane < HALF
    odd = jnp.bitwise_and(me, 1) == 1
    nd, nt = small_ref.shape[:2]

    def small(mask, jm):
        return small_ref[mask, jm].astype(F4)

    for mask in range(0, nd, 2):
        a, b = small(mask, 0), small(mask + 1, 0)
        first, second = jnp.where(odd, b, a), jnp.where(odd, a, b)
        lo = jnp.where(low, first, pltpu.roll(second, HALF, 1))
        hi = jnp.where(low, pltpu.roll(first, HALF, 1), second)
        tile = jnp.right_shift(jnp.bitwise_xor(me, mask), 1)
        at = pl.ds(pl.multiple_of(tile * LANES, LANES), LANES)
        rows_ref[0:5, at] = lo[0:5]
        rows_ref[ROUTER : ROUTER + EXPERTS, at] = lo[5:9]
        rows_ref[DBIAS : DBIAS + EXPERTS, at] = lo[9:13]
        rows_ref[UBIAS : UBIAS + EXPERTS, at] = hi[0:4]
    qr = LANES // nd
    mine = jnp.logical_and(lane >= HALF, lane < HALF + qr)
    for jm in range(nt):
        j = jnp.bitwise_xor(met, jm)
        total = jnp.zeros((SMALL, LANES), F4)
        for mask in range(nd):
            i = jnp.bitwise_xor(me, mask)
            part = jnp.where(mine, small(mask, jm), 0.0)
            total = total + pltpu.roll(part, jnp.bitwise_and(HALF + i * qr, LANES - 1), 1)
        rows_ref[QVB : QVB + 2, pl.ds(pl.multiple_of(j * LANES, LANES), LANES)] = total[4:6]


def assemble(ids, weights, width):
    masks = [m for m, _ in weights]
    pieces = arrays(weights)
    nd, nt = sum(len(m) for m in masks), pieces[0].shape[1]
    return pl.pallas_call(
        partial(assemble_kernel, masks),
        out_shape=[
            jax.ShapeDtypeStruct((4, width, width), BF),
            jax.ShapeDtypeStruct((NROWS, width), F4),
        ],
        in_specs=[SM] + [ANY] * len(pieces),
        out_specs=[VM, VM],
        scratch_shapes=[
            pltpu.VMEM((nd, nt, SMALL, LANES), BF),
            pltpu.SemaphoreType.DMA((5 * nd * nt,)),
        ],
        compiler_params=params(8),
        cost_estimate=cost(2),
        name="assemble",
    )(ids, *in_hbm(pieces))


def attn_forward_kernel(
    nimg, x_ref, rows_ref, w_ref, hn2_ref, x1_out, q_out, k_out, v_out, o_out, pb_out, *scratch
):
    x1_ref, q_ref, k_ref, v_ref, o_ref, pb_ref, sems = scratch
    heads = w_ref.shape[1] // HD
    copies = []

    def leave(src, dst):
        copies.append(pltpu.make_async_copy(src, dst, sems.at[len(copies)]))
        copies[-1].start()

    width = x_ref.shape[1]
    x = x_ref[...].astype(F4)
    n1, _ = moments(x, EPS)
    hn1 = (n1 * rows_ref[0:1, :] + rows_ref[2:3, :]).astype(BF)
    q_ref[...] = (mm(hn1, w_ref[0]) + rows_ref[5:6, :]).astype(BF)
    k_ref[...] = mm(hn1, w_ref[1]).astype(BF)
    v_ref[...] = (mm(hn1, w_ref[2]) + rows_ref[6:7, :]).astype(BF)
    leave(q_ref, q_out)
    leave(k_ref, k_out)
    leave(v_ref, v_out)
    lane = lax.broadcasted_iota(jnp.int32, (PAD, LANES), 1)
    col = lax.broadcasted_iota(jnp.int32, (PAD, PAD), 1)
    for img in range(nimg):
        at = slice(img * PAD, (img + 1) * PAD)
        for pair in range(width // LANES):
            cols = slice(pair * LANES, (pair + 1) * LANES)
            qp, kp, vp = q_ref[at, cols], k_ref[at, cols], v_ref[at, cols]
            acc = jnp.zeros((PAD, LANES), F4)
            for half in range(2):
                mine = (lane < HD) if half == 0 else (lane >= HD)
                qm = jnp.where(mine, qp * jnp.asarray(HD ** (-0.5), BF), jnp.zeros_like(qp))
                s = mm(qm, kp, NT)
                s = jnp.where(col < SEQ, s, NEG)
                e = jnp.exp(s - jnp.max(s, axis=-1, keepdims=True))
                p = (e * (1.0 / jnp.sum(e, axis=-1, keepdims=True))).astype(BF)
                pb_ref[img * heads + 2 * pair + half] = p
                acc = acc + mm(p, jnp.where(mine, vp, jnp.zeros_like(vp)))
            o_ref[at, cols] = acc.astype(BF)
        mine = pl.ds(img * heads, heads)
        leave(pb_ref.at[mine], pb_out.at[mine])
    leave(o_ref, o_out)
    x1 = x + (mm(o_ref[...], w_ref[3], NT) + rows_ref[4:5, :])
    x1_ref[...] = x1
    leave(x1_ref, x1_out)
    n2, _ = moments(x1, EPS)
    hn2_ref[...] = (n2 * rows_ref[1:2, :] + rows_ref[3:4, :]).astype(BF)
    for c in copies:
        c.wait()


def attn_forward(x, rows, full, nimg):
    count, width = x.shape
    heads = width // HD
    saved = [((count, width), F4)] + [((count, width), BF)] * 4
    saved.append(((nimg * heads, PAD, PAD), BF))
    shapes = [jax.ShapeDtypeStruct((count, width), BF)] + [pltpu.HBM(*v) for v in saved]
    return pl.pallas_call(
        partial(attn_forward_kernel, nimg),
        out_shape=shapes,
        in_specs=[VM] * 3,
        out_specs=[VM] + [ANY] * len(saved),
        scratch_shapes=[pltpu.VMEM(*v) for v in saved] + [pltpu.SemaphoreType.DMA((5 + nimg,))],
        compiler_params=params(),
        cost_estimate=cost(9),
        name="attn_forward",
    )(x, rows, full)


def gather_experts_kernel(masks, ids, *refs):
    pieces, (w_ref, sems) = refs[:-2], refs[-2:]
    me = ids[0]
    pairs = []
    for group, ref in zip(masks, pieces):
        dr, ff = ref.shape[2], ref.shape[3]
        for idx, mask in enumerate(group):
            at = pl.ds(pl.multiple_of(jnp.bitwise_xor(me, mask) * dr, dr), dr)
            for e in range(EXPERTS):
                pairs.append((ref.at[idx, e], w_ref.at[at, e * ff : (e + 1) * ff]))
    run_copies(pairs, sems)


def gather_experts(ids, weights, width):
    masks = [m for m, _ in weights]
    pieces = arrays(weights)
    nd = sum(len(m) for m in masks)
    return pl.pallas_call(
        partial(gather_experts_kernel, masks),
        out_shape=jax.ShapeDtypeStruct((width, EXPERTS * pieces[0].shape[3]), BF),
        in_specs=[SM] + [ANY] * len(pieces),
        out_specs=VM,
        scratch_shapes=[pltpu.SemaphoreType.DMA((EXPERTS * nd,))],
        compiler_params=params(8),
        cost_estimate=cost(3),
        name="gather_experts",
    )(ids, *in_hbm(pieces))


def normal_parts(u):
    bell = jnp.exp(-0.5 * (u * u))
    t = 1.0 / (1.0 + (0.3275911 * 2.0 ** (-0.5)) * jnp.abs(u))
    poly = 0.5 * 1.061405429 * t + 0.5 * (-1.453152027)
    poly = poly * t + 0.5 * 1.421413741
    poly = poly * t + 0.5 * (-0.284496736)
    poly = poly * t + 0.5 * 0.254829592
    tail = poly * t * bell
    return jnp.where(u > 0.0, 1.0 - tail, tail), bell


def expert_kernel(
    nimg, shard, ids, keep_ref, hn2_ref, cot_ref, rows_ref, up_ref, dn_ref, m_ref, d_ref, hg_ref, dhp_ref, sm_ref
):
    own = shard == 0
    count = hn2_ref.shape[0]
    ff = hg_ref.shape[1] // EXPERTS
    hn2, cot = hn2_ref[...], cot_ref[...]
    router = exact(rows_ref, ROUTER, ROUTER + 8)
    lane = lax.broadcasted_iota(jnp.int32, (count, 8), 1)
    logits = jnp.where(lane < EXPERTS, mm(hn2, router, NT), NEG)
    e = jnp.exp(logits - jnp.max(logits, axis=-1, keepdims=True))
    probs = e / jnp.sum(e, axis=-1, keepdims=True)
    tile = ids[2 + shard] * nimg
    keep = jnp.concatenate([keep_ref[tile + i] for i in range(nimg)], axis=0)
    on = jnp.logical_or(lane == keep[:, 0:1], lane == keep[:, 1:2])
    gates = jnp.where(on, probs, 0.0).astype(BF)
    gates_f = gates.astype(F4)
    dp = jnp.zeros((count, 8), F4)
    if own:
        dbias = exact(rows_ref, DBIAS, DBIAS + 8)
        dp = mm(cot, dbias, NT)
    for e in range(EXPERTS):
        cols = slice(e * ff, (e + 1) * ff)
        gate = gates_f[:, e : e + 1]
        u = mm(hn2, up_ref[:, cols]) + rows_ref[UBIAS + e : UBIAS + e + 1, 0:ff]
        phi, bell = normal_parts(u)
        h = u * phi
        slope = phi + u * (bell * 0.3989422804014327)
        r = mm(cot, dn_ref[:, cols])
        dp = dp + jnp.where(lane == e, jnp.sum(h * r, axis=-1, keepdims=True), 0.0)
        hg_ref[:, cols] = (h * gate).astype(BF)
        dhp_ref[:, cols] = (r * slope * gate).astype(BF)
    dp = jnp.where(on, dp, 0.0)
    dl = (probs * (dp - jnp.sum(probs * dp, axis=-1, keepdims=True))).astype(BF)
    d_ref[...] = (mm(dhp_ref[...], up_ref[...], NT) + mm(dl, router)).astype(BF)
    m = mm(hg_ref[...], dn_ref[...], NT)
    sm_ref[0:8, :] = mm(dl, hn2, TN)
    if own:
        m = m + mm(gates, dbias)
        sm_ref[8:16, :] = mm(gates, cot, TN)
    else:
        sm_ref[8:16, :] = jnp.zeros((8, sm_ref.shape[1]), F4)
    m_ref[...] = m.astype(BF)


def expert_shard(ids, keep, hn2, cot, rows, up, dn, nimg, shard):
    count, width = hn2.shape
    wide = jax.ShapeDtypeStruct((count, up.shape[1]), BF)
    low = jax.ShapeDtypeStruct((count, width), BF)
    return pl.pallas_call(
        partial(expert_kernel, nimg, shard),
        out_shape=[low, low, wide, wide, jax.ShapeDtypeStruct((16, width), F4)],
        in_specs=[SM] + [VM] * 6,
        out_specs=[VM] * 5,
        compiler_params=params(),
        cost_estimate=cost(7),
        name="expert_shard",
    )(ids, keep, hn2, cot, rows, up, dn)


def expert_grad_kernel(nt, gmasks, ids, *refs):
    hn2s, cots, hgs, dhps = (refs[i * nt : (i + 1) * nt] for i in range(4))
    gub_ref = refs[4 * nt]
    grads = refs[4 * nt + 1 : 4 * nt + 1 + len(gmasks)]
    res_ref = refs[4 * nt + 1 + len(gmasks)]
    me = ids[0]
    ones = jnp.ones((8, hn2s[0].shape[0]), BF)
    sums = None
    for s in range(nt):
        part = mm(ones, dhps[s][...])
        sums = part if sums is None else sums + part
    for which in range(2):
        lefts, rights = ((hn2s, dhps), (cots, hgs))[which]
        left = jnp.concatenate([r[...] for r in lefts], axis=0)
        right = jnp.concatenate([r[...] for r in rights], axis=0)
        total = mm(left, right, TN)
        res_ref[...] = total
        for group, ref in zip(gmasks, grads):
            dr = ref.shape[3]
            for idx, mask in enumerate(group):
                at = pl.ds(pl.multiple_of(jnp.bitwise_xor(me, mask) * dr, dr), dr)
                ref[idx, which, 0] = res_ref[at, :].astype(BF)
    gub_ref[...] = sums[0:1, :]


def expert_grads(ids, hn2s, cots, hgs, dhps, gmasks, dr):
    nt = len(hn2s)
    count, width = hn2s[0].shape
    ff = hgs[0].shape[1] // EXPERTS
    fixed = pl.BlockSpec((count, width), lambda e: (0, 0))
    moving = pl.BlockSpec((count, ff), lambda e: (0, e))
    return pl.pallas_call(
        partial(expert_grad_kernel, nt, gmasks),
        grid=(EXPERTS,),
        out_shape=[jax.ShapeDtypeStruct((EXPERTS, 1, ff), F4)]
        + [jax.ShapeDtypeStruct((len(m), 2, EXPERTS, dr, ff), BF) for m in gmasks],
        in_specs=[SM] + [fixed] * (2 * nt) + [moving] * (2 * nt),
        out_specs=[pl.BlockSpec((None, 1, ff), lambda e: (e, 0, 0))]
        + [pl.BlockSpec((len(m), 2, 1, dr, ff), lambda e: (0, 0, e, 0, 0)) for m in gmasks],
        scratch_shapes=[pltpu.VMEM((width, ff), F4)],
        compiler_params=params(16),
        cost_estimate=cost(9),
        name="expert_grads",
    )(ids, *hn2s, *cots, *hgs, *dhps)


def attn_backward_kernel(nimg, nsm, ngub, gmasks, direct, ids, *refs):
    ins = 12 + ngub + nsm
    recv_ref, own_ref, x_ref, cot_ref = refs[:4]
    rows_ref, w_ref = refs[10:12]
    gubs, sms = refs[12 : 12 + ngub], refs[12 + ngub : ins]
    gtok_ref = refs[ins]
    ngrads = len(gmasks)
    grads = refs[ins + 1 : ins + 1 + ngrads]
    small_ref, do_ref, dq_ref, dk_ref, dv_ref, da_ref, hn1_ref, res_ref = refs[
        ins + 1 + ngrads : ins + 9 + ngrads
    ]
    held = refs[ins + 9 + ngrads :]
    x1_ref, q_ref, k_ref, v_ref, o_ref, pb_ref, sems = held
    copies = [
        pltpu.make_async_copy(a, b, sems.at[n]) for n, (a, b) in enumerate(zip(refs[4:10], held))
    ]
    for c in copies:
        c.start()
    width = x_ref.shape[1]
    dh = recv_ref[...].astype(F4) + own_ref[...].astype(F4)
    cot_f = cot_ref[...].astype(F4)
    copies[0].wait()
    n2, inv2 = moments(x1_ref[...], EPS)
    small_ref[...] = jnp.zeros(small_ref.shape, F4)
    small_ref[1:2, :] = jnp.sum(dh * n2, axis=0, keepdims=True)
    small_ref[3:4, :] = jnp.sum(dh, axis=0, keepdims=True)
    dx1 = cot_f + norm_back(dh * rows_ref[1:2, :], n2, inv2)
    da = dx1.astype(BF)
    da_ref[...] = da
    gtok_ref[...] = dx1
    small_ref[4:5, :] = jnp.sum(da.astype(F4), axis=0, keepdims=True)
    do_ref[...] = mm(da, w_ref[3]).astype(BF)
    lane = lax.broadcasted_iota(jnp.int32, (PAD, LANES), 1)
    scale = HD ** (-0.5)
    for c in copies[1:]:
        c.wait()
    for img in range(nimg):
        at = slice(img * PAD, (img + 1) * PAD)
        for pair in range(width // LANES):
            cols = slice(pair * LANES, (pair + 1) * LANES)
            qp, kp, vp, dop = q_ref[at, cols], k_ref[at, cols], v_ref[at, cols], do_ref[at, cols]
            zero = jnp.zeros_like(qp)
            dq = jnp.zeros((PAD, LANES), F4)
            dk = jnp.zeros((PAD, LANES), F4)
            dv = jnp.zeros((PAD, LANES), F4)
            for half in range(2):
                mine = (lane < HD) if half == 0 else (lane >= HD)
                pb = pb_ref[img * (width // HD) + 2 * pair + half]
                dom = jnp.where(mine, dop, zero)
                dpb = mm(dom, vp, NT)
                p = pb.astype(F4)
                ds = (p * (dpb - jnp.sum(p * dpb, axis=-1, keepdims=True))).astype(BF)
                dv = dv + mm(pb, dom, TN)
                dq = dq + mm(ds, jnp.where(mine, kp, zero))
                dk = dk + mm(ds, jnp.where(mine, qp, zero), TN)
            dq_ref[at, cols] = (dq * scale).astype(BF)
            dk_ref[at, cols] = (dk * scale).astype(BF)
            dv_ref[at, cols] = dv.astype(BF)
    small_ref[QVB : QVB + 1, :] = jnp.sum(dq_ref[...].astype(F4), axis=0, keepdims=True)
    small_ref[QVB + 1 : QVB + 2, :] = jnp.sum(dv_ref[...].astype(F4), axis=0, keepdims=True)
    dh1 = (
        mm(dq_ref[...], w_ref[0], NT)
        + mm(dk_ref[...], w_ref[1], NT)
        + mm(dv_ref[...], w_ref[2], NT)
    )
    n1, inv1 = moments(x_ref[...].astype(F4), EPS)
    hn1_ref[...] = (n1 * rows_ref[0:1, :] + rows_ref[2:3, :]).astype(BF)
    small_ref[0:1, :] = jnp.sum(dh1 * n1, axis=0, keepdims=True)
    small_ref[2:3, :] = jnp.sum(dh1, axis=0, keepdims=True)
    gtok_ref[...] = gtok_ref[...] + norm_back(dh1 * rows_ref[0:1, :], n1, inv1)
    total = sms[0][...]
    for ref in sms[1:]:
        total = total + ref[...]
    small_ref[ROUTER : ROUTER + 16, :] = total
    for e in range(EXPERTS):
        ref, at = gubs[e * ngub // EXPERTS], e % (EXPERTS // ngub)
        small_ref[UBIAS + e : UBIAS + e + 1, 0 : ref.shape[2]] = ref[at]
    me, met = ids[0], ids[1]
    for s in range(4):
        left, right = [(hn1_ref, dq_ref), (hn1_ref, dk_ref), (hn1_ref, dv_ref), (da_ref, o_ref)][s]
        res_ref[...] = mm(left[...], right[...], TN)
        for group, ref in zip(gmasks, grads):
            dr = (ref.shape[2] - (SMALL if direct else 0)) // 4
            for idx, mask in enumerate(group):
                i = jnp.bitwise_xor(me, mask)
                for jm in range(ref.shape[1]):
                    j = jnp.bitwise_xor(met, jm)
                    ref[idx, jm, s * dr : (s + 1) * dr, :] = res_ref[
                        pl.ds(pl.multiple_of(i * dr, dr), dr),
                        pl.ds(pl.multiple_of(j * LANES, LANES), LANES),
                    ].astype(BF)
    if not direct:
        return
    lane = lax.broadcasted_iota(jnp.int32, (SMALL, LANES), 1)
    row = lax.broadcasted_iota(jnp.int32, (SMALL, LANES), 0)
    nd = sum(len(g) for g in gmasks)
    qr = LANES // nd
    blank = jnp.zeros((3, LANES), F4)
    for group, ref in zip(gmasks, grads):
        for idx, mask in enumerate(group):
            i = jnp.bitwise_xor(me, mask)
            odd = jnp.bitwise_and(i, 1) == 1
            tile = pl.ds(pl.multiple_of(jnp.right_shift(i, 1) * LANES, LANES), LANES)
            t = jnp.concatenate(
                [small_ref[0:5, tile], small_ref[ROUTER : ROUTER + 4, tile], small_ref[DBIAS : DBIAS + 4, tile], blank],
                axis=0,
            )
            lo = jnp.where(odd, pltpu.roll(t, HALF, 1), t)
            lo = jnp.where(lane < HALF, lo, 0.0)
            b = jnp.concatenate([small_ref[UBIAS : UBIAS + 8, tile], jnp.zeros((8, LANES), F4)], axis=0)
            hi = jnp.where(odd, b, pltpu.roll(b, HALF, 1))
            hi = jnp.where(jnp.logical_and(lane >= HALF, row < EXPERTS), hi, 0.0)
            for jm in range(ref.shape[1]):
                j = jnp.bitwise_xor(met, jm)
                g = small_ref[0:8, pl.ds(pl.multiple_of(j * LANES, LANES), LANES)]
                g = pltpu.roll(g, 7, 0)
                g = pltpu.roll(g, jnp.bitwise_and(HALF - i * qr + LANES, LANES - 1), 1)
                g = jnp.concatenate([g, jnp.zeros((8, LANES), F4)], axis=0)
                mine = jnp.logical_and(lane >= HALF, lane < HALF + qr)
                mine = jnp.logical_and(mine, jnp.logical_and(row >= 4, row < 6))
                block = lo + jnp.where(mine, g, 0.0)
                if jm == 0:
                    block = block + hi
                ref[idx, jm, 4 * dr :, :] = block.astype(BF)


def attn_backward(ids, recv, own, x, cot, saved, rows, full, gubs, sms, gmasks, direct, nt, dr):
    count, width = x.shape
    nimg = count // PAD
    extra = SMALL if direct else 0
    shapes = [jax.ShapeDtypeStruct((count, width), F4)]
    shapes += [jax.ShapeDtypeStruct((len(m), nt, 4 * dr + extra, LANES), BF) for m in gmasks]
    shapes += [jax.ShapeDtypeStruct((NROWS, width), F4)]
    low = pltpu.VMEM((count, width), BF)
    return pl.pallas_call(
        partial(attn_backward_kernel, nimg, len(sms), len(gubs), gmasks, direct),
        out_shape=shapes,
        in_specs=[SM] + [VM] * 4 + [ANY] * 6 + [VM] * (2 + len(gubs) + len(sms)),
        out_specs=[VM] * len(shapes),
        scratch_shapes=[low] * 6
        + [pltpu.VMEM((width, width), F4)]
        + [pltpu.VMEM(v.shape, v.dtype) for v in saved]
        + [pltpu.SemaphoreType.DMA((6,))],
        compiler_params=params(16),
        cost_estimate=cost(16),
        name="attn_backward",
    )(ids, recv, own, x, cot, *in_hbm(saved), rows, full, *gubs, *sms)


def per_device(
    nd,
    nt,
    tokens,
    cotangent,
    routes,
    slots,
    norm_gains,
    norm_biases,
    w_qkv,
    qv_bias,
    w_out,
    out_bias,
    w_router,
    w_up,
    up_bias,
    w_down,
    down_bias,
):
    me = lax.axis_index("dp").astype(jnp.int32)
    met = lax.axis_index("tensor").astype(jnp.int32)
    width = tokens.shape[1]
    dr = w_qkv.shape[1]
    fr, qr = up_bias.shape[1], qv_bias.shape[1]
    ff = w_up.shape[2]
    nimg = IMG_DEV // nt
    direct = nd == 8 and nt == 4 and dr == HALF and fr == HALF and nd * qr == LANES
    src = jnp.asarray(ring_sources(nt), jnp.int32)[met]
    ids = jnp.concatenate([jnp.stack([me if direct else jnp.zeros_like(me), met]), src])
    even, odd = list(range(0, nd, 2)), list(range(1, nd, 2))

    def canonical(parts):
        if direct:
            return parts
        masks = sum((m for m, _ in parts), ())
        arr = jnp.concatenate([a for _, a in parts], axis=0)
        place = [masks.index(k) for k in range(nd)]
        order = jnp.asarray(place, jnp.int32)[jnp.bitwise_xor(jnp.arange(nd), me)]
        arr = jnp.take(arr, order, axis=0)
        lead = arr.ndim - 2
        arr = jnp.moveaxis(arr, 0, lead - 1)
        arr = arr.reshape(arr.shape[: lead - 1] + (nd * dr,) + arr.shape[-1:])
        return [((0,), arr[None])]

    gmasks = [even, odd] if direct else [[0]]

    def halves(grads, lead, rows):
        if direct:
            return grads
        whole = grads[0][0]
        shape = whole.shape[:lead] + (rows, nd, dr) + whole.shape[-1:]
        whole = jnp.moveaxis(whole.reshape(shape), lead + 1, 0)
        whole = whole.reshape((nd,) + grads[0].shape[1 : lead + 1] + (rows * dr, whole.shape[-1]))
        return [
            jnp.take(whole, jnp.bitwise_xor(jnp.asarray(m, jnp.int32), me), axis=0)
            for m in (even, odd)
        ]

    def images(v):
        return jnp.concatenate(
            [jnp.pad(v[i * SEQ : (i + 1) * SEQ], ((0, PAD - SEQ), (0, 0))) for i in range(nimg)]
        )

    chunk = jnp.concatenate([w_qkv, w_out.T[None]], axis=0)
    if direct:
        wide = [
            jnp.concatenate(
                [norm_gains, norm_biases, out_bias[None], w_router.T, down_bias, jnp.zeros((3, dr), BF)],
                axis=0,
            ),
            jnp.concatenate(
                [up_bias, jnp.pad(qv_bias, ((0, 0), (0, dr - qr))), jnp.zeros((10, dr), BF)], axis=0
            ),
        ]
        chunk = jnp.concatenate([chunk.reshape(4 * dr, LANES), jnp.concatenate(wide, axis=1)], axis=0)
    keep = jnp.where(slots >= 0, routes, -1).reshape(nt * nimg, SEQ, 2)
    keep = jnp.pad(keep, ((0, 0), (0, PAD - SEQ), (0, 0)), constant_values=-1)
    x = images(tokens)
    w_dn = w_down.transpose(0, 2, 1)
    cots = [images(cotangent)]
    for s in range(1, nt):
        cots.append(ring_step(cots[-1], nt, False))
    if direct:
        up_near = plane_first(after(w_up, chunk))
        two = jnp.stack([chunk, xor_send(chunk, "tensor", nt, 1)])
        two = (two, xor_send(two, "tensor", nt, 2))
        two, up_near = lax.optimization_barrier((two, up_near, cots[1]))[:2]
        chunk_z = jnp.concatenate(two)
        quad = [chunk_z] + [to(chunk_z, m) for m in (2, 4, 6)]
        quad = jnp.stack(lax.optimization_barrier((quad, cots[2]))[0])
        up_quad = plane_second(*up_near)
        dn_near = plane_first(after(w_dn, quad))
        quad = after(quad, x, keep, ids, up_quad)
        full, rows = assemble(ids, gather_cores(quad), width)
        up_cores = gather_cores(after(up_quad, quad))
    else:
        up, dn = (
            canonical(gather_dp(w[None], nd))[0][1][0, 0].transpose(1, 0, 2).reshape(width, EXPERTS * ff)
            for w in (w_up, w_dn)
        )
        chunk_z = [chunk] + [xor_send(chunk, "tensor", nt, m) for m in range(1, nt)]
        full = canonical(gather_dp(jnp.stack(chunk_z), nd))[0][1][0]
        at = jnp.bitwise_xor(jnp.arange(nt), met)
        full = jnp.take(full, at, axis=0).transpose(1, 2, 0, 3).reshape(4, width, width)

        def whole(v):
            return lax.all_gather(v, "dp", axis=v.ndim - 1, tiled=True).astype(F4)

        qvb = lax.all_gather(whole(qv_bias), "tensor", axis=1, tiled=True)
        four = jnp.zeros((4, width), F4)
        rows = [whole(norm_gains), whole(norm_biases), whole(out_bias[None]), qvb]
        rows += [jnp.zeros((1, width), F4), whole(w_router.T), four, whole(down_bias), four]
        rows += [jnp.pad(whole(up_bias), ((0, 0), (0, width - nd * fr))), four]
        rows = jnp.concatenate(rows, axis=0)

    saved = attn_forward(x, rows, full, nimg)
    hn2s = [saved[0]]
    def shard(s, *first):
        hn2 = after(hn2s[s], *first)
        return expert_shard(ids, keep, hn2, cots[s], rows, up, dn, nimg, s)

    for s in range(1, nt):
        hn2s.append(ring_step(after(hn2s[-1], *(cots[-1:] if s == 1 else [])), nt, False))
    if direct:
        up = gather_experts(ids, [(m, after(a, hn2s[0])) for m, a in up_cores], width)
        dn_quad = plane_second(*(after(a, hn2s[0], cots[3]) for a in dn_near))
        dn = gather_experts(ids, [(m, after(a, hn2s[1])) for m, a in gather_cores(dn_quad)], width)
    shards = [None, shard(1)] + [None] * (nt - 2)
    total = past = shards[1][1]
    for s in range(2, nt):
        if s == nt - 1:
            shards[0] = shard(0, past)
            shards[s] = shard(s, shards[0][1])
        else:
            shards[s] = shard(s, shards[s - 1][1])
        total = ring_step(total, nt, False)
        past = total
        total = sums([[[(total, None), (shards[s][1], None)]]])[0]
        past = total if s < nt - 1 else past
    total = ring_step(total, nt, False)
    recv = total

    gubs, *egrads = expert_grads(
        ids,
        [hn2s[0], after(hn2s[1], past), *hn2s[2:]],
        cots,
        [r[2] for r in shards],
        [r[3] for r in shards],
        gmasks,
        dr if direct else width,
    )
    ms = [r[0] for r in shards]
    if direct:
        kept_x, kept_y, send_x, send_y = scatter_first(egrads[0], to(after(egrads[1], recv), 1))
        got_x, got_y = to(send_x, 2), to(send_y, 4)
        recv = after(recv, send_x)
    m_sum = ring_step(after(ms[1], recv), nt, False)

    res = attn_backward(
        ids,
        recv,
        shards[0][1],
        x,
        cots[0],
        saved[1:],
        rows,
        full,
        [gubs],
        [r[4] for r in shards],
        gmasks,
        direct,
        nt,
        dr if direct else width,
    )
    gtok, flat = res[0], res[-1]
    if direct:
        keeps, gots, m_sum = lax.optimization_barrier(
            ((kept_x, kept_y), (got_x, got_y), m_sum, gtok)
        )[:3]
        next_x, next_y, base_x, base_y = scatter_second(*keeps, *gots)
        far_x, far_y = to(next_x, 4), to(next_y, 2)
        m_sum = ring_step(sums([[[(m_sum, None), (ms[2], None)]]])[0], nt, False)
        a_odd = after(res[2], next_x)
        keeps = scatter_first(res[1], to(a_odd, 1))
        a_keep, a_send = keeps[:2], keeps[2:]
        a_send, far = lax.optimization_barrier((a_send, (far_x, far_y)))
        g_up, g_down = add_all([base_x, far[0]])[0], add_all([base_y, far[1]])[0]
        a_got = [to(a_send[0], 2), to(a_send[1], 4)]
        m_sum = sums([[[(after(m_sum, *far), None), (ms[3], None)]]])[0]
        a_got = lax.optimization_barrier((a_got, m_sum))[0]
        m_sum = ring_step(m_sum, nt, False)
        a_next_x, a_next_y, a_base_x, a_base_y = scatter_second(*a_keep, *a_got)
        a_far = [to(a_next_x, 4), to(a_next_y, 2)]
        held = sums(
            [[[(b, j), (f, j)]] for b, f in ((a_base_x, a_far[0]), (a_base_y, a_far[1])) for j in (0, 1)]
        )
        parts = [held[0]] + [xor_send(held[m], "tensor", nt, m) for m in range(1, nt)]
        g_qkv, g_out, g_gain, g_bias, g_outb, g_router, g_dbias, g_ub, g_qvb = finish(parts, dr, qr)
        g_outb, g_router = g_outb[0], g_router.T
    else:
        egrads = halves(egrads, 2, 1)
        g_up, g_down = add_all(scatter_dp(*egrads, nd))
        held = add_all(scatter_dp(*halves(res[1:-1], 1, 4), nd)).astype(BF)
        mine = add_all([held[0]] + [xor_send(held[m], "tensor", nt, m) for m in range(1, nt)])
        g_qkv, g_out = mine[: 3 * dr].reshape(3, dr, LANES), mine[3 * dr :]
        for s in range(2, nt):
            m_sum = ring_step(add_all([m_sum, ms[s]]).astype(BF), nt, False)
        g_ub = lax.dynamic_slice(lax.psum(flat, "dp"), (UBIAS, me * fr), (EXPERTS, fr))
        flat = lax.psum(flat, ("dp", "tensor"))
        cut = lax.dynamic_slice(flat, (0, me * dr), (NROWS, dr))
        g_gain, g_bias, g_outb = cut[0:2], cut[2:4], cut[4]
        g_router, g_dbias = cut[ROUTER : ROUTER + 4].T, cut[DBIAS : DBIAS + 4]
        g_qvb = lax.dynamic_slice(flat, (QVB, (met * nd + me) * qr), (2, qr))

    def rows_of(v):
        return jnp.concatenate([v[i * PAD : i * PAD + SEQ] for i in range(nimg)])

    layer_out = rows_of(saved[1] + (m_sum.astype(F4) + ms[0].astype(F4)))
    grad_tokens = rows_of(gtok)

    return (
        layer_out,
        grad_tokens,
        g_gain,
        g_bias,
        g_qkv,
        g_qvb,
        g_out.T,
        g_outb,
        g_router,
        g_up,
        g_ub,
        g_down.transpose(0, 2, 1),
        g_dbias,
    )


def solution(mesh):
    nd, nt = mesh.shape["dp"], mesh.shape["tensor"]
    placed = (
        P(("dp", "tensor"), None),
        P(("dp", "tensor"), None),
        P("dp", None),
        P("dp", None),
        P(None, "dp"),
        P(None, "dp"),
        P(None, "dp", "tensor"),
        P(None, ("tensor", "dp")),
        P("tensor", "dp"),
        P("dp"),
        P("dp", None),
        P(None, "dp", "tensor"),
        P(None, ("tensor", "dp")),
        P(None, "tensor", "dp"),
        P(None, "dp"),
    )
    return jax.shard_map(
        partial(per_device, nd, nt),
        mesh=mesh,
        in_specs=placed,
        out_specs=(
            P(("dp", "tensor"), None),
            P(("dp", "tensor"), None),
            P(None, "dp"),
            P(None, "dp"),
            P(None, "dp", "tensor"),
            P(None, ("tensor", "dp")),
            P("tensor", "dp"),
            P("dp"),
            P("dp", None),
            P(None, "dp", "tensor"),
            P(None, ("tensor", "dp")),
            P(None, "tensor", "dp"),
            P(None, "dp"),
        ),
        check_vma=False,
    )
```

```python
from functools import partial

import jax
import jax.numpy as jnp
import numpy as np
from jax import lax
from jax.experimental import pallas as pl
from jax.experimental.pallas import tpu as pltpu
from jax.sharding import PartitionSpec as P

HD = 64
EXPERTS = 4
SEQ = 197
IMG_DEV = 8
PAD = 200
SMALL = 16
EPS = 1e-06
BF = jnp.bfloat16
F4 = jnp.float32
NEG = -1e30
LANES = 128
HALF = 64

NN = (((1,), (0,)), ((), ()))
NT = (((1,), (1,)), ((), ()))
TN = (((0,), (0,)), ((), ()))

VM = pl.BlockSpec()
SM = pl.BlockSpec(memory_space=pltpu.SMEM)
ANY = pl.BlockSpec(memory_space=pltpu.HBM)


def mm(a, b, dims=NN):
    return lax.dot_general(a, b, dims, preferred_element_type=F4)


def params(mib=12):
    return pltpu.CompilerParams(vmem_limit_bytes=mib * 1024 * 1024)


def cost(us):
    return pl.CostEstimate(flops=0, transcendentals=0, bytes_accessed=int(us * 3.3e4))


def xor_send(x, axis, n, mask):
    return lax.ppermute(x, axis, [(i, i ^ mask) for i in range(n)])


def ring_order(n):
    return [0] + list(range(1, n, 2)) + list(range(2, n, 2))[::-1]


def ring_step(x, n, back):
    ring = ring_order(n)
    pairs = [(ring[p], ring[(p + (-1 if back else 1)) % n]) for p in range(n)]
    return lax.ppermute(x, "tensor", pairs)


def ring_sources(n):
    ring = ring_order(n)
    pos = {r: p for p, r in enumerate(ring)}
    return [[ring[(pos[r] - s) % n] for s in range(n)] for r in range(n)]


def stages_of(n):
    if n <= 8:
        inter = list(range(2, n, 2))
        return ([[1]] if n > 1 else []) + ([inter] if inter else [])
    out, bit = [], 1
    while bit < n:
        out.append([bit])
        bit *= 2
    return out


def gather_dp(x, n):
    parts = [((0,), x[None])]
    for stage in reversed(stages_of(n)):
        new = []
        for mask in stage:
            for masks, arr in parts:
                new.append((tuple(k ^ mask for k in masks), xor_send(arr, "dp", n, mask)))
        parts = parts + new
        if n > 8 and stage != [1]:
            parts = [
                (sum((m for m, _ in parts), ()), jnp.concatenate([a for _, a in parts], axis=0))
            ]
    return parts


def scatter_dp(even, odd, n):
    got = xor_send(odd, "dp", n, 1)
    masks = list(range(0, n, 2))
    own = {k: even[i] for i, k in enumerate(masks)}
    new = {k: got[i] for i, k in enumerate(masks)}
    own = {k: (own[k].astype(F4) + new[k].astype(F4)).astype(BF) for k in masks}
    stages = stages_of(n)[1:]
    for at, stage in enumerate(stages):
        span = 0
        for m in stage:
            span |= m
        rest = [k for k in masks if not k & span]
        recv = []
        for m in stage:
            pack = [own[k ^ m] for k in rest]
            send = pack[0] if len(pack) == 1 else jnp.stack(pack)
            back = xor_send(send, "dp", n, m)
            recv.append([back] if len(pack) == 1 else [back[i] for i in range(len(pack))])
        masks = rest
        if at == len(stages) - 1:
            return [own[0]] + [r[0] for r in recv]
        own = {
            k: sum((r[i].astype(F4) for r in recv), own[k].astype(F4)).astype(BF)
            for i, k in enumerate(rest)
        }
    return [own[0]]


CORE0, CORE1 = (0, 2, 4, 6), (1, 3, 5, 7)


def to(x, mask):
    return xor_send(x, "dp", 8, mask)


def plane_first(x):
    return x, to(x, 2), to(x, 4)


def plane_far(x, from_x, from_y):
    half = x.shape[0] // 2
    return to(from_x[:half], 4), to(from_y[half:], 2)


def plane_stack(x, from_x, from_y, far):
    return jnp.stack([x, from_x, from_y, jnp.concatenate(far, axis=0)])


def gather_cores(quad):
    return [(CORE0, quad), (CORE1, to(quad, 1))]


def scatter_first(even, got):
    half = even.shape[1] // 2
    low, high = slice(0, half), slice(half, 2 * half)

    def both(mask, part):
        return [(even, (mask // 2, part)), (got, (mask // 2, part))]

    return sums(
        [
            [both(0, low), both(4, low)],
            [both(0, high), both(2, high)],
            [both(2, low), both(6, low)],
            [both(4, high), both(6, high)],
        ]
    )


def scatter_second(keep_x, keep_y, got_x, got_y):
    pairs = [(keep_x, got_x), (keep_y, got_y)]
    return sums([[[(k, at), (g, at)]] for at in (1, 0) for k, g in pairs])


def after(x, *first):
    return lax.optimization_barrier((x, *first))[0]


def arrays(parts):
    return [a for _, a in parts]


def sums_kernel(outs, count, *refs):
    for groups, out in zip(outs, refs[count:]):
        for j, group in enumerate(groups):
            total = None
            for n, at in group:
                term = (refs[n][...] if at is None else refs[n][at]).astype(F4)
                total = term if total is None else total + term
            if len(groups) == 1:
                out[...] = total.astype(out.dtype)
            else:
                out[j] = total.astype(out.dtype)


def sums(outs):
    known, flat, index, shapes = {}, [], [], []
    for groups in outs:
        index.append([])
        for group in groups:
            index[-1].append([])
            for v, at in group:
                if id(v) not in known:
                    known[id(v)] = len(flat)
                    flat.append(v)
                index[-1][-1].append((known[id(v)], at))
        v, at = groups[0][0]
        shape = v.shape if at is None else np.broadcast_to(0, v.shape)[at].shape
        shapes.append(shape if len(groups) == 1 else (len(groups),) + shape)
    return pl.pallas_call(
        partial(sums_kernel, index, len(flat)),
        out_shape=[jax.ShapeDtypeStruct(v, BF) for v in shapes],
        in_specs=[VM] * len(flat),
        out_specs=[VM] * len(shapes),
        compiler_params=params(16),
        cost_estimate=cost(1),
        name="sums",
    )(*flat)


def finish_kernel(dr, qr, *refs):
    parts, outs = refs[:4], refs[4:]
    g_qkv, g_out, g_gain, g_bias, g_outb, g_router, g_dbias, g_ub, g_qvb = outs
    total = parts[0][...].astype(F4)
    for ref in parts[1:]:
        total = total + ref[...].astype(F4)
    for s in range(3):
        g_qkv[s] = total[s * dr : (s + 1) * dr]
    g_out[...] = total[3 * dr : 4 * dr]
    low = total[4 * dr :]
    high = pltpu.roll(low, HALF, 1)
    g_gain[...] = low[0:2, :HALF]
    g_bias[...] = low[2:4, :HALF]
    g_outb[...] = low[4:5, :HALF]
    g_router[...] = low[5:9, :HALF]
    g_dbias[...] = low[9:13, :HALF]
    g_ub[...] = high[0:4, :HALF]
    g_qvb[...] = high[4:6, :qr]


def finish(parts, dr, qr):
    rows = [(2, HALF), (2, HALF), (1, HALF), (EXPERTS, HALF), (EXPERTS, HALF), (EXPERTS, HALF), (2, qr)]
    shapes = [(3, dr, LANES), (dr, LANES)] + rows
    return pl.pallas_call(
        partial(finish_kernel, dr, qr),
        out_shape=[jax.ShapeDtypeStruct(v, F4) for v in shapes],
        in_specs=[VM] * 4,
        out_specs=[VM] * len(shapes),
        compiler_params=params(),
        cost_estimate=cost(1),
        name="finish",
    )(*parts)


def add_all(parts):
    return sum((p.astype(F4) for p in parts[1:]), parts[0].astype(F4))


def moments(v, eps_rows):
    center = v - jnp.mean(v, axis=-1, keepdims=True)
    inv = lax.rsqrt(jnp.mean(center * center, axis=-1, keepdims=True) + eps_rows)
    return center * inv, inv


def norm_back(z, normed, inv):
    return inv * (
        z
        - jnp.mean(z, axis=-1, keepdims=True)
        - normed * jnp.mean(z * normed, axis=-1, keepdims=True)
    )


def exact(ref, lo, hi):
    return ref[lo:hi, :].astype(BF)


GAIN, BIAS, OUTB, QVB, ROUTER, DBIAS, UBIAS, NROWS = 0, 2, 4, 5, 8, 16, 24, 32


def in_hbm(values):
    return [pltpu.with_memory_space_constraint(v, pltpu.HBM) for v in values]


def run_copies(pairs, sems):
    copies = [pltpu.make_async_copy(a, b, sems.at[n]) for n, (a, b) in enumerate(pairs)]
    for c in copies:
        c.start()
    for c in copies:
        c.wait()


def assemble_kernel(masks, ids, *refs):
    pieces, (w_ref, rows_ref, small_ref, sems) = refs[:-4], refs[-4:]
    me, met = ids[0], ids[1]
    pairs = []
    for group, ref in zip(masks, pieces):
        dr = (ref.shape[2] - SMALL) // 4
        for idx, mask in enumerate(group):
            i = jnp.bitwise_xor(me, mask)
            for jm in range(ref.shape[1]):
                j = jnp.bitwise_xor(met, jm)
                rows_at = pl.ds(pl.multiple_of(i * dr, dr), dr)
                lanes_at = pl.ds(pl.multiple_of(j * LANES, LANES), LANES)
                for s in range(4):
                    pairs.append(
                        (ref.at[idx, jm, s * dr : (s + 1) * dr], w_ref.at[s, rows_at, lanes_at])
                    )
                pairs.append((ref.at[idx, jm, 4 * dr : 4 * dr + SMALL], small_ref.at[mask, jm]))
    run_copies(pairs, sems)
    rows_ref[...] = jnp.zeros(rows_ref.shape, F4)
    lane = lax.broadcasted_iota(jnp.int32, (SMALL, LANES), 1)
    low = lane < HALF
    odd = jnp.bitwise_and(me, 1) == 1
    nd, nt = small_ref.shape[:2]

    def small(mask, jm):
        return small_ref[mask, jm].astype(F4)

    for mask in range(0, nd, 2):
        a, b = small(mask, 0), small(mask + 1, 0)
        first, second = jnp.where(odd, b, a), jnp.where(odd, a, b)
        lo = jnp.where(low, first, pltpu.roll(second, HALF, 1))
        hi = jnp.where(low, pltpu.roll(first, HALF, 1), second)
        tile = jnp.right_shift(jnp.bitwise_xor(me, mask), 1)
        at = pl.ds(pl.multiple_of(tile * LANES, LANES), LANES)
        rows_ref[0:5, at] = lo[0:5]
        rows_ref[ROUTER : ROUTER + EXPERTS, at] = lo[5:9]
        rows_ref[DBIAS : DBIAS + EXPERTS, at] = lo[9:13]
        rows_ref[UBIAS : UBIAS + EXPERTS, at] = hi[0:4]
    qr = LANES // nd
    mine = jnp.logical_and(lane >= HALF, lane < HALF + qr)
    for jm in range(nt):
        j = jnp.bitwise_xor(met, jm)
        total = jnp.zeros((SMALL, LANES), F4)
        for mask in range(nd):
            i = jnp.bitwise_xor(me, mask)
            part = jnp.where(mine, small(mask, jm), 0.0)
            total = total + pltpu.roll(part, jnp.bitwise_and(HALF + i * qr, LANES - 1), 1)
        rows_ref[QVB : QVB + 2, pl.ds(pl.multiple_of(j * LANES, LANES), LANES)] = total[4:6]


def assemble(ids, weights, width):
    masks = [m for m, _ in weights]
    pieces = arrays(weights)
    nd, nt = sum(len(m) for m in masks), pieces[0].shape[1]
    return pl.pallas_call(
        partial(assemble_kernel, masks),
        out_shape=[
            jax.ShapeDtypeStruct((4, width, width), BF),
            jax.ShapeDtypeStruct((NROWS, width), F4),
        ],
        in_specs=[SM] + [ANY] * len(pieces),
        out_specs=[VM, VM],
        scratch_shapes=[
            pltpu.VMEM((nd, nt, SMALL, LANES), BF),
            pltpu.SemaphoreType.DMA((5 * nd * nt,)),
        ],
        compiler_params=params(8),
        cost_estimate=cost(2),
        name="assemble",
    )(ids, *pieces)


def attn_forward_kernel(
    nimg, x_ref, rows_ref, w_ref, hn2_ref, x1_out, q_out, k_out, v_out, o_out, pb_out, *scratch
):
    x1_ref, q_ref, k_ref, v_ref, o_ref, pb_ref, sems = scratch
    heads = w_ref.shape[1] // HD
    copies = []

    def leave(src, dst):
        copies.append(pltpu.make_async_copy(src, dst, sems.at[len(copies)]))
        copies[-1].start()

    width = x_ref.shape[1]
    x = x_ref[...].astype(F4)
    n1, _ = moments(x, EPS)
    hn1 = (n1 * rows_ref[0:1, :] + rows_ref[2:3, :]).astype(BF)
    q_ref[...] = (mm(hn1, w_ref[0]) + rows_ref[5:6, :]).astype(BF)
    k_ref[...] = mm(hn1, w_ref[1]).astype(BF)
    v_ref[...] = (mm(hn1, w_ref[2]) + rows_ref[6:7, :]).astype(BF)
    leave(q_ref, q_out)
    leave(k_ref, k_out)
    leave(v_ref, v_out)
    lane = lax.broadcasted_iota(jnp.int32, (PAD, LANES), 1)
    col = lax.broadcasted_iota(jnp.int32, (PAD, PAD), 1)
    for img in range(nimg):
        at = slice(img * PAD, (img + 1) * PAD)
        for pair in range(width // LANES):
            cols = slice(pair * LANES, (pair + 1) * LANES)
            qp, kp, vp = q_ref[at, cols], k_ref[at, cols], v_ref[at, cols]
            acc = jnp.zeros((PAD, LANES), F4)
            for half in range(2):
                mine = (lane < HD) if half == 0 else (lane >= HD)
                qm = jnp.where(mine, qp * jnp.asarray(HD ** (-0.5), BF), jnp.zeros_like(qp))
                s = mm(qm, kp, NT)
                s = jnp.where(col < SEQ, s, NEG)
                e = jnp.exp(s - jnp.max(s, axis=-1, keepdims=True))
                p = (e * (1.0 / jnp.sum(e, axis=-1, keepdims=True))).astype(BF)
                pb_ref[img * heads + 2 * pair + half] = p
                acc = acc + mm(p, jnp.where(mine, vp, jnp.zeros_like(vp)))
            o_ref[at, cols] = acc.astype(BF)
        mine = pl.ds(img * heads, heads)
        leave(pb_ref.at[mine], pb_out.at[mine])
    leave(o_ref, o_out)
    x1 = x + (mm(o_ref[...], w_ref[3], NT) + rows_ref[4:5, :])
    x1_ref[...] = x1
    leave(x1_ref, x1_out)
    n2, _ = moments(x1, EPS)
    hn2_ref[...] = (n2 * rows_ref[1:2, :] + rows_ref[3:4, :]).astype(BF)
    for c in copies:
        c.wait()


def attn_forward(x, rows, full, nimg):
    count, width = x.shape
    heads = width // HD
    saved = [((count, width), F4)] + [((count, width), BF)] * 4
    saved.append(((nimg * heads, PAD, PAD), BF))
    shapes = [jax.ShapeDtypeStruct((count, width), BF)] + [pltpu.HBM(*v) for v in saved]
    return pl.pallas_call(
        partial(attn_forward_kernel, nimg),
        out_shape=shapes,
        in_specs=[VM] * 3,
        out_specs=[VM] + [ANY] * len(saved),
        scratch_shapes=[pltpu.VMEM(*v) for v in saved] + [pltpu.SemaphoreType.DMA((5 + nimg,))],
        compiler_params=params(),
        cost_estimate=cost(9),
        name="attn_forward",
    )(x, rows, full)


def gather_experts_kernel(masks, ids, *refs):
    pieces, (w_ref, sems) = refs[:-2], refs[-2:]
    me = ids[0]
    pairs = []
    for group, ref in zip(masks, pieces):
        dr, ff = ref.shape[2], ref.shape[3]
        for idx, mask in enumerate(group):
            at = pl.ds(pl.multiple_of(jnp.bitwise_xor(me, mask) * dr, dr), dr)
            for e in range(EXPERTS):
                pairs.append((ref.at[idx, e], w_ref.at[at, e * ff : (e + 1) * ff]))
    run_copies(pairs, sems)


def gather_experts(ids, weights, width):
    masks = [m for m, _ in weights]
    pieces = arrays(weights)
    nd = sum(len(m) for m in masks)
    return pl.pallas_call(
        partial(gather_experts_kernel, masks),
        out_shape=jax.ShapeDtypeStruct((width, EXPERTS * pieces[0].shape[3]), BF),
        in_specs=[SM] + [ANY] * len(pieces),
        out_specs=VM,
        scratch_shapes=[pltpu.SemaphoreType.DMA((EXPERTS * nd,))],
        compiler_params=params(8),
        cost_estimate=cost(3),
        name="gather_experts",
    )(ids, *pieces)


def normal_parts(u):
    bell = jnp.exp(-0.5 * (u * u))
    t = 1.0 / (1.0 + (0.3275911 * 2.0 ** (-0.5)) * jnp.abs(u))
    poly = 0.5 * 1.061405429 * t + 0.5 * (-1.453152027)
    poly = poly * t + 0.5 * 1.421413741
    poly = poly * t + 0.5 * (-0.284496736)
    poly = poly * t + 0.5 * 0.254829592
    tail = poly * t * bell
    return jnp.where(u > 0.0, 1.0 - tail, tail), bell


def expert_kernel(
    nimg, shard, ids, keep_ref, hn2_ref, cot_ref, rows_ref, up_ref, dn_ref, m_ref, d_ref, hg_ref, dhp_ref, sm_ref
):
    own = shard == 0
    count = hn2_ref.shape[0]
    ff = hg_ref.shape[1] // EXPERTS
    hn2, cot = hn2_ref[...], cot_ref[...]
    router = exact(rows_ref, ROUTER, ROUTER + 8)
    lane = lax.broadcasted_iota(jnp.int32, (count, 8), 1)
    logits = jnp.where(lane < EXPERTS, mm(hn2, router, NT), NEG)
    e = jnp.exp(logits - jnp.max(logits, axis=-1, keepdims=True))
    probs = e / jnp.sum(e, axis=-1, keepdims=True)
    tile = ids[2 + shard] * nimg
    keep = jnp.concatenate([keep_ref[tile + i] for i in range(nimg)], axis=0)
    on = jnp.logical_or(lane == keep[:, 0:1], lane == keep[:, 1:2])
    gates = jnp.where(on, probs, 0.0).astype(BF)
    gates_f = gates.astype(F4)
    dp = jnp.zeros((count, 8), F4)
    if own:
        dbias = exact(rows_ref, DBIAS, DBIAS + 8)
        dp = mm(cot, dbias, NT)

    def pair(i, dp):
        for e in (2 * i, 2 * i + 1):
            cols = pl.ds(pl.multiple_of(e * ff, ff), ff)
            mine = lane == e
            gate = jnp.sum(jnp.where(mine, gates_f, 0.0), axis=-1, keepdims=True)
            u = mm(hn2, up_ref[:, cols]) + rows_ref[pl.ds(UBIAS + e, 1), 0:ff]
            phi, bell = normal_parts(u)
            h = u * phi
            slope = phi + u * (bell * 0.3989422804014327)
            r = mm(cot, dn_ref[:, cols])
            dp = dp + jnp.where(mine, jnp.sum(h * r, axis=-1, keepdims=True), 0.0)
            hg_ref[:, cols] = (h * gate).astype(BF)
            dhp_ref[:, cols] = (r * slope * gate).astype(BF)
        return dp

    dp = lax.fori_loop(0, EXPERTS // 2, pair, dp)
    dp = jnp.where(on, dp, 0.0)
    dl = (probs * (dp - jnp.sum(probs * dp, axis=-1, keepdims=True))).astype(BF)
    d_ref[...] = (mm(dhp_ref[...], up_ref[...], NT) + mm(dl, router)).astype(BF)
    m = mm(hg_ref[...], dn_ref[...], NT)
    sm_ref[0:8, :] = mm(dl, hn2, TN)
    if own:
        m = m + mm(gates, dbias)
        sm_ref[8:16, :] = mm(gates, cot, TN)
    else:
        sm_ref[8:16, :] = jnp.zeros((8, sm_ref.shape[1]), F4)
    m_ref[...] = m.astype(BF)


def expert_shard(ids, keep, hn2, cot, rows, up, dn, nimg, shard):
    count, width = hn2.shape
    wide = jax.ShapeDtypeStruct((count, up.shape[1]), BF)
    low = jax.ShapeDtypeStruct((count, width), BF)
    return pl.pallas_call(
        partial(expert_kernel, nimg, shard),
        out_shape=[low, low, wide, wide, jax.ShapeDtypeStruct((16, width), F4)],
        in_specs=[SM] + [VM] * 6,
        out_specs=[VM] * 5,
        compiler_params=params(),
        cost_estimate=cost(7),
        name="expert_shard",
    )(ids, keep, hn2, cot, rows, up, dn)


def expert_grad_kernel(nt, gmasks, ids, *refs):
    hn2s, cots, hgs, dhps = (refs[i * nt : (i + 1) * nt] for i in range(4))
    gub_ref = refs[4 * nt]
    grads = refs[4 * nt + 1 : 4 * nt + 1 + len(gmasks)]
    res_ref = refs[4 * nt + 1 + len(gmasks)]
    me = ids[0]
    ones = jnp.ones((8, hn2s[0].shape[0]), BF)
    sums = None
    for s in range(nt):
        part = mm(ones, dhps[s][...])
        sums = part if sums is None else sums + part
    for which in range(2):
        lefts, rights = ((hn2s, dhps), (cots, hgs))[which]
        left = jnp.concatenate([r[...] for r in lefts], axis=0)
        right = jnp.concatenate([r[...] for r in rights], axis=0)
        total = mm(left, right, TN)
        res_ref[...] = total
        for group, ref in zip(gmasks, grads):
            dr = ref.shape[3]
            for idx, mask in enumerate(group):
                at = pl.ds(pl.multiple_of(jnp.bitwise_xor(me, mask) * dr, dr), dr)
                ref[idx, which, 0] = res_ref[at, :].astype(BF)
    gub_ref[...] = sums[0:1, :]


def expert_grads(ids, hn2s, cots, hgs, dhps, gmasks, dr):
    nt = len(hn2s)
    count, width = hn2s[0].shape
    ff = hgs[0].shape[1] // EXPERTS
    fixed = pl.BlockSpec((count, width), lambda e: (0, 0))
    moving = pl.BlockSpec((count, ff), lambda e: (0, e))
    return pl.pallas_call(
        partial(expert_grad_kernel, nt, gmasks),
        grid=(EXPERTS,),
        out_shape=[jax.ShapeDtypeStruct((EXPERTS, 1, ff), F4)]
        + [jax.ShapeDtypeStruct((len(m), 2, EXPERTS, dr, ff), BF) for m in gmasks],
        in_specs=[SM] + [fixed] * (2 * nt) + [moving] * (2 * nt),
        out_specs=[pl.BlockSpec((None, 1, ff), lambda e: (e, 0, 0))]
        + [pl.BlockSpec((len(m), 2, 1, dr, ff), lambda e: (0, 0, e, 0, 0)) for m in gmasks],
        scratch_shapes=[pltpu.VMEM((width, ff), F4)],
        compiler_params=params(16),
        cost_estimate=cost(9),
        name="expert_grads",
    )(ids, *hn2s, *cots, *hgs, *dhps)


def attn_backward_kernel(nimg, nsm, ngub, gmasks, direct, ids, *refs):
    ins = 12 + ngub + nsm
    recv_ref, own_ref, x_ref, cot_ref = refs[:4]
    rows_ref, w_ref = refs[10:12]
    gubs, sms = refs[12 : 12 + ngub], refs[12 + ngub : ins]
    gtok_ref = refs[ins]
    ngrads = len(gmasks)
    grads = refs[ins + 1 : ins + 1 + ngrads]
    small_ref, do_ref, dq_ref, dk_ref, dv_ref, da_ref, hn1_ref, res_ref = refs[
        ins + 1 + ngrads : ins + 9 + ngrads
    ]
    held = refs[ins + 9 + ngrads :]
    x1_ref, q_ref, k_ref, v_ref, o_ref, pb_ref, sems = held
    copies = [
        pltpu.make_async_copy(a, b, sems.at[n]) for n, (a, b) in enumerate(zip(refs[4:10], held))
    ]
    for c in copies:
        c.start()
    width = x_ref.shape[1]
    dh = recv_ref[...].astype(F4) + own_ref[...].astype(F4)
    cot_f = cot_ref[...].astype(F4)
    copies[0].wait()
    n2, inv2 = moments(x1_ref[...], EPS)
    small_ref[...] = jnp.zeros(small_ref.shape, F4)
    small_ref[1:2, :] = jnp.sum(dh * n2, axis=0, keepdims=True)
    small_ref[3:4, :] = jnp.sum(dh, axis=0, keepdims=True)
    dx1 = cot_f + norm_back(dh * rows_ref[1:2, :], n2, inv2)
    da = dx1.astype(BF)
    da_ref[...] = da
    gtok_ref[...] = dx1
    small_ref[4:5, :] = jnp.sum(da.astype(F4), axis=0, keepdims=True)
    do_ref[...] = mm(da, w_ref[3]).astype(BF)
    lane = lax.broadcasted_iota(jnp.int32, (PAD, LANES), 1)
    scale = HD ** (-0.5)
    for c in copies[1:]:
        c.wait()

    def pair(n, carry):
        cols = pl.ds(pl.multiple_of(n * LANES, LANES), LANES)
        for img in range(nimg):
            at = slice(img * PAD, (img + 1) * PAD)
            qp, kp, vp, dop = q_ref[at, cols], k_ref[at, cols], v_ref[at, cols], do_ref[at, cols]
            zero = jnp.zeros_like(qp)
            dq = jnp.zeros((PAD, LANES), F4)
            dk = jnp.zeros((PAD, LANES), F4)
            dv = jnp.zeros((PAD, LANES), F4)
            for half in range(2):
                mine = (lane < HD) if half == 0 else (lane >= HD)
                pb = pb_ref[img * (width // HD) + 2 * n + half]
                dom = jnp.where(mine, dop, zero)
                dpb = mm(dom, vp, NT)
                p = pb.astype(F4)
                ds = (p * (dpb - jnp.sum(p * dpb, axis=-1, keepdims=True))).astype(BF)
                dv = dv + mm(pb, dom, TN)
                dq = dq + mm(ds, jnp.where(mine, kp, zero))
                dk = dk + mm(ds, jnp.where(mine, qp, zero), TN)
            dq_ref[at, cols] = (dq * scale).astype(BF)
            dk_ref[at, cols] = (dk * scale).astype(BF)
            dv_ref[at, cols] = dv.astype(BF)
        return carry

    lax.fori_loop(0, width // LANES, pair, 0)
    small_ref[QVB : QVB + 1, :] = jnp.sum(dq_ref[...].astype(F4), axis=0, keepdims=True)
    small_ref[QVB + 1 : QVB + 2, :] = jnp.sum(dv_ref[...].astype(F4), axis=0, keepdims=True)
    dh1 = (
        mm(dq_ref[...], w_ref[0], NT)
        + mm(dk_ref[...], w_ref[1], NT)
        + mm(dv_ref[...], w_ref[2], NT)
    )
    n1, inv1 = moments(x_ref[...].astype(F4), EPS)
    hn1_ref[...] = (n1 * rows_ref[0:1, :] + rows_ref[2:3, :]).astype(BF)
    small_ref[0:1, :] = jnp.sum(dh1 * n1, axis=0, keepdims=True)
    small_ref[2:3, :] = jnp.sum(dh1, axis=0, keepdims=True)
    gtok_ref[...] = gtok_ref[...] + norm_back(dh1 * rows_ref[0:1, :], n1, inv1)
    total = sms[0][...]
    for ref in sms[1:]:
        total = total + ref[...]
    small_ref[ROUTER : ROUTER + 16, :] = total
    for e in range(EXPERTS):
        ref, at = gubs[e * ngub // EXPERTS], e % (EXPERTS // ngub)
        small_ref[UBIAS + e : UBIAS + e + 1, 0 : ref.shape[2]] = ref[at]
    me, met = ids[0], ids[1]
    for s in range(4):
        left, right = [(hn1_ref, dq_ref), (hn1_ref, dk_ref), (hn1_ref, dv_ref), (da_ref, o_ref)][s]
        res_ref[...] = mm(left[...], right[...], TN)
        for group, ref in zip(gmasks, grads):
            dr = (ref.shape[2] - (SMALL if direct else 0)) // 4
            for idx, mask in enumerate(group):
                i = jnp.bitwise_xor(me, mask)
                for jm in range(ref.shape[1]):
                    j = jnp.bitwise_xor(met, jm)
                    ref[idx, jm, s * dr : (s + 1) * dr, :] = res_ref[
                        pl.ds(pl.multiple_of(i * dr, dr), dr),
                        pl.ds(pl.multiple_of(j * LANES, LANES), LANES),
                    ].astype(BF)
    if not direct:
        return
    lane = lax.broadcasted_iota(jnp.int32, (SMALL, LANES), 1)
    row = lax.broadcasted_iota(jnp.int32, (SMALL, LANES), 0)
    nd = sum(len(g) for g in gmasks)
    qr = LANES // nd
    blank = jnp.zeros((3, LANES), F4)
    for group, ref in zip(gmasks, grads):
        for idx, mask in enumerate(group):
            i = jnp.bitwise_xor(me, mask)
            odd = jnp.bitwise_and(i, 1) == 1
            tile = pl.ds(pl.multiple_of(jnp.right_shift(i, 1) * LANES, LANES), LANES)
            t = jnp.concatenate(
                [small_ref[0:5, tile], small_ref[ROUTER : ROUTER + 4, tile], small_ref[DBIAS : DBIAS + 4, tile], blank],
                axis=0,
            )
            lo = jnp.where(odd, pltpu.roll(t, HALF, 1), t)
            lo = jnp.where(lane < HALF, lo, 0.0)
            b = jnp.concatenate([small_ref[UBIAS : UBIAS + 8, tile], jnp.zeros((8, LANES), F4)], axis=0)
            hi = jnp.where(odd, b, pltpu.roll(b, HALF, 1))
            hi = jnp.where(jnp.logical_and(lane >= HALF, row < EXPERTS), hi, 0.0)
            for jm in range(ref.shape[1]):
                j = jnp.bitwise_xor(met, jm)
                g = small_ref[0:8, pl.ds(pl.multiple_of(j * LANES, LANES), LANES)]
                g = pltpu.roll(g, 7, 0)
                g = pltpu.roll(g, jnp.bitwise_and(HALF - i * qr + LANES, LANES - 1), 1)
                g = jnp.concatenate([g, jnp.zeros((8, LANES), F4)], axis=0)
                mine = jnp.logical_and(lane >= HALF, lane < HALF + qr)
                mine = jnp.logical_and(mine, jnp.logical_and(row >= 4, row < 6))
                block = lo + jnp.where(mine, g, 0.0)
                if jm == 0:
                    block = block + hi
                ref[idx, jm, 4 * dr :, :] = block.astype(BF)


def attn_backward(ids, recv, own, x, cot, saved, rows, full, gubs, sms, gmasks, direct, nt, dr):
    count, width = x.shape
    nimg = count // PAD
    extra = SMALL if direct else 0
    shapes = [jax.ShapeDtypeStruct((count, width), F4)]
    shapes += [jax.ShapeDtypeStruct((len(m), nt, 4 * dr + extra, LANES), BF) for m in gmasks]
    shapes += [jax.ShapeDtypeStruct((NROWS, width), F4)]
    low = pltpu.VMEM((count, width), BF)
    return pl.pallas_call(
        partial(attn_backward_kernel, nimg, len(sms), len(gubs), gmasks, direct),
        out_shape=shapes,
        in_specs=[SM] + [VM] * 4 + [ANY] * 6 + [VM] * (2 + len(gubs) + len(sms)),
        out_specs=[VM] * len(shapes),
        scratch_shapes=[low] * 6
        + [pltpu.VMEM((width, width), F4)]
        + [pltpu.VMEM(v.shape, v.dtype) for v in saved]
        + [pltpu.SemaphoreType.DMA((6,))],
        compiler_params=params(16),
        cost_estimate=cost(16),
        name="attn_backward",
    )(ids, recv, own, x, cot, *in_hbm(saved), rows, full, *gubs, *sms)


def per_device(
    nd,
    nt,
    tokens,
    cotangent,
    routes,
    slots,
    norm_gains,
    norm_biases,
    w_qkv,
    qv_bias,
    w_out,
    out_bias,
    w_router,
    w_up,
    up_bias,
    w_down,
    down_bias,
):
    me = lax.axis_index("dp").astype(jnp.int32)
    met = lax.axis_index("tensor").astype(jnp.int32)
    width = tokens.shape[1]
    dr = w_qkv.shape[1]
    fr, qr = up_bias.shape[1], qv_bias.shape[1]
    ff = w_up.shape[2]
    nimg = IMG_DEV // nt
    direct = nd == 8 and nt == 4 and dr == HALF and fr == HALF and nd * qr == LANES
    src = jnp.asarray(ring_sources(nt), jnp.int32)[met]
    ids = jnp.concatenate([jnp.stack([me if direct else jnp.zeros_like(me), met]), src])
    even, odd = list(range(0, nd, 2)), list(range(1, nd, 2))

    def canonical(parts):
        if direct:
            return parts
        masks = sum((m for m, _ in parts), ())
        arr = jnp.concatenate([a for _, a in parts], axis=0)
        place = [masks.index(k) for k in range(nd)]
        order = jnp.asarray(place, jnp.int32)[jnp.bitwise_xor(jnp.arange(nd), me)]
        arr = jnp.take(arr, order, axis=0)
        lead = arr.ndim - 2
        arr = jnp.moveaxis(arr, 0, lead - 1)
        arr = arr.reshape(arr.shape[: lead - 1] + (nd * dr,) + arr.shape[-1:])
        return [((0,), arr[None])]

    gmasks = [even, odd] if direct else [[0]]

    def halves(grads, lead, rows):
        if direct:
            return grads
        whole = grads[0][0]
        shape = whole.shape[:lead] + (rows, nd, dr) + whole.shape[-1:]
        whole = jnp.moveaxis(whole.reshape(shape), lead + 1, 0)
        whole = whole.reshape((nd,) + grads[0].shape[1 : lead + 1] + (rows * dr, whole.shape[-1]))
        return [
            jnp.take(whole, jnp.bitwise_xor(jnp.asarray(m, jnp.int32), me), axis=0)
            for m in (even, odd)
        ]

    def images(v):
        return jnp.concatenate(
            [jnp.pad(v[i * SEQ : (i + 1) * SEQ], ((0, PAD - SEQ), (0, 0))) for i in range(nimg)]
        )

    chunk = jnp.concatenate([w_qkv, w_out.T[None]], axis=0)
    if direct:
        wide = [
            jnp.concatenate(
                [norm_gains, norm_biases, out_bias[None], w_router.T, down_bias, jnp.zeros((3, dr), BF)],
                axis=0,
            ),
            jnp.concatenate(
                [up_bias, jnp.pad(qv_bias, ((0, 0), (0, dr - qr))), jnp.zeros((10, dr), BF)], axis=0
            ),
        ]
        chunk = jnp.concatenate([chunk.reshape(4 * dr, LANES), jnp.concatenate(wide, axis=1)], axis=0)
    keep = jnp.where(slots >= 0, routes, -1).reshape(nt * nimg, SEQ, 2)
    keep = jnp.pad(keep, ((0, 0), (0, PAD - SEQ), (0, 0)), constant_values=-1)
    x = images(tokens)
    w_dn = w_down.transpose(0, 2, 1)
    def ring_all(v):
        out = [v]
        for s in range(1, nt):
            out.append(ring_step(out[-1], nt, False))
        return out

    cot = images(cotangent)
    chunk_z = [chunk] + [xor_send(chunk, "tensor", nt, m) for m in range(1, nt)]
    if direct:
        up_near = plane_first(after(w_up, chunk))
        chunk_z, up_near = lax.optimization_barrier((chunk_z, up_near))
        chunk_z = jnp.stack(chunk_z)
        cots = ring_all(after(cot, chunk_z))
        near = plane_first(chunk_z)
        quad = plane_stack(*near, lax.optimization_barrier((plane_far(*near), cots[2]))[0])
        up_far = lax.optimization_barrier((plane_far(*up_near), cots[1]))[0]
        up_quad = plane_stack(*up_near, up_far)
        dn_near = plane_first(after(w_dn, quad))
        quad = after(quad, x, keep, ids, up_quad)
        (_, quad), (_, other) = gather_cores(quad)
        full, rows = assemble(ids, [(CORE0, quad), (CORE1, other)], width)
        up_cores = gather_cores(after(up_quad, quad))
    else:
        cots = ring_all(cot)
        up, dn = (
            canonical(gather_dp(w[None], nd))[0][1][0, 0].transpose(1, 0, 2).reshape(width, EXPERTS * ff)
            for w in (w_up, w_dn)
        )
        full = canonical(gather_dp(jnp.stack(chunk_z), nd))[0][1][0]
        at = jnp.bitwise_xor(jnp.arange(nt), met)
        full = jnp.take(full, at, axis=0).transpose(1, 2, 0, 3).reshape(4, width, width)

        def whole(v):
            return lax.all_gather(v, "dp", axis=v.ndim - 1, tiled=True).astype(F4)

        qvb = lax.all_gather(whole(qv_bias), "tensor", axis=1, tiled=True)
        four = jnp.zeros((4, width), F4)
        rows = [whole(norm_gains), whole(norm_biases), whole(out_bias[None]), qvb]
        rows += [jnp.zeros((1, width), F4), whole(w_router.T), four, whole(down_bias), four]
        rows += [jnp.pad(whole(up_bias), ((0, 0), (0, width - nd * fr))), four]
        rows = jnp.concatenate(rows, axis=0)

    saved = attn_forward(x, rows, full, nimg)
    hn2s = [saved[0]]
    def shard(s, *first):
        hn2 = after(hn2s[s], *first)
        return expert_shard(ids, keep, hn2, cots[s], rows, up, dn, nimg, s)

    for s in range(1, nt):
        hn2s.append(ring_step(after(hn2s[-1], *(cots[-1:] if s == 1 else [])), nt, False))
    if direct:
        up = gather_experts(ids, [(m, after(a, hn2s[0])) for m, a in up_cores], width)
        dn_near = lax.optimization_barrier((dn_near, hn2s[0], cots[3]))[0]
        dn_quad = after(plane_stack(*dn_near, plane_far(*dn_near)), hn2s[1])
        dn = gather_experts(ids, gather_cores(dn_quad), width)
    shards = [None, shard(1)] + [None] * (nt - 2)
    total = past = shards[1][1]
    for s in range(2, nt):
        if s == nt - 1:
            shards[0] = shard(0, past)
            shards[s] = shard(s, shards[0][1])
        else:
            shards[s] = shard(s, shards[s - 1][1])
        total = ring_step(total, nt, False)
        past = total
        total = sums([[[(total, None), (shards[s][1], None)]]])[0]
        past = total if s < nt - 1 else past
    total = ring_step(total, nt, False)
    recv = total

    gubs, *egrads = expert_grads(
        ids,
        [hn2s[0], after(hn2s[1], past), *hn2s[2:]],
        cots,
        [r[2] for r in shards],
        [r[3] for r in shards],
        gmasks,
        dr if direct else width,
    )
    ms = [r[0] for r in shards]
    if direct:
        kept_x, kept_y, send_x, send_y = scatter_first(egrads[0], to(after(egrads[1], recv), 1))
        got_x, got_y = to(send_x, 2), to(send_y, 4)
        recv = after(recv, send_x)
    m_sum = ring_step(after(ms[1], recv), nt, False)

    res = attn_backward(
        ids,
        recv,
        shards[0][1],
        x,
        cots[0],
        saved[1:],
        rows,
        full,
        [gubs],
        [r[4] for r in shards],
        gmasks,
        direct,
        nt,
        dr if direct else width,
    )
    gtok, flat = res[0], res[-1]
    if direct:
        keeps, gots, m_sum = lax.optimization_barrier(
            ((kept_x, kept_y), (got_x, got_y), m_sum, gtok)
        )[:3]
        next_x, next_y, base_x, base_y = scatter_second(*keeps, *gots)
        far_x, far_y = to(next_x, 4), to(next_y, 2)
        m_sum = ring_step(sums([[[(m_sum, None), (ms[2], None)]]])[0], nt, False)
        a_odd = after(res[2], next_x)
        keeps = scatter_first(res[1], to(a_odd, 1))
        a_keep, a_send = keeps[:2], keeps[2:]
        a_got = to(a_send[0], 2), to(a_send[1], 4)
        m_sum = sums([[[(after(m_sum, a_send[0]), None), (ms[3], None)]]])[0]
        a_got, m_sum = lax.optimization_barrier((a_got, m_sum))
        m_sum = ring_step(m_sum, nt, False)
        a_next_x, a_next_y, a_base_x, a_base_y = scatter_second(*a_keep, *a_got)
        a_far = to(a_next_x, 4), to(a_next_y, 2)
        held = sums(
            [[[(b, j), (f, j)]] for b, f in ((a_base_x, a_far[0]), (a_base_y, a_far[1])) for j in (0, 1)]
        )
        far = lax.optimization_barrier(((far_x, far_y), held))[0]
        g_up, g_down = add_all([base_x, far[0]])[0], add_all([base_y, far[1]])[0]
        parts = [held[0]] + [xor_send(held[m], "tensor", nt, m) for m in range(1, nt)]
        g_qkv, g_out, g_gain, g_bias, g_outb, g_router, g_dbias, g_ub, g_qvb = finish(parts, dr, qr)
        g_outb, g_router = g_outb[0], g_router.T
    else:
        egrads = halves(egrads, 2, 1)
        g_up, g_down = add_all(scatter_dp(*egrads, nd))
        held = add_all(scatter_dp(*halves(res[1:-1], 1, 4), nd)).astype(BF)
        mine = add_all([held[0]] + [xor_send(held[m], "tensor", nt, m) for m in range(1, nt)])
        g_qkv, g_out = mine[: 3 * dr].reshape(3, dr, LANES), mine[3 * dr :]
        for s in range(2, nt):
            m_sum = ring_step(add_all([m_sum, ms[s]]).astype(BF), nt, False)
        g_ub = lax.dynamic_slice(lax.psum(flat, "dp"), (UBIAS, me * fr), (EXPERTS, fr))
        flat = lax.psum(flat, ("dp", "tensor"))
        cut = lax.dynamic_slice(flat, (0, me * dr), (NROWS, dr))
        g_gain, g_bias, g_outb = cut[0:2], cut[2:4], cut[4]
        g_router, g_dbias = cut[ROUTER : ROUTER + 4].T, cut[DBIAS : DBIAS + 4]
        g_qvb = lax.dynamic_slice(flat, (QVB, (met * nd + me) * qr), (2, qr))

    def rows_of(v):
        return jnp.concatenate([v[i * PAD : i * PAD + SEQ] for i in range(nimg)])

    layer_out = rows_of(saved[1] + (m_sum.astype(F4) + ms[0].astype(F4)))
    grad_tokens = rows_of(gtok)

    return (
        layer_out,
        grad_tokens,
        g_gain,
        g_bias,
        g_qkv,
        g_qvb,
        g_out.T,
        g_outb,
        g_router,
        g_up,
        g_ub,
        g_down.transpose(0, 2, 1),
        g_dbias,
    )


def solution(mesh):
    nd, nt = mesh.shape["dp"], mesh.shape["tensor"]
    placed = (
        P(("dp", "tensor"), None),
        P(("dp", "tensor"), None),
        P("dp", None),
        P("dp", None),
        P(None, "dp"),
        P(None, "dp"),
        P(None, "dp", "tensor"),
        P(None, ("tensor", "dp")),
        P("tensor", "dp"),
        P("dp"),
        P("dp", None),
        P(None, "dp", "tensor"),
        P(None, ("tensor", "dp")),
        P(None, "tensor", "dp"),
        P(None, "dp"),
    )
    return jax.shard_map(
        partial(per_device, nd, nt),
        mesh=mesh,
        in_specs=placed,
        out_specs=(
            P(("dp", "tensor"), None),
            P(("dp", "tensor"), None),
            P(None, "dp"),
            P(None, "dp"),
            P(None, "dp", "tensor"),
            P(None, ("tensor", "dp")),
            P("tensor", "dp"),
            P("dp"),
            P("dp", None),
            P(None, "dp", "tensor"),
            P(None, ("tensor", "dp")),
            P(None, "tensor", "dp"),
            P(None, "dp"),
        ),
        check_vma=False,
    )
```

```python
from functools import partial

import jax
import jax.numpy as jnp
import numpy as np
from jax import lax
from jax.experimental import pallas as pl
from jax.experimental.pallas import tpu as pltpu
from jax.sharding import PartitionSpec as P

HD = 64
EXPERTS = 4
SEQ = 197
IMG_DEV = 8
PAD = 200
SMALL = 16
EPS = 1e-06
BF = jnp.bfloat16
F4 = jnp.float32
NEG = -1e30
LANES = 128
HALF = 64

NN = (((1,), (0,)), ((), ()))
NT = (((1,), (1,)), ((), ()))
TN = (((0,), (0,)), ((), ()))

VM = pl.BlockSpec()
SM = pl.BlockSpec(memory_space=pltpu.SMEM)
ANY = pl.BlockSpec(memory_space=pltpu.HBM)


def mm(a, b, dims=NN):
    return lax.dot_general(a, b, dims, preferred_element_type=F4)


def params(mib=12):
    return pltpu.CompilerParams(vmem_limit_bytes=mib * 1024 * 1024)


def cost(us):
    return pl.CostEstimate(flops=0, transcendentals=0, bytes_accessed=int(us * 3.3e4))


def xor_send(x, axis, n, mask):
    return lax.ppermute(x, axis, [(i, i ^ mask) for i in range(n)])


def ring_order(n):
    return [0] + list(range(1, n, 2)) + list(range(2, n, 2))[::-1]


def ring_step(x, n, back):
    ring = ring_order(n)
    pairs = [(ring[p], ring[(p + (-1 if back else 1)) % n]) for p in range(n)]
    return lax.ppermute(x, "tensor", pairs)


def ring_sources(n):
    ring = ring_order(n)
    pos = {r: p for p, r in enumerate(ring)}
    return [[ring[(pos[r] - s) % n] for s in range(n)] for r in range(n)]


def stages_of(n):
    if n <= 8:
        inter = list(range(2, n, 2))
        return ([[1]] if n > 1 else []) + ([inter] if inter else [])
    out, bit = [], 1
    while bit < n:
        out.append([bit])
        bit *= 2
    return out


def gather_dp(x, n):
    parts = [((0,), x[None])]
    for stage in reversed(stages_of(n)):
        new = []
        for mask in stage:
            for masks, arr in parts:
                new.append((tuple(k ^ mask for k in masks), xor_send(arr, "dp", n, mask)))
        parts = parts + new
        if n > 8 and stage != [1]:
            parts = [
                (sum((m for m, _ in parts), ()), jnp.concatenate([a for _, a in parts], axis=0))
            ]
    return parts


def scatter_dp(even, odd, n):
    got = xor_send(odd, "dp", n, 1)
    masks = list(range(0, n, 2))
    own = {k: even[i] for i, k in enumerate(masks)}
    new = {k: got[i] for i, k in enumerate(masks)}
    own = {k: (own[k].astype(F4) + new[k].astype(F4)).astype(BF) for k in masks}
    stages = stages_of(n)[1:]
    for at, stage in enumerate(stages):
        span = 0
        for m in stage:
            span |= m
        rest = [k for k in masks if not k & span]
        recv = []
        for m in stage:
            pack = [own[k ^ m] for k in rest]
            send = pack[0] if len(pack) == 1 else jnp.stack(pack)
            back = xor_send(send, "dp", n, m)
            recv.append([back] if len(pack) == 1 else [back[i] for i in range(len(pack))])
        masks = rest
        if at == len(stages) - 1:
            return [own[0]] + [r[0] for r in recv]
        own = {
            k: sum((r[i].astype(F4) for r in recv), own[k].astype(F4)).astype(BF)
            for i, k in enumerate(rest)
        }
    return [own[0]]


CORE0, CORE1 = (0, 2, 4, 6), (1, 3, 5, 7)


def to(x, mask):
    return xor_send(x, "dp", 8, mask)


def plane_first(x):
    return x, to(x, 2), to(x, 4)


def plane_far(x, from_x, from_y):
    half = x.shape[0] // 2
    return to(from_x[:half], 4), to(from_y[half:], 2)


def plane_stack(x, from_x, from_y, far):
    return jnp.stack([x, from_x, from_y, jnp.concatenate(far, axis=0)])


def gather_cores(quad):
    return [(CORE0, quad), (CORE1, to(quad, 1))]


def scatter_first(even, got):
    half = even.shape[1] // 2
    low, high = slice(0, half), slice(half, 2 * half)

    def both(mask, part):
        return [(even, (mask // 2, part)), (got, (mask // 2, part))]

    return sums(
        [
            [both(0, low), both(4, low)],
            [both(0, high), both(2, high)],
            [both(2, low), both(6, low)],
            [both(4, high), both(6, high)],
        ]
    )


def scatter_second(keep_x, keep_y, got_x, got_y):
    pairs = [(keep_x, got_x), (keep_y, got_y)]
    return sums([[[(k, at), (g, at)]] for at in (1, 0) for k, g in pairs])


def after(x, *first):
    return lax.optimization_barrier((x, *first))[0]


def arrays(parts):
    return [a for _, a in parts]


def sums_kernel(outs, count, *refs):
    for groups, out in zip(outs, refs[count:]):
        for j, group in enumerate(groups):
            total = None
            for n, at in group:
                term = (refs[n][...] if at is None else refs[n][at]).astype(F4)
                total = term if total is None else total + term
            if len(groups) == 1:
                out[...] = total.astype(out.dtype)
            else:
                out[j] = total.astype(out.dtype)


def sums(outs):
    known, flat, index, shapes = {}, [], [], []
    for groups in outs:
        index.append([])
        for group in groups:
            index[-1].append([])
            for v, at in group:
                if id(v) not in known:
                    known[id(v)] = len(flat)
                    flat.append(v)
                index[-1][-1].append((known[id(v)], at))
        v, at = groups[0][0]
        shape = v.shape if at is None else np.broadcast_to(0, v.shape)[at].shape
        shapes.append(shape if len(groups) == 1 else (len(groups),) + shape)
    return pl.pallas_call(
        partial(sums_kernel, index, len(flat)),
        out_shape=[jax.ShapeDtypeStruct(v, BF) for v in shapes],
        in_specs=[VM] * len(flat),
        out_specs=[VM] * len(shapes),
        compiler_params=params(16),
        cost_estimate=cost(1),
        name="sums",
    )(*flat)


def finish_kernel(dr, qr, *refs):
    parts, outs = refs[:4], refs[4:]
    g_qkv, g_out, g_gain, g_bias, g_outb, g_router, g_dbias, g_ub, g_qvb = outs
    total = parts[0][...].astype(F4)
    for ref in parts[1:]:
        total = total + ref[...].astype(F4)
    for s in range(3):
        g_qkv[s] = total[s * dr : (s + 1) * dr]
    g_out[...] = total[3 * dr : 4 * dr]
    low = total[4 * dr :]
    high = pltpu.roll(low, HALF, 1)
    g_gain[...] = low[0:2, :HALF]
    g_bias[...] = low[2:4, :HALF]
    g_outb[...] = low[4:5, :HALF]
    g_router[...] = low[5:9, :HALF]
    g_dbias[...] = low[9:13, :HALF]
    g_ub[...] = high[0:4, :HALF]
    g_qvb[...] = high[4:6, :qr]


def finish(parts, dr, qr):
    rows = [(2, HALF), (2, HALF), (1, HALF), (EXPERTS, HALF), (EXPERTS, HALF), (EXPERTS, HALF), (2, qr)]
    shapes = [(3, dr, LANES), (dr, LANES)] + rows
    return pl.pallas_call(
        partial(finish_kernel, dr, qr),
        out_shape=[jax.ShapeDtypeStruct(v, F4) for v in shapes],
        in_specs=[VM] * 4,
        out_specs=[VM] * len(shapes),
        compiler_params=params(),
        cost_estimate=cost(1),
        name="finish",
    )(*parts)


def add_all(parts):
    return sum((p.astype(F4) for p in parts[1:]), parts[0].astype(F4))


def moments(v, eps_rows):
    center = v - jnp.mean(v, axis=-1, keepdims=True)
    inv = lax.rsqrt(jnp.mean(center * center, axis=-1, keepdims=True) + eps_rows)
    return center * inv, inv


def norm_back(z, normed, inv):
    return inv * (
        z
        - jnp.mean(z, axis=-1, keepdims=True)
        - normed * jnp.mean(z * normed, axis=-1, keepdims=True)
    )


def exact(ref, lo, hi):
    return ref[lo:hi, :].astype(BF)


GAIN, BIAS, OUTB, QVB, ROUTER, DBIAS, UBIAS, NROWS = 0, 2, 4, 5, 8, 16, 24, 32


def in_hbm(values):
    return [pltpu.with_memory_space_constraint(v, pltpu.HBM) for v in values]


def run_copies(pairs, sems):
    copies = [pltpu.make_async_copy(a, b, sems.at[n]) for n, (a, b) in enumerate(pairs)]
    for c in copies:
        c.start()
    for c in copies:
        c.wait()


def assemble_kernel(masks, ids, *refs):
    pieces, (w_ref, rows_ref, small_ref, sems) = refs[:-4], refs[-4:]
    me, met = ids[0], ids[1]
    pairs = []
    for group, ref in zip(masks, pieces):
        dr = (ref.shape[2] - SMALL) // 4
        for idx, mask in enumerate(group):
            i = jnp.bitwise_xor(me, mask)
            for jm in range(ref.shape[1]):
                j = jnp.bitwise_xor(met, jm)
                rows_at = pl.ds(pl.multiple_of(i * dr, dr), dr)
                lanes_at = pl.ds(pl.multiple_of(j * LANES, LANES), LANES)
                for s in range(4):
                    pairs.append(
                        (ref.at[idx, jm, s * dr : (s + 1) * dr], w_ref.at[s, rows_at, lanes_at])
                    )
                pairs.append((ref.at[idx, jm, 4 * dr : 4 * dr + SMALL], small_ref.at[mask, jm]))
    run_copies(pairs, sems)
    rows_ref[...] = jnp.zeros(rows_ref.shape, F4)
    lane = lax.broadcasted_iota(jnp.int32, (SMALL, LANES), 1)
    low = lane < HALF
    odd = jnp.bitwise_and(me, 1) == 1
    nd, nt = small_ref.shape[:2]

    def small(mask, jm):
        return small_ref[mask, jm].astype(F4)

    for mask in range(0, nd, 2):
        a, b = small(mask, 0), small(mask + 1, 0)
        first, second = jnp.where(odd, b, a), jnp.where(odd, a, b)
        lo = jnp.where(low, first, pltpu.roll(second, HALF, 1))
        hi = jnp.where(low, pltpu.roll(first, HALF, 1), second)
        tile = jnp.right_shift(jnp.bitwise_xor(me, mask), 1)
        at = pl.ds(pl.multiple_of(tile * LANES, LANES), LANES)
        rows_ref[0:5, at] = lo[0:5]
        rows_ref[ROUTER : ROUTER + EXPERTS, at] = lo[5:9]
        rows_ref[DBIAS : DBIAS + EXPERTS, at] = lo[9:13]
        rows_ref[UBIAS : UBIAS + EXPERTS, at] = hi[0:4]
    qr = LANES // nd
    mine = jnp.logical_and(lane >= HALF, lane < HALF + qr)
    for jm in range(nt):
        j = jnp.bitwise_xor(met, jm)
        total = jnp.zeros((SMALL, LANES), F4)
        for mask in range(nd):
            i = jnp.bitwise_xor(me, mask)
            part = jnp.where(mine, small(mask, jm), 0.0)
            total = total + pltpu.roll(part, jnp.bitwise_and(HALF + i * qr, LANES - 1), 1)
        rows_ref[QVB : QVB + 2, pl.ds(pl.multiple_of(j * LANES, LANES), LANES)] = total[4:6]


def assemble(ids, weights, width):
    masks = [m for m, _ in weights]
    pieces = arrays(weights)
    nd, nt = sum(len(m) for m in masks), pieces[0].shape[1]
    return pl.pallas_call(
        partial(assemble_kernel, masks),
        out_shape=[
            jax.ShapeDtypeStruct((4, width, width), BF),
            jax.ShapeDtypeStruct((NROWS, width), F4),
        ],
        in_specs=[SM] + [ANY] * len(pieces),
        out_specs=[VM, VM],
        scratch_shapes=[
            pltpu.VMEM((nd, nt, SMALL, LANES), BF),
            pltpu.SemaphoreType.DMA((5 * nd * nt,)),
        ],
        compiler_params=params(8),
        cost_estimate=cost(2),
        name="assemble",
    )(ids, *pieces)


def attn_forward_kernel(
    nimg, x_ref, rows_ref, w_ref, hn2_ref, x1_out, q_out, k_out, v_out, o_out, pb_out, *scratch
):
    x1_ref, q_ref, k_ref, v_ref, o_ref, pb_ref, sems = scratch
    heads = w_ref.shape[1] // HD
    copies = []

    def leave(src, dst):
        copies.append(pltpu.make_async_copy(src, dst, sems.at[len(copies)]))
        copies[-1].start()

    width = x_ref.shape[1]
    x = x_ref[...].astype(F4)
    n1, _ = moments(x, EPS)
    hn1 = (n1 * rows_ref[0:1, :] + rows_ref[2:3, :]).astype(BF)
    q_ref[...] = (mm(hn1, w_ref[0]) + rows_ref[5:6, :]).astype(BF)
    k_ref[...] = mm(hn1, w_ref[1]).astype(BF)
    v_ref[...] = (mm(hn1, w_ref[2]) + rows_ref[6:7, :]).astype(BF)
    leave(q_ref, q_out)
    leave(k_ref, k_out)
    leave(v_ref, v_out)
    lane = lax.broadcasted_iota(jnp.int32, (PAD, LANES), 1)
    col = lax.broadcasted_iota(jnp.int32, (PAD, PAD), 1)
    for img in range(nimg):
        at = slice(img * PAD, (img + 1) * PAD)
        for pair in range(width // LANES):
            cols = slice(pair * LANES, (pair + 1) * LANES)
            qp, kp, vp = q_ref[at, cols], k_ref[at, cols], v_ref[at, cols]
            acc = jnp.zeros((PAD, LANES), F4)
            for half in range(2):
                mine = (lane < HD) if half == 0 else (lane >= HD)
                qm = jnp.where(mine, qp * jnp.asarray(HD ** (-0.5), BF), jnp.zeros_like(qp))
                s = mm(qm, kp, NT)
                s = jnp.where(col < SEQ, s, NEG)
                e = jnp.exp(s - jnp.max(s, axis=-1, keepdims=True))
                p = (e * (1.0 / jnp.sum(e, axis=-1, keepdims=True))).astype(BF)
                pb_ref[img * heads + 2 * pair + half] = p
                acc = acc + mm(p, jnp.where(mine, vp, jnp.zeros_like(vp)))
            o_ref[at, cols] = acc.astype(BF)
        mine = pl.ds(img * heads, heads)
        leave(pb_ref.at[mine], pb_out.at[mine])
    leave(o_ref, o_out)
    x1 = x + (mm(o_ref[...], w_ref[3], NT) + rows_ref[4:5, :])
    x1_ref[...] = x1
    leave(x1_ref, x1_out)
    n2, _ = moments(x1, EPS)
    hn2_ref[...] = (n2 * rows_ref[1:2, :] + rows_ref[3:4, :]).astype(BF)
    for c in copies:
        c.wait()


def attn_forward(x, rows, full, nimg):
    count, width = x.shape
    heads = width // HD
    saved = [((count, width), F4)] + [((count, width), BF)] * 4
    saved.append(((nimg * heads, PAD, PAD), BF))
    shapes = [jax.ShapeDtypeStruct((count, width), BF)] + [pltpu.HBM(*v) for v in saved]
    return pl.pallas_call(
        partial(attn_forward_kernel, nimg),
        out_shape=shapes,
        in_specs=[VM] * 3,
        out_specs=[VM] + [ANY] * len(saved),
        scratch_shapes=[pltpu.VMEM(*v) for v in saved] + [pltpu.SemaphoreType.DMA((5 + nimg,))],
        compiler_params=params(),
        cost_estimate=cost(9),
        name="attn_forward",
    )(x, rows, full)


def gather_experts_kernel(masks, ids, *refs):
    pieces, (up_ref, dn_ref, sems) = refs[:-3], refs[-3:]
    me = ids[0]
    pairs = []
    for group, ref in zip(masks, pieces):
        dr, ff = ref.shape[2], ref.shape[3]
        for idx, mask in enumerate(group):
            at = pl.ds(pl.multiple_of(jnp.bitwise_xor(me, mask) * dr, dr), dr)
            for e in range(EXPERTS):
                cols = slice(e * ff, (e + 1) * ff)
                pairs.append((ref.at[idx, e], up_ref.at[at, cols]))
                pairs.append((ref.at[idx, EXPERTS + e], dn_ref.at[at, cols]))
    run_copies(pairs, sems)


def gather_experts(ids, weights, width):
    masks = [m for m, _ in weights]
    pieces = arrays(weights)
    nd = sum(len(m) for m in masks)
    whole = jax.ShapeDtypeStruct((width, EXPERTS * pieces[0].shape[3]), BF)
    return pl.pallas_call(
        partial(gather_experts_kernel, masks),
        out_shape=[whole, whole],
        in_specs=[SM] + [ANY] * len(pieces),
        out_specs=[VM, VM],
        scratch_shapes=[pltpu.SemaphoreType.DMA((2 * EXPERTS * nd,))],
        compiler_params=params(8),
        cost_estimate=cost(3),
        name="gather_experts",
    )(ids, *pieces)


def normal_parts(u):
    bell = jnp.exp(-0.5 * (u * u))
    t = 1.0 / (1.0 + (0.3275911 * 2.0 ** (-0.5)) * jnp.abs(u))
    poly = 0.5 * 1.061405429 * t + 0.5 * (-1.453152027)
    poly = poly * t + 0.5 * 1.421413741
    poly = poly * t + 0.5 * (-0.284496736)
    poly = poly * t + 0.5 * 0.254829592
    tail = poly * t * bell
    return jnp.where(u > 0.0, 1.0 - tail, tail), bell


def expert_kernel(
    nimg, shard, ids, keep_ref, hn2_ref, cot_ref, rows_ref, up_ref, dn_ref, m_ref, d_ref, hg_ref, dhp_ref, sm_ref
):
    own = shard == 0
    count = hn2_ref.shape[0]
    ff = hg_ref.shape[1] // EXPERTS
    hn2, cot = hn2_ref[...], cot_ref[...]
    router = exact(rows_ref, ROUTER, ROUTER + 8)
    lane = lax.broadcasted_iota(jnp.int32, (count, 8), 1)
    logits = jnp.where(lane < EXPERTS, mm(hn2, router, NT), NEG)
    e = jnp.exp(logits - jnp.max(logits, axis=-1, keepdims=True))
    probs = e / jnp.sum(e, axis=-1, keepdims=True)
    tile = ids[2 + shard] * nimg
    keep = jnp.concatenate([keep_ref[tile + i] for i in range(nimg)], axis=0)
    on = jnp.logical_or(lane == keep[:, 0:1], lane == keep[:, 1:2])
    gates = jnp.where(on, probs, 0.0).astype(BF)
    gates_f = gates.astype(F4)
    dp = jnp.zeros((count, 8), F4)
    if own:
        dbias = exact(rows_ref, DBIAS, DBIAS + 8)
        dp = mm(cot, dbias, NT)

    def pair(i, dp):
        for e in (2 * i, 2 * i + 1):
            cols = pl.ds(pl.multiple_of(e * ff, ff), ff)
            mine = lane == e
            gate = jnp.sum(jnp.where(mine, gates_f, 0.0), axis=-1, keepdims=True)
            u = mm(hn2, up_ref[:, cols]) + rows_ref[pl.ds(UBIAS + e, 1), 0:ff]
            phi, bell = normal_parts(u)
            h = u * phi
            slope = phi + u * (bell * 0.3989422804014327)
            r = mm(cot, dn_ref[:, cols])
            dp = dp + jnp.where(mine, jnp.sum(h * r, axis=-1, keepdims=True), 0.0)
            hg_ref[:, cols] = (h * gate).astype(BF)
            dhp_ref[:, cols] = (r * slope * gate).astype(BF)
        return dp

    dp = lax.fori_loop(0, EXPERTS // 2, pair, dp)
    dp = jnp.where(on, dp, 0.0)
    dl = (probs * (dp - jnp.sum(probs * dp, axis=-1, keepdims=True))).astype(BF)
    d_ref[...] = (mm(dhp_ref[...], up_ref[...], NT) + mm(dl, router)).astype(BF)
    m = mm(hg_ref[...], dn_ref[...], NT)
    sm_ref[0:8, :] = mm(dl, hn2, TN)
    if own:
        m = m + mm(gates, dbias)
        sm_ref[8:16, :] = mm(gates, cot, TN)
    else:
        sm_ref[8:16, :] = jnp.zeros((8, sm_ref.shape[1]), F4)
    m_ref[...] = m.astype(BF)


def expert_shard(ids, keep, hn2, cot, rows, up, dn, nimg, shard):
    count, width = hn2.shape
    wide = jax.ShapeDtypeStruct((count, up.shape[1]), BF)
    low = jax.ShapeDtypeStruct((count, width), BF)
    return pl.pallas_call(
        partial(expert_kernel, nimg, shard),
        out_shape=[low, low, wide, wide, jax.ShapeDtypeStruct((16, width), F4)],
        in_specs=[SM] + [VM] * 6,
        out_specs=[VM] * 5,
        compiler_params=params(),
        cost_estimate=cost(7),
        name="expert_shard",
    )(ids, keep, hn2, cot, rows, up, dn)


def expert_grad_kernel(nt, gmasks, ids, *refs):
    hn2s, cots, hgs, dhps = (refs[i * nt : (i + 1) * nt] for i in range(4))
    gub_ref = refs[4 * nt]
    grads = refs[4 * nt + 1 : 4 * nt + 1 + len(gmasks)]
    res_ref = refs[4 * nt + 1 + len(gmasks)]
    me = ids[0]
    ff = gub_ref.shape[2]
    ones = jnp.ones((8, hn2s[0].shape[0]), BF)

    def expert(e, carry):
        cols = pl.ds(pl.multiple_of(e * ff, ff), ff)
        sums_ = [mm(ones, r[:, cols]) for r in dhps]
        gub_ref[e] = sum(sums_[1:], sums_[0])[0:1, :]
        for which in range(2):
            lefts, rights = ((hn2s, dhps), (cots, hgs))[which]
            left = jnp.concatenate([r[...] for r in lefts], axis=0)
            right = jnp.concatenate([r[:, cols] for r in rights], axis=0)
            res_ref[which] = mm(left, right, TN)
            for group, ref in zip(gmasks, grads):
                dr = ref.shape[3]
                for idx, mask in enumerate(group):
                    at = pl.ds(pl.multiple_of(jnp.bitwise_xor(me, mask) * dr, dr), dr)
                    ref[idx, which, e] = res_ref[which, at, :].astype(BF)
        return carry

    lax.fori_loop(0, EXPERTS, expert, 0)


def expert_grads(ids, hn2s, cots, hgs, dhps, gmasks, dr):
    nt = len(hn2s)
    width = hn2s[0].shape[1]
    ff = hgs[0].shape[1] // EXPERTS
    return pl.pallas_call(
        partial(expert_grad_kernel, nt, gmasks),
        out_shape=[jax.ShapeDtypeStruct((EXPERTS, 1, ff), F4)]
        + [jax.ShapeDtypeStruct((len(m), 2, EXPERTS, dr, ff), BF) for m in gmasks],
        in_specs=[SM] + [VM] * (4 * nt),
        out_specs=[VM] * (1 + len(gmasks)),
        scratch_shapes=[pltpu.VMEM((2, width, ff), F4)],
        compiler_params=params(16),
        cost_estimate=cost(9),
        name="expert_grads",
    )(ids, *hn2s, *cots, *hgs, *dhps)


def attn_backward_kernel(nimg, nsm, ngub, gmasks, direct, ids, *refs):
    ins = 12 + ngub + nsm
    recv_ref, own_ref, x_ref, cot_ref = refs[:4]
    rows_ref, w_ref = refs[10:12]
    gubs, sms = refs[12 : 12 + ngub], refs[12 + ngub : ins]
    gtok_ref = refs[ins]
    ngrads = len(gmasks)
    grads = refs[ins + 1 : ins + 1 + ngrads]
    small_ref, do_ref, dq_ref, dk_ref, dv_ref, da_ref, hn1_ref, res_ref = refs[
        ins + 1 + ngrads : ins + 9 + ngrads
    ]
    held = refs[ins + 9 + ngrads :]
    x1_ref, q_ref, k_ref, v_ref, o_ref, pb_ref, sems = held
    copies = [
        pltpu.make_async_copy(a, b, sems.at[n]) for n, (a, b) in enumerate(zip(refs[4:10], held))
    ]
    for c in copies:
        c.start()
    width = x_ref.shape[1]
    dh = recv_ref[...].astype(F4) + own_ref[...].astype(F4)
    cot_f = cot_ref[...].astype(F4)
    copies[0].wait()
    n2, inv2 = moments(x1_ref[...], EPS)
    small_ref[...] = jnp.zeros(small_ref.shape, F4)
    small_ref[1:2, :] = jnp.sum(dh * n2, axis=0, keepdims=True)
    small_ref[3:4, :] = jnp.sum(dh, axis=0, keepdims=True)
    dx1 = cot_f + norm_back(dh * rows_ref[1:2, :], n2, inv2)
    da = dx1.astype(BF)
    da_ref[...] = da
    gtok_ref[...] = dx1
    small_ref[4:5, :] = jnp.sum(da.astype(F4), axis=0, keepdims=True)
    do_ref[...] = mm(da, w_ref[3]).astype(BF)
    lane = lax.broadcasted_iota(jnp.int32, (PAD, LANES), 1)
    scale = HD ** (-0.5)
    for c in copies[1:]:
        c.wait()

    def pairs(at_pair, carry):
        for n in (2 * at_pair, 2 * at_pair + 1):
            cols = pl.ds(pl.multiple_of(n * LANES, LANES), LANES)
            for img in range(nimg):
                at = slice(img * PAD, (img + 1) * PAD)
                qp, kp, vp, dop = q_ref[at, cols], k_ref[at, cols], v_ref[at, cols], do_ref[at, cols]
                zero = jnp.zeros_like(qp)
                dq = jnp.zeros((PAD, LANES), F4)
                dk = jnp.zeros((PAD, LANES), F4)
                dv = jnp.zeros((PAD, LANES), F4)
                for half in range(2):
                    mine = (lane < HD) if half == 0 else (lane >= HD)
                    pb = pb_ref[img * (width // HD) + 2 * n + half]
                    dom = jnp.where(mine, dop, zero)
                    dpb = mm(dom, vp, NT)
                    p = pb.astype(F4)
                    ds = (p * (dpb - jnp.sum(p * dpb, axis=-1, keepdims=True))).astype(BF)
                    dv = dv + mm(pb, dom, TN)
                    dq = dq + mm(ds, jnp.where(mine, kp, zero))
                    dk = dk + mm(ds, jnp.where(mine, qp, zero), TN)
                dq_ref[at, cols] = (dq * scale).astype(BF)
                dk_ref[at, cols] = (dk * scale).astype(BF)
                dv_ref[at, cols] = dv.astype(BF)
        return carry

    lax.fori_loop(0, width // LANES // 2, pairs, 0)
    small_ref[QVB : QVB + 1, :] = jnp.sum(dq_ref[...].astype(F4), axis=0, keepdims=True)
    small_ref[QVB + 1 : QVB + 2, :] = jnp.sum(dv_ref[...].astype(F4), axis=0, keepdims=True)
    dh1 = (
        mm(dq_ref[...], w_ref[0], NT)
        + mm(dk_ref[...], w_ref[1], NT)
        + mm(dv_ref[...], w_ref[2], NT)
    )
    n1, inv1 = moments(x_ref[...].astype(F4), EPS)
    hn1_ref[...] = (n1 * rows_ref[0:1, :] + rows_ref[2:3, :]).astype(BF)
    small_ref[0:1, :] = jnp.sum(dh1 * n1, axis=0, keepdims=True)
    small_ref[2:3, :] = jnp.sum(dh1, axis=0, keepdims=True)
    gtok_ref[...] = gtok_ref[...] + norm_back(dh1 * rows_ref[0:1, :], n1, inv1)
    total = sms[0][...]
    for ref in sms[1:]:
        total = total + ref[...]
    small_ref[ROUTER : ROUTER + 16, :] = total
    for e in range(EXPERTS):
        ref, at = gubs[e * ngub // EXPERTS], e % (EXPERTS // ngub)
        small_ref[UBIAS + e : UBIAS + e + 1, 0 : ref.shape[2]] = ref[at]
    me, met = ids[0], ids[1]
    for s in range(4):
        left, right = [(hn1_ref, dq_ref), (hn1_ref, dk_ref), (hn1_ref, dv_ref), (da_ref, o_ref)][s]
        res_ref[...] = mm(left[...], right[...], TN)
        for group, ref in zip(gmasks, grads):
            dr = (ref.shape[2] - (SMALL if direct else 0)) // 4
            for idx, mask in enumerate(group):
                i = jnp.bitwise_xor(me, mask)
                for jm in range(ref.shape[1]):
                    j = jnp.bitwise_xor(met, jm)
                    ref[idx, jm, s * dr : (s + 1) * dr, :] = res_ref[
                        pl.ds(pl.multiple_of(i * dr, dr), dr),
                        pl.ds(pl.multiple_of(j * LANES, LANES), LANES),
                    ].astype(BF)
    if not direct:
        return
    lane = lax.broadcasted_iota(jnp.int32, (SMALL, LANES), 1)
    row = lax.broadcasted_iota(jnp.int32, (SMALL, LANES), 0)
    nd = sum(len(g) for g in gmasks)
    qr = LANES // nd
    blank = jnp.zeros((3, LANES), F4)
    for group, ref in zip(gmasks, grads):
        for idx, mask in enumerate(group):
            i = jnp.bitwise_xor(me, mask)
            odd = jnp.bitwise_and(i, 1) == 1
            tile = pl.ds(pl.multiple_of(jnp.right_shift(i, 1) * LANES, LANES), LANES)
            t = jnp.concatenate(
                [small_ref[0:5, tile], small_ref[ROUTER : ROUTER + 4, tile], small_ref[DBIAS : DBIAS + 4, tile], blank],
                axis=0,
            )
            lo = jnp.where(odd, pltpu.roll(t, HALF, 1), t)
            lo = jnp.where(lane < HALF, lo, 0.0)
            b = jnp.concatenate([small_ref[UBIAS : UBIAS + 8, tile], jnp.zeros((8, LANES), F4)], axis=0)
            hi = jnp.where(odd, b, pltpu.roll(b, HALF, 1))
            hi = jnp.where(jnp.logical_and(lane >= HALF, row < EXPERTS), hi, 0.0)
            for jm in range(ref.shape[1]):
                j = jnp.bitwise_xor(met, jm)
                g = small_ref[0:8, pl.ds(pl.multiple_of(j * LANES, LANES), LANES)]
                g = pltpu.roll(g, 7, 0)
                g = pltpu.roll(g, jnp.bitwise_and(HALF - i * qr + LANES, LANES - 1), 1)
                g = jnp.concatenate([g, jnp.zeros((8, LANES), F4)], axis=0)
                mine = jnp.logical_and(lane >= HALF, lane < HALF + qr)
                mine = jnp.logical_and(mine, jnp.logical_and(row >= 4, row < 6))
                block = lo + jnp.where(mine, g, 0.0)
                if jm == 0:
                    block = block + hi
                ref[idx, jm, 4 * dr :, :] = block.astype(BF)


def attn_backward(ids, recv, own, x, cot, saved, rows, full, gubs, sms, gmasks, direct, nt, dr):
    count, width = x.shape
    nimg = count // PAD
    extra = SMALL if direct else 0
    shapes = [jax.ShapeDtypeStruct((count, width), F4)]
    shapes += [jax.ShapeDtypeStruct((len(m), nt, 4 * dr + extra, LANES), BF) for m in gmasks]
    shapes += [jax.ShapeDtypeStruct((NROWS, width), F4)]
    low = pltpu.VMEM((count, width), BF)
    return pl.pallas_call(
        partial(attn_backward_kernel, nimg, len(sms), len(gubs), gmasks, direct),
        out_shape=shapes,
        in_specs=[SM] + [VM] * 4 + [ANY] * 6 + [VM] * (2 + len(gubs) + len(sms)),
        out_specs=[VM] * len(shapes),
        scratch_shapes=[low] * 6
        + [pltpu.VMEM((width, width), F4)]
        + [pltpu.VMEM(v.shape, v.dtype) for v in saved]
        + [pltpu.SemaphoreType.DMA((6,))],
        compiler_params=params(16),
        cost_estimate=cost(16),
        name="attn_backward",
    )(ids, recv, own, x, cot, *in_hbm(saved), rows, full, *gubs, *sms)


def per_device(
    nd,
    nt,
    tokens,
    cotangent,
    routes,
    slots,
    norm_gains,
    norm_biases,
    w_qkv,
    qv_bias,
    w_out,
    out_bias,
    w_router,
    w_up,
    up_bias,
    w_down,
    down_bias,
):
    me = lax.axis_index("dp").astype(jnp.int32)
    met = lax.axis_index("tensor").astype(jnp.int32)
    width = tokens.shape[1]
    dr = w_qkv.shape[1]
    fr, qr = up_bias.shape[1], qv_bias.shape[1]
    ff = w_up.shape[2]
    nimg = IMG_DEV // nt
    direct = nd == 8 and nt == 4 and dr == HALF and fr == HALF and nd * qr == LANES
    src = jnp.asarray(ring_sources(nt), jnp.int32)[met]
    ids = jnp.concatenate([jnp.stack([me if direct else jnp.zeros_like(me), met]), src])
    even, odd = list(range(0, nd, 2)), list(range(1, nd, 2))

    def canonical(parts):
        if direct:
            return parts
        masks = sum((m for m, _ in parts), ())
        arr = jnp.concatenate([a for _, a in parts], axis=0)
        place = [masks.index(k) for k in range(nd)]
        order = jnp.asarray(place, jnp.int32)[jnp.bitwise_xor(jnp.arange(nd), me)]
        arr = jnp.take(arr, order, axis=0)
        lead = arr.ndim - 2
        arr = jnp.moveaxis(arr, 0, lead - 1)
        arr = arr.reshape(arr.shape[: lead - 1] + (nd * dr,) + arr.shape[-1:])
        return [((0,), arr[None])]

    gmasks = [even, odd] if direct else [[0]]

    def halves(grads, lead, rows):
        if direct:
            return grads
        whole = grads[0][0]
        shape = whole.shape[:lead] + (rows, nd, dr) + whole.shape[-1:]
        whole = jnp.moveaxis(whole.reshape(shape), lead + 1, 0)
        whole = whole.reshape((nd,) + grads[0].shape[1 : lead + 1] + (rows * dr, whole.shape[-1]))
        return [
            jnp.take(whole, jnp.bitwise_xor(jnp.asarray(m, jnp.int32), me), axis=0)
            for m in (even, odd)
        ]

    def images(v):
        return jnp.concatenate(
            [jnp.pad(v[i * SEQ : (i + 1) * SEQ], ((0, PAD - SEQ), (0, 0))) for i in range(nimg)]
        )

    chunk = jnp.concatenate([w_qkv, w_out.T[None]], axis=0)
    if direct:
        wide = [
            jnp.concatenate(
                [norm_gains, norm_biases, out_bias[None], w_router.T, down_bias, jnp.zeros((3, dr), BF)],
                axis=0,
            ),
            jnp.concatenate(
                [up_bias, jnp.pad(qv_bias, ((0, 0), (0, dr - qr))), jnp.zeros((10, dr), BF)], axis=0
            ),
        ]
        chunk = jnp.concatenate([chunk.reshape(4 * dr, LANES), jnp.concatenate(wide, axis=1)], axis=0)
    keep = jnp.where(slots >= 0, routes, -1).reshape(nt * nimg, SEQ, 2)
    keep = jnp.pad(keep, ((0, 0), (0, PAD - SEQ), (0, 0)), constant_values=-1)
    x = images(tokens)
    w_dn = w_down.transpose(0, 2, 1)
    def ring_all(v):
        out = [v]
        for s in range(1, nt):
            out.append(ring_step(out[-1], nt, False))
        return out

    cot = images(cotangent)
    chunk_z = [chunk] + [xor_send(chunk, "tensor", nt, m) for m in range(1, nt)]
    if direct:
        chunk_z = jnp.stack(chunk_z)
        cots = ring_all(after(cot, chunk_z))
        near = plane_first(chunk_z)
        quad = plane_stack(*near, lax.optimization_barrier((plane_far(*near), cots[1]))[0])
        layers = plane_first(after(jnp.concatenate([w_up, w_dn]), quad))
        full, rows = assemble(ids, gather_cores(after(quad, x, keep, ids)), width)
    else:
        cots = ring_all(cot)
        up, dn = (
            canonical(gather_dp(w[None], nd))[0][1][0, 0].transpose(1, 0, 2).reshape(width, EXPERTS * ff)
            for w in (w_up, w_dn)
        )
        full = canonical(gather_dp(jnp.stack(chunk_z), nd))[0][1][0]
        at = jnp.bitwise_xor(jnp.arange(nt), met)
        full = jnp.take(full, at, axis=0).transpose(1, 2, 0, 3).reshape(4, width, width)

        def whole(v):
            return lax.all_gather(v, "dp", axis=v.ndim - 1, tiled=True).astype(F4)

        qvb = lax.all_gather(whole(qv_bias), "tensor", axis=1, tiled=True)
        four = jnp.zeros((4, width), F4)
        rows = [whole(norm_gains), whole(norm_biases), whole(out_bias[None]), qvb]
        rows += [jnp.zeros((1, width), F4), whole(w_router.T), four, whole(down_bias), four]
        rows += [jnp.pad(whole(up_bias), ((0, 0), (0, width - nd * fr))), four]
        rows = jnp.concatenate(rows, axis=0)

    saved = attn_forward(x, rows, full, nimg)
    hn2s = [saved[0]]
    def shard(s, *first):
        hn2 = after(hn2s[s], *first)
        return expert_shard(ids, keep, hn2, cots[s], rows, up, dn, nimg, s)

    for s in range(1, nt):
        hn2s.append(ring_step(after(hn2s[-1], *(cots[2:] if s == nt - 1 else [])), nt, False))
    if direct:
        layers = lax.optimization_barrier((layers, hn2s[0], cots[2]))[0]
        far = lax.optimization_barrier((plane_far(*layers), hn2s[1]))[0]
        layers = plane_stack(*layers, far)
        up, dn = gather_experts(ids, gather_cores(layers), width)
    shards = [None, shard(1)] + [None] * (nt - 2)
    total = past = shards[1][1]
    for s in range(2, nt):
        if s == nt - 1:
            shards[0] = shard(0, past)
            shards[s] = shard(s, shards[0][1])
        else:
            shards[s] = shard(s, shards[s - 1][1])
        total = ring_step(total, nt, False)
        past = total
        total = sums([[[(total, None), (shards[s][1], None)]]])[0]
        past = total if s < nt - 1 else past
    total = ring_step(total, nt, False)
    recv = total

    gubs, *egrads = expert_grads(
        ids,
        [hn2s[0], after(hn2s[1], past), *hn2s[2:]],
        cots,
        [r[2] for r in shards],
        [r[3] for r in shards],
        gmasks,
        dr if direct else width,
    )
    ms = [r[0] for r in shards]
    if direct:
        kept_x, kept_y, send_x, send_y = scatter_first(egrads[0], to(after(egrads[1], recv), 1))
        got_x, got_y = to(send_x, 2), to(send_y, 4)
        recv = after(recv, send_x)
    m_sum = ring_step(after(ms[1], recv), nt, False)

    res = attn_backward(
        ids,
        recv,
        shards[0][1],
        x,
        cots[0],
        saved[1:],
        rows,
        full,
        [gubs],
        [r[4] for r in shards],
        gmasks,
        direct,
        nt,
        dr if direct else width,
    )
    gtok, flat = res[0], res[-1]
    if direct:
        keeps, gots, m_sum = lax.optimization_barrier(
            ((kept_x, kept_y), (got_x, got_y), m_sum, gtok)
        )[:3]
        next_x, next_y, base_x, base_y = scatter_second(*keeps, *gots)
        far_x, far_y = to(next_x, 4), to(next_y, 2)
        m_sum = ring_step(sums([[[(m_sum, None), (ms[2], None)]]])[0], nt, False)
        a_odd = after(res[2], next_x)
        keeps = scatter_first(res[1], to(a_odd, 1))
        a_keep, a_send = keeps[:2], keeps[2:]
        a_got = to(a_send[0], 2), to(a_send[1], 4)
        m_sum = sums([[[(after(m_sum, a_send[0]), None), (ms[3], None)]]])[0]
        a_got, m_sum = lax.optimization_barrier((a_got, m_sum))
        m_sum = ring_step(m_sum, nt, False)
        a_next_x, a_next_y, a_base_x, a_base_y = scatter_second(*a_keep, *a_got)
        a_far = to(a_next_x, 4), to(a_next_y, 2)
        held = sums(
            [[[(b, j), (f, j)]] for b, f in ((a_base_x, a_far[0]), (a_base_y, a_far[1])) for j in (0, 1)]
        )
        far = lax.optimization_barrier(((far_x, far_y), held))[0]
        g_up, g_down = add_all([base_x, far[0]])[0], add_all([base_y, far[1]])[0]
        parts = [held[0]] + [xor_send(held[m], "tensor", nt, m) for m in range(1, nt)]
        g_qkv, g_out, g_gain, g_bias, g_outb, g_router, g_dbias, g_ub, g_qvb = finish(parts, dr, qr)
        g_outb, g_router = g_outb[0], g_router.T
    else:
        egrads = halves(egrads, 2, 1)
        g_up, g_down = add_all(scatter_dp(*egrads, nd))
        held = add_all(scatter_dp(*halves(res[1:-1], 1, 4), nd)).astype(BF)
        mine = add_all([held[0]] + [xor_send(held[m], "tensor", nt, m) for m in range(1, nt)])
        g_qkv, g_out = mine[: 3 * dr].reshape(3, dr, LANES), mine[3 * dr :]
        for s in range(2, nt):
            m_sum = ring_step(add_all([m_sum, ms[s]]).astype(BF), nt, False)
        g_ub = lax.dynamic_slice(lax.psum(flat, "dp"), (UBIAS, me * fr), (EXPERTS, fr))
        flat = lax.psum(flat, ("dp", "tensor"))
        cut = lax.dynamic_slice(flat, (0, me * dr), (NROWS, dr))
        g_gain, g_bias, g_outb = cut[0:2], cut[2:4], cut[4]
        g_router, g_dbias = cut[ROUTER : ROUTER + 4].T, cut[DBIAS : DBIAS + 4]
        g_qvb = lax.dynamic_slice(flat, (QVB, (met * nd + me) * qr), (2, qr))

    def rows_of(v):
        return jnp.concatenate([v[i * PAD : i * PAD + SEQ] for i in range(nimg)])

    layer_out = rows_of(saved[1] + (m_sum.astype(F4) + ms[0].astype(F4)))
    grad_tokens = rows_of(gtok)

    return (
        layer_out,
        grad_tokens,
        g_gain,
        g_bias,
        g_qkv,
        g_qvb,
        g_out.T,
        g_outb,
        g_router,
        g_up,
        g_ub,
        g_down.transpose(0, 2, 1),
        g_dbias,
    )


def solution(mesh):
    nd, nt = mesh.shape["dp"], mesh.shape["tensor"]
    placed = (
        P(("dp", "tensor"), None),
        P(("dp", "tensor"), None),
        P("dp", None),
        P("dp", None),
        P(None, "dp"),
        P(None, "dp"),
        P(None, "dp", "tensor"),
        P(None, ("tensor", "dp")),
        P("tensor", "dp"),
        P("dp"),
        P("dp", None),
        P(None, "dp", "tensor"),
        P(None, ("tensor", "dp")),
        P(None, "tensor", "dp"),
        P(None, "dp"),
    )
    return jax.shard_map(
        partial(per_device, nd, nt),
        mesh=mesh,
        in_specs=placed,
        out_specs=(
            P(("dp", "tensor"), None),
            P(("dp", "tensor"), None),
            P(None, "dp"),
            P(None, "dp"),
            P(None, "dp", "tensor"),
            P(None, ("tensor", "dp")),
            P("tensor", "dp"),
            P("dp"),
            P("dp", None),
            P(None, "dp", "tensor"),
            P(None, ("tensor", "dp")),
            P(None, "tensor", "dp"),
            P(None, "dp"),
        ),
        check_vma=False,
    )
```

```python
from functools import partial

import jax
import jax.numpy as jnp
import numpy as np
from jax import lax
from jax.experimental import pallas as pl
from jax.experimental.pallas import tpu as pltpu
from jax.sharding import PartitionSpec as P

HD = 64
EXPERTS = 4
SEQ = 197
IMG_DEV = 8
PAD = 200
SMALL = 16
EPS = 1e-06
BF = jnp.bfloat16
F4 = jnp.float32
NEG = -1e30
LANES = 128
HALF = 64

NN = (((1,), (0,)), ((), ()))
NT = (((1,), (1,)), ((), ()))
TN = (((0,), (0,)), ((), ()))

VM = pl.BlockSpec()
SM = pl.BlockSpec(memory_space=pltpu.SMEM)
ANY = pl.BlockSpec(memory_space=pltpu.HBM)


def mm(a, b, dims=NN):
    return lax.dot_general(a, b, dims, preferred_element_type=F4)


def params(mib=12):
    return pltpu.CompilerParams(vmem_limit_bytes=mib * 1024 * 1024)


def cost(us):
    return pl.CostEstimate(flops=0, transcendentals=0, bytes_accessed=int(us * 3.3e4))


def xor_send(x, axis, n, mask):
    return lax.ppermute(x, axis, [(i, i ^ mask) for i in range(n)])


def ring_order(n):
    return [0] + list(range(1, n, 2)) + list(range(2, n, 2))[::-1]


def ring_step(x, n, back):
    ring = ring_order(n)
    pairs = [(ring[p], ring[(p + (-1 if back else 1)) % n]) for p in range(n)]
    return lax.ppermute(x, "tensor", pairs)


def ring_sources(n):
    ring = ring_order(n)
    pos = {r: p for p, r in enumerate(ring)}
    return [[ring[(pos[r] - s) % n] for s in range(n)] for r in range(n)]


def stages_of(n):
    if n <= 8:
        inter = list(range(2, n, 2))
        return ([[1]] if n > 1 else []) + ([inter] if inter else [])
    out, bit = [], 1
    while bit < n:
        out.append([bit])
        bit *= 2
    return out


def gather_dp(x, n):
    parts = [((0,), x[None])]
    for stage in reversed(stages_of(n)):
        new = []
        for mask in stage:
            for masks, arr in parts:
                new.append((tuple(k ^ mask for k in masks), xor_send(arr, "dp", n, mask)))
        parts = parts + new
        if n > 8 and stage != [1]:
            parts = [
                (sum((m for m, _ in parts), ()), jnp.concatenate([a for _, a in parts], axis=0))
            ]
    return parts


def scatter_dp(even, odd, n):
    got = xor_send(odd, "dp", n, 1)
    masks = list(range(0, n, 2))
    own = {k: even[i] for i, k in enumerate(masks)}
    new = {k: got[i] for i, k in enumerate(masks)}
    own = {k: (own[k].astype(F4) + new[k].astype(F4)).astype(BF) for k in masks}
    stages = stages_of(n)[1:]
    for at, stage in enumerate(stages):
        span = 0
        for m in stage:
            span |= m
        rest = [k for k in masks if not k & span]
        recv = []
        for m in stage:
            pack = [own[k ^ m] for k in rest]
            send = pack[0] if len(pack) == 1 else jnp.stack(pack)
            back = xor_send(send, "dp", n, m)
            recv.append([back] if len(pack) == 1 else [back[i] for i in range(len(pack))])
        masks = rest
        if at == len(stages) - 1:
            return [own[0]] + [r[0] for r in recv]
        own = {
            k: sum((r[i].astype(F4) for r in recv), own[k].astype(F4)).astype(BF)
            for i, k in enumerate(rest)
        }
    return [own[0]]


CORE0, CORE1 = (0, 2, 4, 6), (1, 3, 5, 7)


def to(x, mask):
    return xor_send(x, "dp", 8, mask)


def plane_first(x):
    return x, to(x, 2), to(x, 4)


def plane_far(x, from_x, from_y):
    half = x.shape[0] // 2
    return to(from_x[:half], 4), to(from_y[half:], 2)


def plane_stack(x, from_x, from_y, far):
    return jnp.stack([x, from_x, from_y, jnp.concatenate(far, axis=0)])


def gather_cores(quad):
    return [(CORE0, quad), (CORE1, to(quad, 1))]


def scatter_first(even, got):
    half = even.shape[1] // 2
    low, high = slice(0, half), slice(half, 2 * half)

    def both(mask, part):
        return [(even, (mask // 2, part)), (got, (mask // 2, part))]

    return sums(
        [
            [both(0, low), both(4, low)],
            [both(0, high), both(2, high)],
            [both(2, low), both(6, low)],
            [both(4, high), both(6, high)],
        ]
    )


def scatter_second(keep_x, keep_y, got_x, got_y):
    pairs = [(keep_x, got_x), (keep_y, got_y)]
    return sums([[[(k, at), (g, at)]] for at in (1, 0) for k, g in pairs])


def after(x, *first):
    return lax.optimization_barrier((x, *first))[0]


def arrays(parts):
    return [a for _, a in parts]


def sums_kernel(outs, count, *refs):
    for groups, out in zip(outs, refs[count:]):
        for j, group in enumerate(groups):
            total = None
            for n, at in group:
                term = (refs[n][...] if at is None else refs[n][at]).astype(F4)
                total = term if total is None else total + term
            if len(groups) == 1:
                out[...] = total.astype(out.dtype)
            else:
                out[j] = total.astype(out.dtype)


def sums(outs):
    known, flat, index, shapes = {}, [], [], []
    for groups in outs:
        index.append([])
        for group in groups:
            index[-1].append([])
            for v, at in group:
                if id(v) not in known:
                    known[id(v)] = len(flat)
                    flat.append(v)
                index[-1][-1].append((known[id(v)], at))
        v, at = groups[0][0]
        shape = v.shape if at is None else np.broadcast_to(0, v.shape)[at].shape
        shapes.append(shape if len(groups) == 1 else (len(groups),) + shape)
    return pl.pallas_call(
        partial(sums_kernel, index, len(flat)),
        out_shape=[jax.ShapeDtypeStruct(v, BF) for v in shapes],
        in_specs=[VM] * len(flat),
        out_specs=[VM] * len(shapes),
        compiler_params=params(16),
        cost_estimate=cost(1),
        name="sums",
    )(*flat)


def finish_kernel(dr, qr, *refs):
    parts, outs = refs[:2], refs[2:]
    g_qkv, g_out, g_gain, g_bias, g_outb, g_router, g_dbias, g_ub, g_qvb = outs
    total = parts[0][...].astype(F4)
    for ref in parts[1:]:
        total = total + ref[...].astype(F4)
    for s in range(3):
        g_qkv[s] = total[s * dr : (s + 1) * dr]
    g_out[...] = total[3 * dr : 4 * dr]
    low = total[4 * dr :]
    high = pltpu.roll(low, HALF, 1)
    g_gain[...] = low[0:2, :HALF]
    g_bias[...] = low[2:4, :HALF]
    g_outb[...] = low[4:5, :HALF]
    g_router[...] = low[5:9, :HALF]
    g_dbias[...] = low[9:13, :HALF]
    g_ub[...] = high[0:4, :HALF]
    g_qvb[...] = high[4:6, :qr]


def finish(parts, dr, qr):
    rows = [(2, HALF), (2, HALF), (1, HALF), (EXPERTS, HALF), (EXPERTS, HALF), (EXPERTS, HALF), (2, qr)]
    shapes = [(3, dr, LANES), (dr, LANES)] + rows
    return pl.pallas_call(
        partial(finish_kernel, dr, qr),
        out_shape=[jax.ShapeDtypeStruct(v, F4) for v in shapes],
        in_specs=[VM] * 2,
        out_specs=[VM] * len(shapes),
        compiler_params=params(),
        cost_estimate=cost(1),
        name="finish",
    )(*parts)


def add_all(parts):
    return sum((p.astype(F4) for p in parts[1:]), parts[0].astype(F4))


def moments(v, eps_rows):
    center = v - jnp.mean(v, axis=-1, keepdims=True)
    inv = lax.rsqrt(jnp.mean(center * center, axis=-1, keepdims=True) + eps_rows)
    return center * inv, inv


def norm_back(z, normed, inv):
    return inv * (
        z
        - jnp.mean(z, axis=-1, keepdims=True)
        - normed * jnp.mean(z * normed, axis=-1, keepdims=True)
    )


def exact(ref, lo, hi):
    return ref[lo:hi, :].astype(BF)


GAIN, BIAS, OUTB, QVB, ROUTER, DBIAS, UBIAS, NROWS = 0, 2, 4, 5, 8, 16, 24, 32


def in_hbm(values):
    return [pltpu.with_memory_space_constraint(v, pltpu.HBM) for v in values]


def run_copies(pairs, sems):
    copies = [pltpu.make_async_copy(a, b, sems.at[n]) for n, (a, b) in enumerate(pairs)]
    for c in copies:
        c.start()
    for c in copies:
        c.wait()


def assemble_kernel(masks, ids, *refs):
    pieces, (w_ref, rows_ref, small_ref, sems) = refs[:-4], refs[-4:]
    me, met = ids[0], ids[1]
    pairs = []
    for group, ref in zip(masks, pieces):
        dr = (ref.shape[2] - SMALL) // 4
        for idx, mask in enumerate(group):
            i = jnp.bitwise_xor(me, mask)
            for jm in range(ref.shape[1]):
                j = jnp.bitwise_xor(met, jm)
                rows_at = pl.ds(pl.multiple_of(i * dr, dr), dr)
                lanes_at = pl.ds(pl.multiple_of(j * LANES, LANES), LANES)
                for s in range(4):
                    pairs.append(
                        (ref.at[idx, jm, s * dr : (s + 1) * dr], w_ref.at[s, rows_at, lanes_at])
                    )
                pairs.append((ref.at[idx, jm, 4 * dr : 4 * dr + SMALL], small_ref.at[mask, jm]))
    run_copies(pairs, sems)
    rows_ref[...] = jnp.zeros(rows_ref.shape, F4)
    lane = lax.broadcasted_iota(jnp.int32, (SMALL, LANES), 1)
    low = lane < HALF
    odd = jnp.bitwise_and(me, 1) == 1
    nd, nt = small_ref.shape[:2]

    def small(mask, jm):
        return small_ref[mask, jm].astype(F4)

    for mask in range(0, nd, 2):
        a, b = small(mask, 0), small(mask + 1, 0)
        first, second = jnp.where(odd, b, a), jnp.where(odd, a, b)
        lo = jnp.where(low, first, pltpu.roll(second, HALF, 1))
        hi = jnp.where(low, pltpu.roll(first, HALF, 1), second)
        tile = jnp.right_shift(jnp.bitwise_xor(me, mask), 1)
        at = pl.ds(pl.multiple_of(tile * LANES, LANES), LANES)
        rows_ref[0:5, at] = lo[0:5]
        rows_ref[ROUTER : ROUTER + EXPERTS, at] = lo[5:9]
        rows_ref[DBIAS : DBIAS + EXPERTS, at] = lo[9:13]
        rows_ref[UBIAS : UBIAS + EXPERTS, at] = hi[0:4]
    qr = LANES // nd
    mine = jnp.logical_and(lane >= HALF, lane < HALF + qr)
    for jm in range(nt):
        j = jnp.bitwise_xor(met, jm)
        total = jnp.zeros((SMALL, LANES), F4)
        for mask in range(nd):
            i = jnp.bitwise_xor(me, mask)
            part = jnp.where(mine, small(mask, jm), 0.0)
            total = total + pltpu.roll(part, jnp.bitwise_and(HALF + i * qr, LANES - 1), 1)
        rows_ref[QVB : QVB + 2, pl.ds(pl.multiple_of(j * LANES, LANES), LANES)] = total[4:6]


def assemble(ids, weights, width):
    masks = [m for m, _ in weights]
    pieces = arrays(weights)
    nd, nt = sum(len(m) for m in masks), pieces[0].shape[1]
    return pl.pallas_call(
        partial(assemble_kernel, masks),
        out_shape=[
            jax.ShapeDtypeStruct((4, width, width), BF),
            jax.ShapeDtypeStruct((NROWS, width), F4),
        ],
        in_specs=[SM] + [ANY] * len(pieces),
        out_specs=[VM, VM],
        scratch_shapes=[
            pltpu.VMEM((nd, nt, SMALL, LANES), BF),
            pltpu.SemaphoreType.DMA((5 * nd * nt,)),
        ],
        compiler_params=params(8),
        cost_estimate=cost(2),
        name="assemble",
    )(ids, *pieces)


def attn_forward_kernel(
    nimg, x_ref, rows_ref, w_ref, hn2_ref, x1_out, q_out, k_out, v_out, o_out, pb_out, *scratch
):
    x1_ref, q_ref, k_ref, v_ref, o_ref, pb_ref, sems = scratch
    heads = w_ref.shape[1] // HD
    copies = []

    def leave(src, dst):
        copies.append(pltpu.make_async_copy(src, dst, sems.at[len(copies)]))
        copies[-1].start()

    width = x_ref.shape[1]
    x = x_ref[...].astype(F4)
    n1, _ = moments(x, EPS)
    hn1 = (n1 * rows_ref[0:1, :] + rows_ref[2:3, :]).astype(BF)
    q_ref[...] = (mm(hn1, w_ref[0]) + rows_ref[5:6, :]).astype(BF)
    k_ref[...] = mm(hn1, w_ref[1]).astype(BF)
    v_ref[...] = (mm(hn1, w_ref[2]) + rows_ref[6:7, :]).astype(BF)
    leave(q_ref, q_out)
    leave(k_ref, k_out)
    leave(v_ref, v_out)
    lane = lax.broadcasted_iota(jnp.int32, (PAD, LANES), 1)
    col = lax.broadcasted_iota(jnp.int32, (PAD, PAD), 1)
    for img in range(nimg):
        at = slice(img * PAD, (img + 1) * PAD)
        for pair in range(width // LANES):
            cols = slice(pair * LANES, (pair + 1) * LANES)
            qp, kp, vp = q_ref[at, cols], k_ref[at, cols], v_ref[at, cols]
            acc = jnp.zeros((PAD, LANES), F4)
            for half in range(2):
                mine = (lane < HD) if half == 0 else (lane >= HD)
                qm = jnp.where(mine, qp * jnp.asarray(HD ** (-0.5), BF), jnp.zeros_like(qp))
                s = mm(qm, kp, NT)
                s = jnp.where(col < SEQ, s, NEG)
                e = jnp.exp(s - jnp.max(s, axis=-1, keepdims=True))
                p = (e * (1.0 / jnp.sum(e, axis=-1, keepdims=True))).astype(BF)
                pb_ref[img * heads + 2 * pair + half] = p
                acc = acc + mm(p, jnp.where(mine, vp, jnp.zeros_like(vp)))
            o_ref[at, cols] = acc.astype(BF)
        mine = pl.ds(img * heads, heads)
        leave(pb_ref.at[mine], pb_out.at[mine])
    leave(o_ref, o_out)
    x1 = x + (mm(o_ref[...], w_ref[3], NT) + rows_ref[4:5, :])
    x1_ref[...] = x1
    leave(x1_ref, x1_out)
    n2, _ = moments(x1, EPS)
    hn2_ref[...] = (n2 * rows_ref[1:2, :] + rows_ref[3:4, :]).astype(BF)
    for c in copies:
        c.wait()


def attn_forward(x, rows, full, nimg):
    count, width = x.shape
    heads = width // HD
    saved = [((count, width), F4)] + [((count, width), BF)] * 4
    saved.append(((nimg * heads, PAD, PAD), BF))
    shapes = [jax.ShapeDtypeStruct((count, width), BF)] + [pltpu.HBM(*v) for v in saved]
    return pl.pallas_call(
        partial(attn_forward_kernel, nimg),
        out_shape=shapes,
        in_specs=[VM] * 3,
        out_specs=[VM] + [ANY] * len(saved),
        scratch_shapes=[pltpu.VMEM(*v) for v in saved] + [pltpu.SemaphoreType.DMA((5 + nimg,))],
        compiler_params=params(),
        cost_estimate=cost(9),
        name="attn_forward",
    )(x, rows, full)


def gather_experts_kernel(masks, ids, *refs):
    pieces, (up_ref, dn_ref, sems) = refs[:-3], refs[-3:]
    me = ids[0]
    pairs = []
    for group, ref in zip(masks, pieces):
        dr, ff = ref.shape[2], ref.shape[3]
        for idx, mask in enumerate(group):
            at = pl.ds(pl.multiple_of(jnp.bitwise_xor(me, mask) * dr, dr), dr)
            for e in range(EXPERTS):
                cols = slice(e * ff, (e + 1) * ff)
                pairs.append((ref.at[idx, e], up_ref.at[at, cols]))
                pairs.append((ref.at[idx, EXPERTS + e], dn_ref.at[at, cols]))
    run_copies(pairs, sems)


def gather_experts(ids, weights, width):
    masks = [m for m, _ in weights]
    pieces = arrays(weights)
    nd = sum(len(m) for m in masks)
    whole = jax.ShapeDtypeStruct((width, EXPERTS * pieces[0].shape[3]), BF)
    return pl.pallas_call(
        partial(gather_experts_kernel, masks),
        out_shape=[whole, whole],
        in_specs=[SM] + [ANY] * len(pieces),
        out_specs=[VM, VM],
        scratch_shapes=[pltpu.SemaphoreType.DMA((2 * EXPERTS * nd,))],
        compiler_params=params(8),
        cost_estimate=cost(3),
        name="gather_experts",
    )(ids, *pieces)


def normal_parts(u):
    bell = jnp.exp(-0.5 * (u * u))
    t = 1.0 / (1.0 + (0.3275911 * 2.0 ** (-0.5)) * jnp.abs(u))
    poly = 0.5 * 1.061405429 * t + 0.5 * (-1.453152027)
    poly = poly * t + 0.5 * 1.421413741
    poly = poly * t + 0.5 * (-0.284496736)
    poly = poly * t + 0.5 * 0.254829592
    tail = poly * t * bell
    return jnp.where(u > 0.0, 1.0 - tail, tail), bell


def expert_kernel(
    nimg, shard, ids, keep_ref, hn2_ref, cot_ref, rows_ref, up_ref, dn_ref, m_ref, d_ref, hg_ref, dhp_ref, sm_ref
):
    own = shard == 0
    count = hn2_ref.shape[0]
    ff = hg_ref.shape[1] // EXPERTS
    hn2, cot = hn2_ref[...], cot_ref[...]
    router = exact(rows_ref, ROUTER, ROUTER + 8)
    lane = lax.broadcasted_iota(jnp.int32, (count, 8), 1)
    logits = jnp.where(lane < EXPERTS, mm(hn2, router, NT), NEG)
    e = jnp.exp(logits - jnp.max(logits, axis=-1, keepdims=True))
    probs = e / jnp.sum(e, axis=-1, keepdims=True)
    tile = ids[2 + shard] * nimg
    keep = jnp.concatenate([keep_ref[tile + i] for i in range(nimg)], axis=0)
    on = jnp.logical_or(lane == keep[:, 0:1], lane == keep[:, 1:2])
    gates = jnp.where(on, probs, 0.0).astype(BF)
    gates_f = gates.astype(F4)
    dp = jnp.zeros((count, 8), F4)
    if own:
        dbias = exact(rows_ref, DBIAS, DBIAS + 8)
        dp = mm(cot, dbias, NT)

    def pair(i, dp):
        for e in (2 * i, 2 * i + 1):
            cols = pl.ds(pl.multiple_of(e * ff, ff), ff)
            mine = lane == e
            gate = jnp.sum(jnp.where(mine, gates_f, 0.0), axis=-1, keepdims=True)
            u = mm(hn2, up_ref[:, cols]) + rows_ref[pl.ds(UBIAS + e, 1), 0:ff]
            phi, bell = normal_parts(u)
            h = u * phi
            slope = phi + u * (bell * 0.3989422804014327)
            r = mm(cot, dn_ref[:, cols])
            dp = dp + jnp.where(mine, jnp.sum(h * r, axis=-1, keepdims=True), 0.0)
            hg_ref[:, cols] = (h * gate).astype(BF)
            dhp_ref[:, cols] = (r * slope * gate).astype(BF)
        return dp

    dp = lax.fori_loop(0, EXPERTS // 2, pair, dp)
    dp = jnp.where(on, dp, 0.0)
    dl = (probs * (dp - jnp.sum(probs * dp, axis=-1, keepdims=True))).astype(BF)
    d_ref[...] = (mm(dhp_ref[...], up_ref[...], NT) + mm(dl, router)).astype(BF)
    m = mm(hg_ref[...], dn_ref[...], NT)
    sm_ref[0:8, :] = mm(dl, hn2, TN)
    if own:
        m = m + mm(gates, dbias)
        sm_ref[8:16, :] = mm(gates, cot, TN)
    else:
        sm_ref[8:16, :] = jnp.zeros((8, sm_ref.shape[1]), F4)
    m_ref[...] = m.astype(BF)


def expert_shard(ids, keep, hn2, cot, rows, up, dn, nimg, shard):
    count, width = hn2.shape
    wide = jax.ShapeDtypeStruct((count, up.shape[1]), BF)
    low = jax.ShapeDtypeStruct((count, width), BF)
    return pl.pallas_call(
        partial(expert_kernel, nimg, shard),
        out_shape=[low, low, wide, wide, jax.ShapeDtypeStruct((16, width), F4)],
        in_specs=[SM] + [VM] * 6,
        out_specs=[VM] * 5,
        compiler_params=params(),
        cost_estimate=cost(7),
        name="expert_shard",
    )(ids, keep, hn2, cot, rows, up, dn)


def expert_grad_kernel(nt, gmasks, ids, *refs):
    hn2s, cots, hgs, dhps = (refs[i * nt : (i + 1) * nt] for i in range(4))
    gub_ref = refs[4 * nt]
    grads = refs[4 * nt + 1 : 4 * nt + 1 + len(gmasks)]
    res_ref = refs[4 * nt + 1 + len(gmasks)]
    me = ids[0]
    ff = gub_ref.shape[2]
    ones = jnp.ones((8, hn2s[0].shape[0]), BF)

    def expert(e, carry):
        cols = pl.ds(pl.multiple_of(e * ff, ff), ff)
        sums_ = [mm(ones, r[:, cols]) for r in dhps]
        gub_ref[e] = sum(sums_[1:], sums_[0])[0:1, :]
        for which in range(2):
            lefts, rights = ((hn2s, dhps), (cots, hgs))[which]
            left = jnp.concatenate([r[...] for r in lefts], axis=0)
            right = jnp.concatenate([r[:, cols] for r in rights], axis=0)
            res_ref[which] = mm(left, right, TN)
            for group, ref in zip(gmasks, grads):
                dr = ref.shape[3]
                for idx, mask in enumerate(group):
                    at = pl.ds(pl.multiple_of(jnp.bitwise_xor(me, mask) * dr, dr), dr)
                    ref[idx, which, e] = res_ref[which, at, :].astype(BF)
        return carry

    lax.fori_loop(0, EXPERTS, expert, 0)


def expert_grads(ids, hn2s, cots, hgs, dhps, gmasks, dr):
    nt = len(hn2s)
    width = hn2s[0].shape[1]
    ff = hgs[0].shape[1] // EXPERTS
    return pl.pallas_call(
        partial(expert_grad_kernel, nt, gmasks),
        out_shape=[jax.ShapeDtypeStruct((EXPERTS, 1, ff), F4)]
        + [jax.ShapeDtypeStruct((len(m), 2, EXPERTS, dr, ff), BF) for m in gmasks],
        in_specs=[SM] + [VM] * (4 * nt),
        out_specs=[VM] * (1 + len(gmasks)),
        scratch_shapes=[pltpu.VMEM((2, width, ff), F4)],
        compiler_params=params(16),
        cost_estimate=cost(9),
        name="expert_grads",
    )(ids, *hn2s, *cots, *hgs, *dhps)


def attn_backward_kernel(nimg, nsm, ngub, gmasks, direct, ids, *refs):
    ins = 12 + ngub + nsm
    recv_ref, own_ref, x_ref, cot_ref = refs[:4]
    rows_ref, w_ref = refs[10:12]
    gubs, sms = refs[12 : 12 + ngub], refs[12 + ngub : ins]
    gtok_ref = refs[ins]
    ngrads = len(gmasks)
    grads = refs[ins + 1 : ins + 1 + ngrads]
    small_ref, do_ref, dq_ref, dk_ref, dv_ref, da_ref, hn1_ref, res_ref = refs[
        ins + 1 + ngrads : ins + 9 + ngrads
    ]
    held = refs[ins + 9 + ngrads :]
    x1_ref, q_ref, k_ref, v_ref, o_ref, pb_ref, sems = held
    copies = [
        pltpu.make_async_copy(a, b, sems.at[n]) for n, (a, b) in enumerate(zip(refs[4:10], held))
    ]
    for c in copies:
        c.start()
    width = x_ref.shape[1]
    dh = recv_ref[...].astype(F4) + own_ref[...].astype(F4)
    cot_f = cot_ref[...].astype(F4)
    copies[0].wait()
    n2, inv2 = moments(x1_ref[...], EPS)
    small_ref[...] = jnp.zeros(small_ref.shape, F4)
    small_ref[1:2, :] = jnp.sum(dh * n2, axis=0, keepdims=True)
    small_ref[3:4, :] = jnp.sum(dh, axis=0, keepdims=True)
    dx1 = cot_f + norm_back(dh * rows_ref[1:2, :], n2, inv2)
    da = dx1.astype(BF)
    da_ref[...] = da
    gtok_ref[...] = dx1
    small_ref[4:5, :] = jnp.sum(da.astype(F4), axis=0, keepdims=True)
    do_ref[...] = mm(da, w_ref[3]).astype(BF)
    lane = lax.broadcasted_iota(jnp.int32, (PAD, LANES), 1)
    scale = HD ** (-0.5)
    for c in copies[1:]:
        c.wait()

    def pairs(at_pair, carry):
        for n in (2 * at_pair, 2 * at_pair + 1):
            cols = pl.ds(pl.multiple_of(n * LANES, LANES), LANES)
            for img in range(nimg):
                at = slice(img * PAD, (img + 1) * PAD)
                qp, kp, vp, dop = q_ref[at, cols], k_ref[at, cols], v_ref[at, cols], do_ref[at, cols]
                zero = jnp.zeros_like(qp)
                dq = jnp.zeros((PAD, LANES), F4)
                dk = jnp.zeros((PAD, LANES), F4)
                dv = jnp.zeros((PAD, LANES), F4)
                for half in range(2):
                    mine = (lane < HD) if half == 0 else (lane >= HD)
                    pb = pb_ref[img * (width // HD) + 2 * n + half]
                    dom = jnp.where(mine, dop, zero)
                    dpb = mm(dom, vp, NT)
                    p = pb.astype(F4)
                    ds = (p * (dpb - jnp.sum(p * dpb, axis=-1, keepdims=True))).astype(BF)
                    dv = dv + mm(pb, dom, TN)
                    dq = dq + mm(ds, jnp.where(mine, kp, zero))
                    dk = dk + mm(ds, jnp.where(mine, qp, zero), TN)
                dq_ref[at, cols] = (dq * scale).astype(BF)
                dk_ref[at, cols] = (dk * scale).astype(BF)
                dv_ref[at, cols] = dv.astype(BF)
        return carry

    lax.fori_loop(0, width // LANES // 2, pairs, 0)
    small_ref[QVB : QVB + 1, :] = jnp.sum(dq_ref[...].astype(F4), axis=0, keepdims=True)
    small_ref[QVB + 1 : QVB + 2, :] = jnp.sum(dv_ref[...].astype(F4), axis=0, keepdims=True)
    dh1 = (
        mm(dq_ref[...], w_ref[0], NT)
        + mm(dk_ref[...], w_ref[1], NT)
        + mm(dv_ref[...], w_ref[2], NT)
    )
    n1, inv1 = moments(x_ref[...].astype(F4), EPS)
    hn1_ref[...] = (n1 * rows_ref[0:1, :] + rows_ref[2:3, :]).astype(BF)
    small_ref[0:1, :] = jnp.sum(dh1 * n1, axis=0, keepdims=True)
    small_ref[2:3, :] = jnp.sum(dh1, axis=0, keepdims=True)
    gtok_ref[...] = gtok_ref[...] + norm_back(dh1 * rows_ref[0:1, :], n1, inv1)
    total = sms[0][...]
    for ref in sms[1:]:
        total = total + ref[...]
    small_ref[ROUTER : ROUTER + 16, :] = total
    for e in range(EXPERTS):
        ref, at = gubs[e * ngub // EXPERTS], e % (EXPERTS // ngub)
        small_ref[UBIAS + e : UBIAS + e + 1, 0 : ref.shape[2]] = ref[at]
    me, met = ids[0], ids[1]
    for s in range(4):
        left, right = [(hn1_ref, dq_ref), (hn1_ref, dk_ref), (hn1_ref, dv_ref), (da_ref, o_ref)][s]
        res_ref[...] = mm(left[...], right[...], TN)
        for group, ref in zip(gmasks, grads):
            dr = (ref.shape[2] - (SMALL if direct else 0)) // 4
            for idx, mask in enumerate(group):
                i = jnp.bitwise_xor(me, mask)
                for jm in range(ref.shape[1]):
                    j = jnp.bitwise_xor(met, jm)
                    ref[idx, jm, s * dr : (s + 1) * dr, :] = res_ref[
                        pl.ds(pl.multiple_of(i * dr, dr), dr),
                        pl.ds(pl.multiple_of(j * LANES, LANES), LANES),
                    ].astype(BF)
    if not direct:
        return
    lane = lax.broadcasted_iota(jnp.int32, (SMALL, LANES), 1)
    row = lax.broadcasted_iota(jnp.int32, (SMALL, LANES), 0)
    nd = sum(len(g) for g in gmasks)
    qr = LANES // nd
    blank = jnp.zeros((3, LANES), F4)
    for group, ref in zip(gmasks, grads):
        for idx, mask in enumerate(group):
            i = jnp.bitwise_xor(me, mask)
            odd = jnp.bitwise_and(i, 1) == 1
            tile = pl.ds(pl.multiple_of(jnp.right_shift(i, 1) * LANES, LANES), LANES)
            t = jnp.concatenate(
                [small_ref[0:5, tile], small_ref[ROUTER : ROUTER + 4, tile], small_ref[DBIAS : DBIAS + 4, tile], blank],
                axis=0,
            )
            lo = jnp.where(odd, pltpu.roll(t, HALF, 1), t)
            lo = jnp.where(lane < HALF, lo, 0.0)
            b = jnp.concatenate([small_ref[UBIAS : UBIAS + 8, tile], jnp.zeros((8, LANES), F4)], axis=0)
            hi = jnp.where(odd, b, pltpu.roll(b, HALF, 1))
            hi = jnp.where(jnp.logical_and(lane >= HALF, row < EXPERTS), hi, 0.0)
            for jm in range(ref.shape[1]):
                j = jnp.bitwise_xor(met, jm)
                g = small_ref[0:8, pl.ds(pl.multiple_of(j * LANES, LANES), LANES)]
                g = pltpu.roll(g, 7, 0)
                g = pltpu.roll(g, jnp.bitwise_and(HALF - i * qr + LANES, LANES - 1), 1)
                g = jnp.concatenate([g, jnp.zeros((8, LANES), F4)], axis=0)
                mine = jnp.logical_and(lane >= HALF, lane < HALF + qr)
                mine = jnp.logical_and(mine, jnp.logical_and(row >= 4, row < 6))
                block = lo + jnp.where(mine, g, 0.0)
                if jm == 0:
                    block = block + hi
                ref[idx, jm, 4 * dr :, :] = block.astype(BF)


def attn_backward(ids, recv, own, x, cot, saved, rows, full, gubs, sms, gmasks, direct, nt, dr):
    count, width = x.shape
    nimg = count // PAD
    extra = SMALL if direct else 0
    shapes = [jax.ShapeDtypeStruct((count, width), F4)]
    shapes += [jax.ShapeDtypeStruct((len(m), nt, 4 * dr + extra, LANES), BF) for m in gmasks]
    shapes += [jax.ShapeDtypeStruct((NROWS, width), F4)]
    low = pltpu.VMEM((count, width), BF)
    return pl.pallas_call(
        partial(attn_backward_kernel, nimg, len(sms), len(gubs), gmasks, direct),
        out_shape=shapes,
        in_specs=[SM] + [VM] * 4 + [ANY] * 6 + [VM] * (2 + len(gubs) + len(sms)),
        out_specs=[VM] * len(shapes),
        scratch_shapes=[low] * 6
        + [pltpu.VMEM((width, width), F4)]
        + [pltpu.VMEM(v.shape, v.dtype) for v in saved]
        + [pltpu.SemaphoreType.DMA((6,))],
        compiler_params=params(16),
        cost_estimate=cost(16),
        name="attn_backward",
    )(ids, recv, own, x, cot, *in_hbm(saved), rows, full, *gubs, *sms)


def per_device(
    nd,
    nt,
    tokens,
    cotangent,
    routes,
    slots,
    norm_gains,
    norm_biases,
    w_qkv,
    qv_bias,
    w_out,
    out_bias,
    w_router,
    w_up,
    up_bias,
    w_down,
    down_bias,
):
    me = lax.axis_index("dp").astype(jnp.int32)
    met = lax.axis_index("tensor").astype(jnp.int32)
    width = tokens.shape[1]
    dr = w_qkv.shape[1]
    fr, qr = up_bias.shape[1], qv_bias.shape[1]
    ff = w_up.shape[2]
    nimg = IMG_DEV // nt
    direct = nd == 8 and nt == 4 and dr == HALF and fr == HALF and nd * qr == LANES
    src = jnp.asarray(ring_sources(nt), jnp.int32)[met]
    ids = jnp.concatenate([jnp.stack([me if direct else jnp.zeros_like(me), met]), src])
    even, odd = list(range(0, nd, 2)), list(range(1, nd, 2))

    def canonical(parts):
        if direct:
            return parts
        masks = sum((m for m, _ in parts), ())
        arr = jnp.concatenate([a for _, a in parts], axis=0)
        place = [masks.index(k) for k in range(nd)]
        order = jnp.asarray(place, jnp.int32)[jnp.bitwise_xor(jnp.arange(nd), me)]
        arr = jnp.take(arr, order, axis=0)
        lead = arr.ndim - 2
        arr = jnp.moveaxis(arr, 0, lead - 1)
        arr = arr.reshape(arr.shape[: lead - 1] + (nd * dr,) + arr.shape[-1:])
        return [((0,), arr[None])]

    gmasks = [even, odd] if direct else [[0]]

    def halves(grads, lead, rows):
        if direct:
            return grads
        whole = grads[0][0]
        shape = whole.shape[:lead] + (rows, nd, dr) + whole.shape[-1:]
        whole = jnp.moveaxis(whole.reshape(shape), lead + 1, 0)
        whole = whole.reshape((nd,) + grads[0].shape[1 : lead + 1] + (rows * dr, whole.shape[-1]))
        return [
            jnp.take(whole, jnp.bitwise_xor(jnp.asarray(m, jnp.int32), me), axis=0)
            for m in (even, odd)
        ]

    def images(v):
        return jnp.concatenate(
            [jnp.pad(v[i * SEQ : (i + 1) * SEQ], ((0, PAD - SEQ), (0, 0))) for i in range(nimg)]
        )

    chunk = jnp.concatenate([w_qkv, w_out.T[None]], axis=0)
    if direct:
        wide = [
            jnp.concatenate(
                [norm_gains, norm_biases, out_bias[None], w_router.T, down_bias, jnp.zeros((3, dr), BF)],
                axis=0,
            ),
            jnp.concatenate(
                [up_bias, jnp.pad(qv_bias, ((0, 0), (0, dr - qr))), jnp.zeros((10, dr), BF)], axis=0
            ),
        ]
        chunk = jnp.concatenate([chunk.reshape(4 * dr, LANES), jnp.concatenate(wide, axis=1)], axis=0)
    keep = jnp.where(slots >= 0, routes, -1).reshape(nt * nimg, SEQ, 2)
    keep = jnp.pad(keep, ((0, 0), (0, PAD - SEQ), (0, 0)), constant_values=-1)
    x = images(tokens)
    w_dn = w_down.transpose(0, 2, 1)
    def ring_all(v):
        out = [v]
        for s in range(1, nt):
            out.append(ring_step(out[-1], nt, False))
        return out

    cot = images(cotangent)
    chunk_z = [chunk] + [xor_send(chunk, "tensor", nt, m) for m in range(1, nt)]
    if direct:
        chunk_z = jnp.stack(chunk_z)
        cots = ring_all(after(cot, chunk_z))
        near = plane_first(chunk_z)
        quad = plane_stack(*near, lax.optimization_barrier((plane_far(*near), cots[1]))[0])
        layers = plane_first(after(jnp.concatenate([w_up, w_dn]), quad))
        full, rows = assemble(ids, gather_cores(after(quad, x, keep, ids)), width)
    else:
        cots = ring_all(cot)
        up, dn = (
            canonical(gather_dp(w[None], nd))[0][1][0, 0].transpose(1, 0, 2).reshape(width, EXPERTS * ff)
            for w in (w_up, w_dn)
        )
        full = canonical(gather_dp(jnp.stack(chunk_z), nd))[0][1][0]
        at = jnp.bitwise_xor(jnp.arange(nt), met)
        full = jnp.take(full, at, axis=0).transpose(1, 2, 0, 3).reshape(4, width, width)

        def whole(v):
            return lax.all_gather(v, "dp", axis=v.ndim - 1, tiled=True).astype(F4)

        qvb = lax.all_gather(whole(qv_bias), "tensor", axis=1, tiled=True)
        four = jnp.zeros((4, width), F4)
        rows = [whole(norm_gains), whole(norm_biases), whole(out_bias[None]), qvb]
        rows += [jnp.zeros((1, width), F4), whole(w_router.T), four, whole(down_bias), four]
        rows += [jnp.pad(whole(up_bias), ((0, 0), (0, width - nd * fr))), four]
        rows = jnp.concatenate(rows, axis=0)

    saved = attn_forward(x, rows, full, nimg)
    hn2s = [saved[0]]
    def shard(s, *first):
        hn2 = after(hn2s[s], *first)
        return expert_shard(ids, keep, hn2, cots[s], rows, up, dn, nimg, s)

    for s in range(1, nt):
        hn2s.append(ring_step(after(hn2s[-1], *(cots[2:] if s == nt - 1 else [])), nt, False))
    if direct:
        layers = lax.optimization_barrier((layers, hn2s[0]))[0]
        far = lax.optimization_barrier((plane_far(*layers), hn2s[1], cots[2]))[0]
        layers = plane_stack(*layers, far)
        up, dn = gather_experts(ids, gather_cores(layers), width)
    shards = [None, shard(1)] + [None] * (nt - 2)
    total = past = shards[1][1]
    for s in range(2, nt):
        if s == nt - 1:
            shards[0] = shard(0, past)
            shards[s] = shard(s, shards[0][1])
        else:
            shards[s] = shard(s, shards[s - 1][1])
        total = ring_step(total, nt, False)
        past = total
        total = sums([[[(total, None), (shards[s][1], None)]]])[0]
        past = total if s < nt - 1 else past
    total = ring_step(total, nt, False)
    recv = total

    gubs, *egrads = expert_grads(
        ids,
        [hn2s[0], after(hn2s[1], past), *hn2s[2:]],
        cots,
        [r[2] for r in shards],
        [r[3] for r in shards],
        gmasks,
        dr if direct else width,
    )
    ms = [r[0] for r in shards]
    if direct:
        other = to(after(egrads[1], recv), 1)
    m_sum = ring_step(after(ms[1], recv), nt, False)

    res = attn_backward(
        ids,
        recv,
        shards[0][1],
        x,
        cots[0],
        saved[1:],
        rows,
        full,
        [gubs],
        [r[4] for r in shards],
        gmasks,
        direct,
        nt,
        dr if direct else width,
    )
    gtok, flat = res[0], res[-1]
    def rows_of(v):
        return jnp.concatenate([v[i * PAD : i * PAD + SEQ] for i in range(nimg)])

    grad_tokens = rows_of(gtok)
    if direct:
        other, m_sum, odd = lax.optimization_barrier((other, m_sum, res[2]))
        a_other = to(odd, 1)
        m_sum = ring_step(sums([[[(m_sum, None), (ms[2], None)]]])[0], nt, False)
        a_kept_x, a_kept_y, a_send_x, a_send_y = scatter_first(res[1], a_other)
        a_got = to(a_send_x, 2), to(a_send_y, 4)
        kept_x, kept_y, send_x, send_y = scatter_first(egrads[0], after(other, a_send_x))
        a_got = lax.optimization_barrier((a_got, send_x))[0]
        a_next_x, a_next_y, a_base_x, a_base_y = scatter_second(a_kept_x, a_kept_y, *a_got)
        a_far = to(a_next_x, 4), to(a_next_y, 2)
        send_x, send_y, m_sum = lax.optimization_barrier((send_x, send_y, m_sum, a_next_x))[:3]
        got = to(send_x, 2), to(send_y, 4)
        m_sum = ring_step(sums([[[(m_sum, None), (ms[3], None)]]])[0], nt, False)
        keep_z, send_z = sums([[[(v, None), (f, None)]] for v, f in zip((a_base_x, a_base_y), a_far)])
        got_z = xor_send(send_z, "tensor", nt, 2)
        got, got_z = lax.optimization_barrier((got, got_z))
        mine, next_z = sums([[[(keep_z, j), (got_z, j)]] for j in (0, 1)])
        next_x, next_y, base_x, base_y = scatter_second(kept_x, kept_y, *got)
        far = to(next_x, 4), to(next_y, 2)
        parts = [mine, xor_send(next_z, "tensor", nt, 1)]
        layer_out = rows_of(saved[1] + (m_sum.astype(F4) + ms[0].astype(F4)))
        parts = lax.optimization_barrier((parts, layer_out, grad_tokens))[0]
        g_qkv, g_out, g_gain, g_bias, g_outb, g_router, g_dbias, g_ub, g_qvb = finish(parts, dr, qr)
        g_up, g_down = add_all([base_x, far[0]])[0], add_all([base_y, far[1]])[0]
        g_outb, g_router = g_outb[0], g_router.T
    else:
        egrads = halves(egrads, 2, 1)
        g_up, g_down = add_all(scatter_dp(*egrads, nd))
        held = add_all(scatter_dp(*halves(res[1:-1], 1, 4), nd)).astype(BF)
        mine = add_all([held[0]] + [xor_send(held[m], "tensor", nt, m) for m in range(1, nt)])
        g_qkv, g_out = mine[: 3 * dr].reshape(3, dr, LANES), mine[3 * dr :]
        for s in range(2, nt):
            m_sum = ring_step(add_all([m_sum, ms[s]]).astype(BF), nt, False)
        layer_out = rows_of(saved[1] + (m_sum.astype(F4) + ms[0].astype(F4)))
        g_ub = lax.dynamic_slice(lax.psum(flat, "dp"), (UBIAS, me * fr), (EXPERTS, fr))
        flat = lax.psum(flat, ("dp", "tensor"))
        cut = lax.dynamic_slice(flat, (0, me * dr), (NROWS, dr))
        g_gain, g_bias, g_outb = cut[0:2], cut[2:4], cut[4]
        g_router, g_dbias = cut[ROUTER : ROUTER + 4].T, cut[DBIAS : DBIAS + 4]
        g_qvb = lax.dynamic_slice(flat, (QVB, (met * nd + me) * qr), (2, qr))

    return (
        layer_out,
        grad_tokens,
        g_gain,
        g_bias,
        g_qkv,
        g_qvb,
        g_out.T,
        g_outb,
        g_router,
        g_up,
        g_ub,
        g_down.transpose(0, 2, 1),
        g_dbias,
    )


def solution(mesh):
    nd, nt = mesh.shape["dp"], mesh.shape["tensor"]
    placed = (
        P(("dp", "tensor"), None),
        P(("dp", "tensor"), None),
        P("dp", None),
        P("dp", None),
        P(None, "dp"),
        P(None, "dp"),
        P(None, "dp", "tensor"),
        P(None, ("tensor", "dp")),
        P("tensor", "dp"),
        P("dp"),
        P("dp", None),
        P(None, "dp", "tensor"),
        P(None, ("tensor", "dp")),
        P(None, "tensor", "dp"),
        P(None, "dp"),
    )
    return jax.shard_map(
        partial(per_device, nd, nt),
        mesh=mesh,
        in_specs=placed,
        out_specs=(
            P(("dp", "tensor"), None),
            P(("dp", "tensor"), None),
            P(None, "dp"),
            P(None, "dp"),
            P(None, "dp", "tensor"),
            P(None, ("tensor", "dp")),
            P("tensor", "dp"),
            P("dp"),
            P("dp", None),
            P(None, "dp", "tensor"),
            P(None, ("tensor", "dp")),
            P(None, "tensor", "dp"),
            P(None, "dp"),
        ),
        check_vma=False,
    )
```

```python
from functools import partial

import jax
import jax.numpy as jnp
import numpy as np
from jax import lax
from jax.experimental import pallas as pl
from jax.experimental.pallas import tpu as pltpu
from jax.sharding import PartitionSpec as P

HD = 64
EXPERTS = 4
SEQ = 197
IMG_DEV = 8
PAD = 200
SMALL = 16
EPS = 1e-06
BF = jnp.bfloat16
F4 = jnp.float32
NEG = -1e30
LANES = 128
HALF = 64

NN = (((1,), (0,)), ((), ()))
NT = (((1,), (1,)), ((), ()))
TN = (((0,), (0,)), ((), ()))

VM = pl.BlockSpec()
SM = pl.BlockSpec(memory_space=pltpu.SMEM)
ANY = pl.BlockSpec(memory_space=pltpu.HBM)


def mm(a, b, dims=NN):
    return lax.dot_general(a, b, dims, preferred_element_type=F4)


def params(mib=12):
    return pltpu.CompilerParams(vmem_limit_bytes=mib * 1024 * 1024)


def cost(us):
    return pl.CostEstimate(flops=0, transcendentals=0, bytes_accessed=int(us * 3.3e4))


def xor_send(x, axis, n, mask):
    return lax.ppermute(x, axis, [(i, i ^ mask) for i in range(n)])


def ring_order(n):
    return [0] + list(range(1, n, 2)) + list(range(2, n, 2))[::-1]


def ring_step(x, n, back):
    ring = ring_order(n)
    pairs = [(ring[p], ring[(p + (-1 if back else 1)) % n]) for p in range(n)]
    return lax.ppermute(x, "tensor", pairs)


def ring_sources(n):
    ring = ring_order(n)
    pos = {r: p for p, r in enumerate(ring)}
    return [[ring[(pos[r] - s) % n] for s in range(n)] for r in range(n)]


def stages_of(n):
    if n <= 8:
        inter = list(range(2, n, 2))
        return ([[1]] if n > 1 else []) + ([inter] if inter else [])
    out, bit = [], 1
    while bit < n:
        out.append([bit])
        bit *= 2
    return out


def gather_dp(x, n):
    parts = [((0,), x[None])]
    for stage in reversed(stages_of(n)):
        new = []
        for mask in stage:
            for masks, arr in parts:
                new.append((tuple(k ^ mask for k in masks), xor_send(arr, "dp", n, mask)))
        parts = parts + new
        if n > 8 and stage != [1]:
            parts = [
                (sum((m for m, _ in parts), ()), jnp.concatenate([a for _, a in parts], axis=0))
            ]
    return parts


def scatter_dp(even, odd, n):
    got = xor_send(odd, "dp", n, 1)
    masks = list(range(0, n, 2))
    own = {k: even[i] for i, k in enumerate(masks)}
    new = {k: got[i] for i, k in enumerate(masks)}
    own = {k: (own[k].astype(F4) + new[k].astype(F4)).astype(BF) for k in masks}
    stages = stages_of(n)[1:]
    for at, stage in enumerate(stages):
        span = 0
        for m in stage:
            span |= m
        rest = [k for k in masks if not k & span]
        recv = []
        for m in stage:
            pack = [own[k ^ m] for k in rest]
            send = pack[0] if len(pack) == 1 else jnp.stack(pack)
            back = xor_send(send, "dp", n, m)
            recv.append([back] if len(pack) == 1 else [back[i] for i in range(len(pack))])
        masks = rest
        if at == len(stages) - 1:
            return [own[0]] + [r[0] for r in recv]
        own = {
            k: sum((r[i].astype(F4) for r in recv), own[k].astype(F4)).astype(BF)
            for i, k in enumerate(rest)
        }
    return [own[0]]


CORE0, CORE1 = (0, 2, 4, 6), (1, 3, 5, 7)


def to(x, mask):
    return xor_send(x, "dp", 8, mask)


def plane_first(x):
    return x, to(x, 2), to(x, 4)


def plane_far(x, from_x, from_y):
    half = x.shape[0] // 2
    return to(from_x[:half], 4), to(from_y[half:], 2)


def plane_stack(x, from_x, from_y, far):
    return jnp.stack([x, from_x, from_y, jnp.concatenate(far, axis=0)])


def gather_cores(quad):
    return [(CORE0, quad), (CORE1, to(quad, 1))]


def scatter_first(even, got):
    half = even.shape[1] // 2
    low, high = slice(0, half), slice(half, 2 * half)

    def both(mask, part):
        return [(even, (mask // 2, part)), (got, (mask // 2, part))]

    return sums(
        [
            [both(0, low), both(4, low)],
            [both(0, high), both(2, high)],
            [both(2, low), both(6, low)],
            [both(4, high), both(6, high)],
        ]
    )


def scatter_second(keep_x, keep_y, got_x, got_y):
    pairs = [(keep_x, got_x), (keep_y, got_y)]
    return sums([[[(k, at), (g, at)]] for at in (1, 0) for k, g in pairs])


def after(x, *first):
    return lax.optimization_barrier((x, *first))[0]


def arrays(parts):
    return [a for _, a in parts]


def sums_kernel(outs, count, *refs):
    for groups, out in zip(outs, refs[count:]):
        for j, group in enumerate(groups):
            total = None
            for n, at in group:
                term = (refs[n][...] if at is None else refs[n][at]).astype(F4)
                total = term if total is None else total + term
            if len(groups) == 1:
                out[...] = total.astype(out.dtype)
            else:
                out[j] = total.astype(out.dtype)


def sums(outs):
    known, flat, index, shapes = {}, [], [], []
    for groups in outs:
        index.append([])
        for group in groups:
            index[-1].append([])
            for v, at in group:
                if id(v) not in known:
                    known[id(v)] = len(flat)
                    flat.append(v)
                index[-1][-1].append((known[id(v)], at))
        v, at = groups[0][0]
        shape = v.shape if at is None else np.broadcast_to(0, v.shape)[at].shape
        shapes.append(shape if len(groups) == 1 else (len(groups),) + shape)
    return pl.pallas_call(
        partial(sums_kernel, index, len(flat)),
        out_shape=[jax.ShapeDtypeStruct(v, BF) for v in shapes],
        in_specs=[VM] * len(flat),
        out_specs=[VM] * len(shapes),
        compiler_params=params(16),
        cost_estimate=cost(1),
        name="sums",
    )(*flat)


def finish_kernel(dr, qr, *refs):
    parts, outs = refs[:2], refs[2:]
    g_qkv, g_out, g_gain, g_bias, g_outb, g_router, g_dbias, g_ub, g_qvb = outs
    total = parts[0][...].astype(F4)
    for ref in parts[1:]:
        total = total + ref[...].astype(F4)
    for s in range(3):
        g_qkv[s] = total[s * dr : (s + 1) * dr]
    g_out[...] = total[3 * dr : 4 * dr]
    low = total[4 * dr :]
    high = pltpu.roll(low, HALF, 1)
    g_gain[...] = low[0:2, :HALF]
    g_bias[...] = low[2:4, :HALF]
    g_outb[...] = low[4:5, :HALF]
    g_router[...] = low[5:9, :HALF]
    g_dbias[...] = low[9:13, :HALF]
    g_ub[...] = high[0:4, :HALF]
    g_qvb[...] = high[4:6, :qr]


def finish(parts, dr, qr):
    rows = [(2, HALF), (2, HALF), (1, HALF), (EXPERTS, HALF), (EXPERTS, HALF), (EXPERTS, HALF), (2, qr)]
    shapes = [(3, dr, LANES), (dr, LANES)] + rows
    return pl.pallas_call(
        partial(finish_kernel, dr, qr),
        out_shape=[jax.ShapeDtypeStruct(v, F4) for v in shapes],
        in_specs=[VM] * 2,
        out_specs=[VM] * len(shapes),
        compiler_params=params(),
        cost_estimate=cost(1),
        name="finish",
    )(*parts)


def add_all(parts):
    return sum((p.astype(F4) for p in parts[1:]), parts[0].astype(F4))


def moments(v, eps_rows):
    center = v - jnp.mean(v, axis=-1, keepdims=True)
    inv = lax.rsqrt(jnp.mean(center * center, axis=-1, keepdims=True) + eps_rows)
    return center * inv, inv


def norm_back(z, normed, inv):
    return inv * (
        z
        - jnp.mean(z, axis=-1, keepdims=True)
        - normed * jnp.mean(z * normed, axis=-1, keepdims=True)
    )


def exact(ref, lo, hi):
    return ref[lo:hi, :].astype(BF)


GAIN, BIAS, OUTB, QVB, ROUTER, DBIAS, UBIAS, NROWS = 0, 2, 4, 5, 8, 16, 24, 32


def in_hbm(values):
    return [pltpu.with_memory_space_constraint(v, pltpu.HBM) for v in values]


def run_copies(pairs, sems):
    copies = [pltpu.make_async_copy(a, b, sems.at[n]) for n, (a, b) in enumerate(pairs)]
    for c in copies:
        c.start()
    for c in copies:
        c.wait()


def assemble_kernel(masks, ids, *refs):
    pieces, (w_ref, rows_ref, small_ref, sems) = refs[:-4], refs[-4:]
    me, met = ids[0], ids[1]
    pairs = []
    for group, ref in zip(masks, pieces):
        dr = (ref.shape[2] - SMALL) // 4
        for idx, mask in enumerate(group):
            i = jnp.bitwise_xor(me, mask)
            for jm in range(ref.shape[1]):
                j = jnp.bitwise_xor(met, jm)
                rows_at = pl.ds(pl.multiple_of(i * dr, dr), dr)
                lanes_at = pl.ds(pl.multiple_of(j * LANES, LANES), LANES)
                whole = ref.at[idx, jm, 0 : 4 * dr].reshape(4, dr, LANES)
                pairs.append((whole, w_ref.at[:, rows_at, lanes_at]))
                pairs.append((ref.at[idx, jm, 4 * dr : 4 * dr + SMALL], small_ref.at[mask, jm]))
    run_copies(pairs, sems)
    rows_ref[...] = jnp.zeros(rows_ref.shape, F4)
    lane = lax.broadcasted_iota(jnp.int32, (SMALL, LANES), 1)
    low = lane < HALF
    odd = jnp.bitwise_and(me, 1) == 1
    nd, nt = small_ref.shape[:2]

    def small(mask, jm):
        return small_ref[mask, jm].astype(F4)

    for mask in range(0, nd, 2):
        a, b = small(mask, 0), small(mask + 1, 0)
        first, second = jnp.where(odd, b, a), jnp.where(odd, a, b)
        lo = jnp.where(low, first, pltpu.roll(second, HALF, 1))
        hi = jnp.where(low, pltpu.roll(first, HALF, 1), second)
        tile = jnp.right_shift(jnp.bitwise_xor(me, mask), 1)
        at = pl.ds(pl.multiple_of(tile * LANES, LANES), LANES)
        rows_ref[0:5, at] = lo[0:5]
        rows_ref[ROUTER : ROUTER + EXPERTS, at] = lo[5:9]
        rows_ref[DBIAS : DBIAS + EXPERTS, at] = lo[9:13]
        rows_ref[UBIAS : UBIAS + EXPERTS, at] = hi[0:4]
    qr = LANES // nd
    mine = jnp.logical_and(lane >= HALF, lane < HALF + qr)
    for jm in range(nt):
        j = jnp.bitwise_xor(met, jm)
        total = jnp.zeros((SMALL, LANES), F4)
        for mask in range(nd):
            i = jnp.bitwise_xor(me, mask)
            part = jnp.where(mine, small(mask, jm), 0.0)
            total = total + pltpu.roll(part, jnp.bitwise_and(HALF + i * qr, LANES - 1), 1)
        rows_ref[QVB : QVB + 2, pl.ds(pl.multiple_of(j * LANES, LANES), LANES)] = total[4:6]


def assemble(ids, weights, width):
    masks = [m for m, _ in weights]
    pieces = arrays(weights)
    nd, nt = sum(len(m) for m in masks), pieces[0].shape[1]
    return pl.pallas_call(
        partial(assemble_kernel, masks),
        out_shape=[
            jax.ShapeDtypeStruct((4, width, width), BF),
            jax.ShapeDtypeStruct((NROWS, width), F4),
        ],
        in_specs=[SM] + [ANY] * len(pieces),
        out_specs=[VM, VM],
        scratch_shapes=[
            pltpu.VMEM((nd, nt, SMALL, LANES), BF),
            pltpu.SemaphoreType.DMA((2 * nd * nt,)),
        ],
        compiler_params=params(8),
        cost_estimate=cost(2),
        name="assemble",
    )(ids, *pieces)


def attn_forward_kernel(
    nimg, x_ref, rows_ref, w_ref, hn2_ref, x1_out, q_out, k_out, v_out, o_out, pb_out, *scratch
):
    x1_ref, q_ref, k_ref, v_ref, o_ref, pb_ref, sems = scratch
    heads = w_ref.shape[1] // HD
    copies = []

    def leave(src, dst):
        copies.append(pltpu.make_async_copy(src, dst, sems.at[len(copies)]))
        copies[-1].start()

    width = x_ref.shape[1]
    x = x_ref[...].astype(F4)
    n1, _ = moments(x, EPS)
    hn1 = (n1 * rows_ref[0:1, :] + rows_ref[2:3, :]).astype(BF)
    q_ref[...] = (mm(hn1, w_ref[0]) + rows_ref[5:6, :]).astype(BF)
    k_ref[...] = mm(hn1, w_ref[1]).astype(BF)
    v_ref[...] = (mm(hn1, w_ref[2]) + rows_ref[6:7, :]).astype(BF)
    leave(q_ref, q_out)
    leave(k_ref, k_out)
    leave(v_ref, v_out)
    lane = lax.broadcasted_iota(jnp.int32, (PAD, LANES), 1)
    col = lax.broadcasted_iota(jnp.int32, (PAD, PAD), 1)
    for img in range(nimg):
        at = slice(img * PAD, (img + 1) * PAD)
        for pair in range(width // LANES):
            cols = slice(pair * LANES, (pair + 1) * LANES)
            qp, kp, vp = q_ref[at, cols], k_ref[at, cols], v_ref[at, cols]
            acc = jnp.zeros((PAD, LANES), F4)
            for half in range(2):
                mine = (lane < HD) if half == 0 else (lane >= HD)
                qm = jnp.where(mine, qp * jnp.asarray(HD ** (-0.5), BF), jnp.zeros_like(qp))
                s = mm(qm, kp, NT)
                s = jnp.where(col < SEQ, s, NEG)
                e = jnp.exp(s - jnp.max(s, axis=-1, keepdims=True))
                p = (e * (1.0 / jnp.sum(e, axis=-1, keepdims=True))).astype(BF)
                pb_ref[img * heads + 2 * pair + half] = p
                acc = acc + mm(p, jnp.where(mine, vp, jnp.zeros_like(vp)))
            o_ref[at, cols] = acc.astype(BF)
        mine = pl.ds(img * heads, heads)
        leave(pb_ref.at[mine], pb_out.at[mine])
    leave(o_ref, o_out)
    x1 = x + (mm(o_ref[...], w_ref[3], NT) + rows_ref[4:5, :])
    x1_ref[...] = x1
    leave(x1_ref, x1_out)
    n2, _ = moments(x1, EPS)
    hn2_ref[...] = (n2 * rows_ref[1:2, :] + rows_ref[3:4, :]).astype(BF)
    for c in copies:
        c.wait()


def attn_forward(x, rows, full, nimg):
    count, width = x.shape
    heads = width // HD
    saved = [((count, width), F4)] + [((count, width), BF)] * 4
    saved.append(((nimg * heads, PAD, PAD), BF))
    shapes = [jax.ShapeDtypeStruct((count, width), BF)] + [pltpu.HBM(*v) for v in saved]
    return pl.pallas_call(
        partial(attn_forward_kernel, nimg),
        out_shape=shapes,
        in_specs=[VM] * 3,
        out_specs=[VM] + [ANY] * len(saved),
        scratch_shapes=[pltpu.VMEM(*v) for v in saved] + [pltpu.SemaphoreType.DMA((5 + nimg,))],
        compiler_params=params(),
        cost_estimate=cost(9),
        name="attn_forward",
    )(x, rows, full)


def gather_experts_kernel(masks, ids, *refs):
    pieces, (up_ref, dn_ref, sems) = refs[:-3], refs[-3:]
    me = ids[0]
    pairs = []
    for group, ref in zip(masks, pieces):
        dr, ff = ref.shape[2], ref.shape[3]
        for idx, mask in enumerate(group):
            at = pl.ds(pl.multiple_of(jnp.bitwise_xor(me, mask) * dr, dr), dr)
            for e in range(EXPERTS):
                cols = slice(e * ff, (e + 1) * ff)
                pairs.append((ref.at[idx, e], up_ref.at[at, cols]))
                pairs.append((ref.at[idx, EXPERTS + e], dn_ref.at[at, cols]))
    run_copies(pairs, sems)


def gather_experts(ids, weights, width):
    masks = [m for m, _ in weights]
    pieces = arrays(weights)
    nd = sum(len(m) for m in masks)
    whole = jax.ShapeDtypeStruct((width, EXPERTS * pieces[0].shape[3]), BF)
    return pl.pallas_call(
        partial(gather_experts_kernel, masks),
        out_shape=[whole, whole],
        in_specs=[SM] + [ANY] * len(pieces),
        out_specs=[VM, VM],
        scratch_shapes=[pltpu.SemaphoreType.DMA((2 * EXPERTS * nd,))],
        compiler_params=params(8),
        cost_estimate=cost(3),
        name="gather_experts",
    )(ids, *pieces)


def normal_parts(u):
    bell = jnp.exp(-0.5 * (u * u))
    t = 1.0 / (1.0 + (0.3275911 * 2.0 ** (-0.5)) * jnp.abs(u))
    poly = 0.5 * 1.061405429 * t + 0.5 * (-1.453152027)
    poly = poly * t + 0.5 * 1.421413741
    poly = poly * t + 0.5 * (-0.284496736)
    poly = poly * t + 0.5 * 0.254829592
    tail = poly * t * bell
    return jnp.where(u > 0.0, 1.0 - tail, tail), bell


def expert_kernel(
    nimg, shard, ids, keep_ref, hn2_ref, cot_ref, rows_ref, up_ref, dn_ref, m_ref, d_ref, hg_ref, dhp_ref, sm_ref
):
    own = shard == 0
    count = hn2_ref.shape[0]
    ff = hg_ref.shape[1] // EXPERTS
    hn2, cot = hn2_ref[...], cot_ref[...]
    router = exact(rows_ref, ROUTER, ROUTER + 8)
    lane = lax.broadcasted_iota(jnp.int32, (count, 8), 1)
    logits = jnp.where(lane < EXPERTS, mm(hn2, router, NT), NEG)
    e = jnp.exp(logits - jnp.max(logits, axis=-1, keepdims=True))
    probs = e / jnp.sum(e, axis=-1, keepdims=True)
    tile = ids[2 + shard] * nimg
    keep = jnp.concatenate([keep_ref[tile + i] for i in range(nimg)], axis=0)
    on = jnp.logical_or(lane == keep[:, 0:1], lane == keep[:, 1:2])
    gates = jnp.where(on, probs, 0.0).astype(BF)
    gates_f = gates.astype(F4)
    dp = jnp.zeros((count, 8), F4)
    if own:
        dbias = exact(rows_ref, DBIAS, DBIAS + 8)
        dp = mm(cot, dbias, NT)

    def pair(i, dp):
        for e in (2 * i, 2 * i + 1):
            cols = pl.ds(pl.multiple_of(e * ff, ff), ff)
            mine = lane == e
            gate = jnp.sum(jnp.where(mine, gates_f, 0.0), axis=-1, keepdims=True)
            u = mm(hn2, up_ref[:, cols]) + rows_ref[pl.ds(UBIAS + e, 1), 0:ff]
            phi, bell = normal_parts(u)
            h = u * phi
            slope = phi + u * (bell * 0.3989422804014327)
            r = mm(cot, dn_ref[:, cols])
            dp = dp + jnp.where(mine, jnp.sum(h * r, axis=-1, keepdims=True), 0.0)
            hg_ref[:, cols] = (h * gate).astype(BF)
            dhp_ref[:, cols] = (r * slope * gate).astype(BF)
        return dp

    dp = lax.fori_loop(0, EXPERTS // 2, pair, dp)
    dp = jnp.where(on, dp, 0.0)
    dl = (probs * (dp - jnp.sum(probs * dp, axis=-1, keepdims=True))).astype(BF)
    d_ref[...] = (mm(dhp_ref[...], up_ref[...], NT) + mm(dl, router)).astype(BF)
    m = mm(hg_ref[...], dn_ref[...], NT)
    sm_ref[0:8, :] = mm(dl, hn2, TN)
    if own:
        m = m + mm(gates, dbias)
        sm_ref[8:16, :] = mm(gates, cot, TN)
    else:
        sm_ref[8:16, :] = jnp.zeros((8, sm_ref.shape[1]), F4)
    m_ref[...] = m.astype(BF)


def expert_shard(ids, keep, hn2, cot, rows, up, dn, nimg, shard):
    count, width = hn2.shape
    wide = jax.ShapeDtypeStruct((count, up.shape[1]), BF)
    low = jax.ShapeDtypeStruct((count, width), BF)
    return pl.pallas_call(
        partial(expert_kernel, nimg, shard),
        out_shape=[low, low, wide, wide, jax.ShapeDtypeStruct((16, width), F4)],
        in_specs=[SM] + [VM] * 6,
        out_specs=[VM] * 5,
        compiler_params=params(),
        cost_estimate=cost(7),
        name="expert_shard",
    )(ids, keep, hn2, cot, rows, up, dn)


def expert_grad_kernel(nt, gmasks, ids, *refs):
    hn2s, cots, hgs, dhps = (refs[i * nt : (i + 1) * nt] for i in range(4))
    gub_ref = refs[4 * nt]
    grads = refs[4 * nt + 1 : 4 * nt + 1 + len(gmasks)]
    res_ref = refs[4 * nt + 1 + len(gmasks)]
    me = ids[0]
    ff = gub_ref.shape[2]
    ones = jnp.ones((8, hn2s[0].shape[0]), BF)

    def expert(e, carry):
        cols = pl.ds(pl.multiple_of(e * ff, ff), ff)
        sums_ = [mm(ones, r[:, cols]) for r in dhps]
        gub_ref[e] = sum(sums_[1:], sums_[0])[0:1, :]
        for which in range(2):
            lefts, rights = ((hn2s, dhps), (cots, hgs))[which]
            left = jnp.concatenate([r[...] for r in lefts], axis=0)
            right = jnp.concatenate([r[:, cols] for r in rights], axis=0)
            res_ref[which] = mm(left, right, TN)
            for group, ref in zip(gmasks, grads):
                dr = ref.shape[3]
                for idx, mask in enumerate(group):
                    at = pl.ds(pl.multiple_of(jnp.bitwise_xor(me, mask) * dr, dr), dr)
                    ref[idx, which, e] = res_ref[which, at, :].astype(BF)
        return carry

    lax.fori_loop(0, EXPERTS, expert, 0)


def expert_grads(ids, hn2s, cots, hgs, dhps, gmasks, dr):
    nt = len(hn2s)
    width = hn2s[0].shape[1]
    ff = hgs[0].shape[1] // EXPERTS
    return pl.pallas_call(
        partial(expert_grad_kernel, nt, gmasks),
        out_shape=[jax.ShapeDtypeStruct((EXPERTS, 1, ff), F4)]
        + [jax.ShapeDtypeStruct((len(m), 2, EXPERTS, dr, ff), BF) for m in gmasks],
        in_specs=[SM] + [VM] * (4 * nt),
        out_specs=[VM] * (1 + len(gmasks)),
        scratch_shapes=[pltpu.VMEM((2, width, ff), F4)],
        compiler_params=params(16),
        cost_estimate=cost(9),
        name="expert_grads",
    )(ids, *hn2s, *cots, *hgs, *dhps)


def attn_backward_kernel(nimg, nsm, ngub, gmasks, direct, ids, *refs):
    ins = 12 + ngub + nsm
    recv_ref, own_ref, x_ref, cot_ref = refs[:4]
    rows_ref, w_ref = refs[10:12]
    gubs, sms = refs[12 : 12 + ngub], refs[12 + ngub : ins]
    gtok_ref = refs[ins]
    ngrads = len(gmasks)
    grads = refs[ins + 1 : ins + 1 + ngrads]
    small_ref, do_ref, dq_ref, dk_ref, dv_ref, da_ref, hn1_ref, res_ref = refs[
        ins + 1 + ngrads : ins + 9 + ngrads
    ]
    held = refs[ins + 9 + ngrads :]
    x1_ref, q_ref, k_ref, v_ref, o_ref, pb_ref, sems = held
    copies = [
        pltpu.make_async_copy(a, b, sems.at[n]) for n, (a, b) in enumerate(zip(refs[4:10], held))
    ]
    for c in copies:
        c.start()
    width = x_ref.shape[1]
    dh = recv_ref[...].astype(F4) + own_ref[...].astype(F4)
    cot_f = cot_ref[...].astype(F4)
    copies[0].wait()
    n2, inv2 = moments(x1_ref[...], EPS)
    small_ref[...] = jnp.zeros(small_ref.shape, F4)
    small_ref[1:2, :] = jnp.sum(dh * n2, axis=0, keepdims=True)
    small_ref[3:4, :] = jnp.sum(dh, axis=0, keepdims=True)
    dx1 = cot_f + norm_back(dh * rows_ref[1:2, :], n2, inv2)
    da = dx1.astype(BF)
    da_ref[...] = da
    gtok_ref[...] = dx1
    small_ref[4:5, :] = jnp.sum(da.astype(F4), axis=0, keepdims=True)
    do_ref[...] = mm(da, w_ref[3]).astype(BF)
    lane = lax.broadcasted_iota(jnp.int32, (PAD, LANES), 1)
    scale = HD ** (-0.5)
    for c in copies[1:]:
        c.wait()

    def pairs(at_pair, carry):
        for n in (2 * at_pair, 2 * at_pair + 1):
            cols = pl.ds(pl.multiple_of(n * LANES, LANES), LANES)
            for img in range(nimg):
                at = slice(img * PAD, (img + 1) * PAD)
                qp, kp, vp, dop = q_ref[at, cols], k_ref[at, cols], v_ref[at, cols], do_ref[at, cols]
                zero = jnp.zeros_like(qp)
                dq = jnp.zeros((PAD, LANES), F4)
                dk = jnp.zeros((PAD, LANES), F4)
                dv = jnp.zeros((PAD, LANES), F4)
                for half in range(2):
                    mine = (lane < HD) if half == 0 else (lane >= HD)
                    pb = pb_ref[img * (width // HD) + 2 * n + half]
                    dom = jnp.where(mine, dop, zero)
                    dpb = mm(dom, vp, NT)
                    p = pb.astype(F4)
                    ds = (p * (dpb - jnp.sum(p * dpb, axis=-1, keepdims=True))).astype(BF)
                    dv = dv + mm(pb, dom, TN)
                    dq = dq + mm(ds, jnp.where(mine, kp, zero))
                    dk = dk + mm(ds, jnp.where(mine, qp, zero), TN)
                dq_ref[at, cols] = (dq * scale).astype(BF)
                dk_ref[at, cols] = (dk * scale).astype(BF)
                dv_ref[at, cols] = dv.astype(BF)
        return carry

    lax.fori_loop(0, width // LANES // 2, pairs, 0)
    small_ref[QVB : QVB + 1, :] = jnp.sum(dq_ref[...].astype(F4), axis=0, keepdims=True)
    small_ref[QVB + 1 : QVB + 2, :] = jnp.sum(dv_ref[...].astype(F4), axis=0, keepdims=True)
    dh1 = (
        mm(dq_ref[...], w_ref[0], NT)
        + mm(dk_ref[...], w_ref[1], NT)
        + mm(dv_ref[...], w_ref[2], NT)
    )
    n1, inv1 = moments(x_ref[...].astype(F4), EPS)
    hn1_ref[...] = (n1 * rows_ref[0:1, :] + rows_ref[2:3, :]).astype(BF)
    small_ref[0:1, :] = jnp.sum(dh1 * n1, axis=0, keepdims=True)
    small_ref[2:3, :] = jnp.sum(dh1, axis=0, keepdims=True)
    gtok_ref[...] = gtok_ref[...] + norm_back(dh1 * rows_ref[0:1, :], n1, inv1)
    total = sms[0][...]
    for ref in sms[1:]:
        total = total + ref[...]
    small_ref[ROUTER : ROUTER + 16, :] = total
    for e in range(EXPERTS):
        ref, at = gubs[e * ngub // EXPERTS], e % (EXPERTS // ngub)
        small_ref[UBIAS + e : UBIAS + e + 1, 0 : ref.shape[2]] = ref[at]
    me, met = ids[0], ids[1]
    for s in range(4):
        left, right = [(hn1_ref, dq_ref), (hn1_ref, dk_ref), (hn1_ref, dv_ref), (da_ref, o_ref)][s]
        res_ref[...] = mm(left[...], right[...], TN)
        for group, ref in zip(gmasks, grads):
            dr = (ref.shape[2] - (SMALL if direct else 0)) // 4
            for idx, mask in enumerate(group):
                i = jnp.bitwise_xor(me, mask)
                for jm in range(ref.shape[1]):
                    j = jnp.bitwise_xor(met, jm)
                    ref[idx, jm, s * dr : (s + 1) * dr, :] = res_ref[
                        pl.ds(pl.multiple_of(i * dr, dr), dr),
                        pl.ds(pl.multiple_of(j * LANES, LANES), LANES),
                    ].astype(BF)
    if not direct:
        return
    lane = lax.broadcasted_iota(jnp.int32, (SMALL, LANES), 1)
    row = lax.broadcasted_iota(jnp.int32, (SMALL, LANES), 0)
    nd = sum(len(g) for g in gmasks)
    qr = LANES // nd
    blank = jnp.zeros((3, LANES), F4)
    for group, ref in zip(gmasks, grads):
        for idx, mask in enumerate(group):
            i = jnp.bitwise_xor(me, mask)
            odd = jnp.bitwise_and(i, 1) == 1
            tile = pl.ds(pl.multiple_of(jnp.right_shift(i, 1) * LANES, LANES), LANES)
            t = jnp.concatenate(
                [small_ref[0:5, tile], small_ref[ROUTER : ROUTER + 4, tile], small_ref[DBIAS : DBIAS + 4, tile], blank],
                axis=0,
            )
            lo = jnp.where(odd, pltpu.roll(t, HALF, 1), t)
            lo = jnp.where(lane < HALF, lo, 0.0)
            b = jnp.concatenate([small_ref[UBIAS : UBIAS + 8, tile], jnp.zeros((8, LANES), F4)], axis=0)
            hi = jnp.where(odd, b, pltpu.roll(b, HALF, 1))
            hi = jnp.where(jnp.logical_and(lane >= HALF, row < EXPERTS), hi, 0.0)
            for jm in range(ref.shape[1]):
                j = jnp.bitwise_xor(met, jm)
                g = small_ref[0:8, pl.ds(pl.multiple_of(j * LANES, LANES), LANES)]
                g = pltpu.roll(g, 7, 0)
                g = pltpu.roll(g, jnp.bitwise_and(HALF - i * qr + LANES, LANES - 1), 1)
                g = jnp.concatenate([g, jnp.zeros((8, LANES), F4)], axis=0)
                mine = jnp.logical_and(lane >= HALF, lane < HALF + qr)
                mine = jnp.logical_and(mine, jnp.logical_and(row >= 4, row < 6))
                block = lo + jnp.where(mine, g, 0.0)
                if jm == 0:
                    block = block + hi
                ref[idx, jm, 4 * dr :, :] = block.astype(BF)


def attn_backward(ids, recv, own, x, cot, saved, rows, full, gubs, sms, gmasks, direct, nt, dr):
    count, width = x.shape
    nimg = count // PAD
    extra = SMALL if direct else 0
    shapes = [jax.ShapeDtypeStruct((count, width), F4)]
    shapes += [jax.ShapeDtypeStruct((len(m), nt, 4 * dr + extra, LANES), BF) for m in gmasks]
    shapes += [jax.ShapeDtypeStruct((NROWS, width), F4)]
    low = pltpu.VMEM((count, width), BF)
    return pl.pallas_call(
        partial(attn_backward_kernel, nimg, len(sms), len(gubs), gmasks, direct),
        out_shape=shapes,
        in_specs=[SM] + [VM] * 4 + [ANY] * 6 + [VM] * (2 + len(gubs) + len(sms)),
        out_specs=[VM] * len(shapes),
        scratch_shapes=[low] * 6
        + [pltpu.VMEM((width, width), F4)]
        + [pltpu.VMEM(v.shape, v.dtype) for v in saved]
        + [pltpu.SemaphoreType.DMA((6,))],
        compiler_params=params(16),
        cost_estimate=cost(16),
        name="attn_backward",
    )(ids, recv, own, x, cot, *in_hbm(saved), rows, full, *gubs, *sms)


def per_device(
    nd,
    nt,
    tokens,
    cotangent,
    routes,
    slots,
    norm_gains,
    norm_biases,
    w_qkv,
    qv_bias,
    w_out,
    out_bias,
    w_router,
    w_up,
    up_bias,
    w_down,
    down_bias,
):
    me = lax.axis_index("dp").astype(jnp.int32)
    met = lax.axis_index("tensor").astype(jnp.int32)
    width = tokens.shape[1]
    dr = w_qkv.shape[1]
    fr, qr = up_bias.shape[1], qv_bias.shape[1]
    ff = w_up.shape[2]
    nimg = IMG_DEV // nt
    direct = nd == 8 and nt == 4 and dr == HALF and fr == HALF and nd * qr == LANES
    src = jnp.asarray(ring_sources(nt), jnp.int32)[met]
    ids = jnp.concatenate([jnp.stack([me if direct else jnp.zeros_like(me), met]), src])
    even, odd = list(range(0, nd, 2)), list(range(1, nd, 2))

    def canonical(parts):
        if direct:
            return parts
        masks = sum((m for m, _ in parts), ())
        arr = jnp.concatenate([a for _, a in parts], axis=0)
        place = [masks.index(k) for k in range(nd)]
        order = jnp.asarray(place, jnp.int32)[jnp.bitwise_xor(jnp.arange(nd), me)]
        arr = jnp.take(arr, order, axis=0)
        lead = arr.ndim - 2
        arr = jnp.moveaxis(arr, 0, lead - 1)
        arr = arr.reshape(arr.shape[: lead - 1] + (nd * dr,) + arr.shape[-1:])
        return [((0,), arr[None])]

    gmasks = [even, odd] if direct else [[0]]

    def halves(grads, lead, rows):
        if direct:
            return grads
        whole = grads[0][0]
        shape = whole.shape[:lead] + (rows, nd, dr) + whole.shape[-1:]
        whole = jnp.moveaxis(whole.reshape(shape), lead + 1, 0)
        whole = whole.reshape((nd,) + grads[0].shape[1 : lead + 1] + (rows * dr, whole.shape[-1]))
        return [
            jnp.take(whole, jnp.bitwise_xor(jnp.asarray(m, jnp.int32), me), axis=0)
            for m in (even, odd)
        ]

    def images(v):
        return jnp.concatenate(
            [jnp.pad(v[i * SEQ : (i + 1) * SEQ], ((0, PAD - SEQ), (0, 0))) for i in range(nimg)]
        )

    chunk = jnp.concatenate([w_qkv, w_out.T[None]], axis=0)
    if direct:
        wide = [
            jnp.concatenate(
                [norm_gains, norm_biases, out_bias[None], w_router.T, down_bias, jnp.zeros((3, dr), BF)],
                axis=0,
            ),
            jnp.concatenate(
                [up_bias, jnp.pad(qv_bias, ((0, 0), (0, dr - qr))), jnp.zeros((10, dr), BF)], axis=0
            ),
        ]
        chunk = jnp.concatenate([chunk.reshape(4 * dr, LANES), jnp.concatenate(wide, axis=1)], axis=0)
    keep = jnp.where(slots >= 0, routes, -1).reshape(nt * nimg, SEQ, 2)
    keep = jnp.pad(keep, ((0, 0), (0, PAD - SEQ), (0, 0)), constant_values=-1)
    x = images(tokens)
    w_dn = w_down.transpose(0, 2, 1)
    def ring_all(v):
        out = [v]
        for s in range(1, nt):
            out.append(ring_step(out[-1], nt, False))
        return out

    cot = images(cotangent)
    chunk_z = [chunk] + [xor_send(chunk, "tensor", nt, m) for m in range(1, nt)]
    if direct:
        chunk_z = jnp.stack(chunk_z)
        cots = ring_all(after(cot, chunk_z))
        near = plane_first(chunk_z)
        quad = plane_stack(*near, lax.optimization_barrier((plane_far(*near), cots[1]))[0])
        layers = plane_first(after(jnp.concatenate([w_up, w_dn]), quad))
        full, rows = assemble(ids, gather_cores(after(quad, x, keep, ids)), width)
    else:
        cots = ring_all(cot)
        up, dn = (
            canonical(gather_dp(w[None], nd))[0][1][0, 0].transpose(1, 0, 2).reshape(width, EXPERTS * ff)
            for w in (w_up, w_dn)
        )
        full = canonical(gather_dp(jnp.stack(chunk_z), nd))[0][1][0]
        at = jnp.bitwise_xor(jnp.arange(nt), met)
        full = jnp.take(full, at, axis=0).transpose(1, 2, 0, 3).reshape(4, width, width)

        def whole(v):
            return lax.all_gather(v, "dp", axis=v.ndim - 1, tiled=True).astype(F4)

        qvb = lax.all_gather(whole(qv_bias), "tensor", axis=1, tiled=True)
        four = jnp.zeros((4, width), F4)
        rows = [whole(norm_gains), whole(norm_biases), whole(out_bias[None]), qvb]
        rows += [jnp.zeros((1, width), F4), whole(w_router.T), four, whole(down_bias), four]
        rows += [jnp.pad(whole(up_bias), ((0, 0), (0, width - nd * fr))), four]
        rows = jnp.concatenate(rows, axis=0)

    saved = attn_forward(x, rows, full, nimg)
    hn2s = [saved[0]]
    def shard(s, *first):
        hn2 = after(hn2s[s], *first)
        return expert_shard(ids, keep, hn2, cots[s], rows, up, dn, nimg, s)

    for s in range(1, nt):
        hn2s.append(ring_step(after(hn2s[-1], *(cots[2:] if s == nt - 1 else [])), nt, False))
    if direct:
        layers = lax.optimization_barrier((layers, hn2s[0]))[0]
        far = lax.optimization_barrier((plane_far(*layers), hn2s[1], cots[2]))[0]
        layers = plane_stack(*layers, far)
        up, dn = gather_experts(ids, gather_cores(layers), width)
    shards = [None, shard(1)] + [None] * (nt - 2)
    total = past = shards[1][1]
    for s in range(2, nt):
        if s == nt - 1:
            shards[0] = shard(0, past)
            shards[s] = shard(s, shards[0][1])
        else:
            shards[s] = shard(s, shards[s - 1][1])
        total = ring_step(total, nt, False)
        past = total
        total = sums([[[(total, None), (shards[s][1], None)]]])[0]
        past = total if s < nt - 1 else past
    total = ring_step(total, nt, False)
    recv = total

    gubs, *egrads = expert_grads(
        ids,
        [hn2s[0], after(hn2s[1], past), *hn2s[2:]],
        cots,
        [r[2] for r in shards],
        [r[3] for r in shards],
        gmasks,
        dr if direct else width,
    )
    ms = [r[0] for r in shards]
    if direct:
        other = to(after(egrads[1], recv), 1)
    m_sum = ring_step(after(ms[1], recv), nt, False)

    res = attn_backward(
        ids,
        recv,
        shards[0][1],
        x,
        cots[0],
        saved[1:],
        rows,
        full,
        [gubs],
        [r[4] for r in shards],
        gmasks,
        direct,
        nt,
        dr if direct else width,
    )
    gtok, flat = res[0], res[-1]
    def rows_of(v):
        return jnp.concatenate([v[i * PAD : i * PAD + SEQ] for i in range(nimg)])

    grad_tokens = rows_of(gtok)
    if direct:
        other, m_sum, odd = lax.optimization_barrier((other, m_sum, res[2]))
        a_other = to(odd, 1)
        m_sum = ring_step(sums([[[(m_sum, None), (ms[2], None)]]])[0], nt, False)
        a_kept_x, a_kept_y, a_send_x, a_send_y = scatter_first(res[1], a_other)
        a_got = to(a_send_x, 2), to(a_send_y, 4)
        kept_x, kept_y, send_x, send_y = scatter_first(egrads[0], after(other, a_send_x))
        a_got = lax.optimization_barrier((a_got, send_x))[0]
        a_next_x, a_next_y, a_base_x, a_base_y = scatter_second(a_kept_x, a_kept_y, *a_got)
        a_far = to(a_next_x, 4), to(a_next_y, 2)
        send_x, send_y, m_sum = lax.optimization_barrier((send_x, send_y, m_sum, a_next_x))[:3]
        got = to(send_x, 2), to(send_y, 4)
        m_sum = ring_step(sums([[[(m_sum, None), (ms[3], None)]]])[0], nt, False)
        keep_z, send_z = sums([[[(v, None), (f, None)]] for v, f in zip((a_base_x, a_base_y), a_far)])
        got_z = xor_send(send_z, "tensor", nt, 2)
        got, got_z = lax.optimization_barrier((got, got_z))
        mine, next_z = sums([[[(keep_z, j), (got_z, j)]] for j in (0, 1)])
        next_x, next_y, base_x, base_y = scatter_second(kept_x, kept_y, *got)
        far = to(next_x, 4), to(next_y, 2)
        parts = [mine, xor_send(next_z, "tensor", nt, 1)]
        layer_out = rows_of(saved[1] + (m_sum.astype(F4) + ms[0].astype(F4)))
        parts = lax.optimization_barrier((parts, layer_out, grad_tokens))[0]
        g_qkv, g_out, g_gain, g_bias, g_outb, g_router, g_dbias, g_ub, g_qvb = finish(parts, dr, qr)
        g_up, g_down = add_all([base_x, far[0]])[0], add_all([base_y, far[1]])[0]
        g_outb, g_router = g_outb[0], g_router.T
    else:
        egrads = halves(egrads, 2, 1)
        g_up, g_down = add_all(scatter_dp(*egrads, nd))
        held = add_all(scatter_dp(*halves(res[1:-1], 1, 4), nd)).astype(BF)
        mine = add_all([held[0]] + [xor_send(held[m], "tensor", nt, m) for m in range(1, nt)])
        g_qkv, g_out = mine[: 3 * dr].reshape(3, dr, LANES), mine[3 * dr :]
        for s in range(2, nt):
            m_sum = ring_step(add_all([m_sum, ms[s]]).astype(BF), nt, False)
        layer_out = rows_of(saved[1] + (m_sum.astype(F4) + ms[0].astype(F4)))
        g_ub = lax.dynamic_slice(lax.psum(flat, "dp"), (UBIAS, me * fr), (EXPERTS, fr))
        flat = lax.psum(flat, ("dp", "tensor"))
        cut = lax.dynamic_slice(flat, (0, me * dr), (NROWS, dr))
        g_gain, g_bias, g_outb = cut[0:2], cut[2:4], cut[4]
        g_router, g_dbias = cut[ROUTER : ROUTER + 4].T, cut[DBIAS : DBIAS + 4]
        g_qvb = lax.dynamic_slice(flat, (QVB, (met * nd + me) * qr), (2, qr))

    return (
        layer_out,
        grad_tokens,
        g_gain,
        g_bias,
        g_qkv,
        g_qvb,
        g_out.T,
        g_outb,
        g_router,
        g_up,
        g_ub,
        g_down.transpose(0, 2, 1),
        g_dbias,
    )


def solution(mesh):
    nd, nt = mesh.shape["dp"], mesh.shape["tensor"]
    placed = (
        P(("dp", "tensor"), None),
        P(("dp", "tensor"), None),
        P("dp", None),
        P("dp", None),
        P(None, "dp"),
        P(None, "dp"),
        P(None, "dp", "tensor"),
        P(None, ("tensor", "dp")),
        P("tensor", "dp"),
        P("dp"),
        P("dp", None),
        P(None, "dp", "tensor"),
        P(None, ("tensor", "dp")),
        P(None, "tensor", "dp"),
        P(None, "dp"),
    )
    return jax.shard_map(
        partial(per_device, nd, nt),
        mesh=mesh,
        in_specs=placed,
        out_specs=(
            P(("dp", "tensor"), None),
            P(("dp", "tensor"), None),
            P(None, "dp"),
            P(None, "dp"),
            P(None, "dp", "tensor"),
            P(None, ("tensor", "dp")),
            P("tensor", "dp"),
            P("dp"),
            P("dp", None),
            P(None, "dp", "tensor"),
            P(None, ("tensor", "dp")),
            P(None, "tensor", "dp"),
            P(None, "dp"),
        ),
        check_vma=False,
    )
```
